128 devices in a mesh: lat: 8 (over y, core), lon: 16 (over z, x).
Axes of the slice: x: 4, y: 4, z: 4, core: 2. Of those that a mesh axis runs over, the one named last changes fastest.
Arguments:
- increment: float32 [2, 50, 128, 1024], P(None, None, 'lon', 'lat'), may hold values from -6 to 6
- residual: float32 [2, 50, 128, 1024], P(None, None, 'lon', 'lat'), may hold values from -21 to 21
- direction: float32 [2, 50, 128, 1024], P(None, None, 'lon', 'lat'), may hold values from -21 to 21
- diffusivity: float32 [2, 50, 128, 1024], P(None, None, 'lon', 'lat'), may hold values from 0.03 to 0.24
- deviation: float32 [2, 50, 128, 1024], P(None, None, 'lon', 'lat'), may hold values from 0.5 to 2
- stencil: int32 [16384, 128], P(('lat', 'lon')), may hold values from 0 to 51070, as said below
- bilinear: float32 [16384, 4, 128], P(('lat', 'lon')), may hold values from 0 to 1, as said below
- obs_weight: float32 [2, 16384, 128], P(None, ('lat', 'lon')), may hold values from 2 to 6
- block_owner: int32 [16384, 1], P(('lat', 'lon')), may hold values from 0 to 127; in each aligned block of 128 rows (0 to 127, 128 to 255, ...) at most 2 rows name the same one
- correlation: float32 [16384, 128], P(('lat', 'lon')), may hold values from -0.5 to 2, as said below
Outputs:
- next_increment: float32 [2, 50, 128, 1024], P(None, None, 'lon', 'lat')
- next_residual: float32 [2, 50, 128, 1024], P(None, None, 'lon', 'lat')
- next_direction: float32 [2, 50, 128, 1024], P(None, None, 'lon', 'lat')
The draws below stay inside these ranges and needn't reach their ends.
Inputs may be any that keep to these rules, and one draw needn't show every extreme that they name: `stencil`: each entry is (l * 8 + i) * 128 + j for a level l, a longitude cell i < 7 and a latitude cell j < 127 of the block's tile, so that all four cells of the square lie in that tile. `bilinear`: the four weights of each observation are non-negative and sum to one. `block_owner`: among the 128 blocks of one tile no owner is named more than 2 times, and in every draw some tile names some owner exactly 2 times. `correlation`: each owner's 128 x 128 matrix is symmetric and positive definite.
All inputs are finite; a program needn't handle non-finite values.
Results may differ from the reference program's by a relative error of at most 0.0001.
Values sent between devices are 32-bit elements; how exact they have to be, the bound alone decides.
A program may use at most 64 MiB of HBM per device.

```python
import math
import jax
import jax.numpy as jnp
import numpy as np
from jax import lax

VARS = 2
LEV = 50
CLON = 8
CLAT = 128
STEPS = 4
OB = 128
CAP = 2
ITERS = 1
TILES = 128
NB = 128
NLAT = 1024
NLON = 128
N_LAT = 8
N_LON = 16


def rising_field(key):
    first_key, second_key = jax.random.split(key)
    field_shape = (VARS, LEV, NLON, NLAT)
    lon_pos = (jnp.arange(NLON, dtype=jnp.float32) / NLON)[None, None, :, None]
    lat_pos = (jnp.arange(NLAT, dtype=jnp.float32) / NLAT)[None, None, None, :]
    roughness = jnp.exp(jax.random.uniform(second_key, field_shape, jnp.float32, -0.7, 0.7))
    base_values = jnp.clip(jax.random.normal(first_key, field_shape, jnp.float32), -6.0, 6.0)
    growth = 3.0 ** (0.5 * (lon_pos + lat_pos) - 0.5)
    return base_values * growth * roughness


def draw_residual(key, part):
    return rising_field(jax.random.fold_in(key, 11))


def draw_direction(key, part):
    return rising_field(jax.random.fold_in(key, 13))


def draw_stencil(key, part):
    level_key, lon_key, lat_key = jax.random.split(jax.random.fold_in(key, 5), 3)
    block_shape = (TILES * NB, OB)
    level_index = jax.random.randint(level_key, block_shape, 0, LEV)
    lon_cell = jax.random.randint(lon_key, block_shape, 0, CLON - 1)
    lat_cell = jax.random.randint(lat_key, block_shape, 0, CLAT - 1)
    return ((level_index * CLON + lon_cell) * CLAT + lat_cell).astype(jnp.int32)


def draw_bilinear(key, part):
    lon_key, lat_key = jax.random.split(jax.random.fold_in(key, 7))
    block_shape = (TILES * NB, 1, OB)
    lon_frac = jax.random.uniform(lon_key, block_shape, jnp.float32, 0.1, 0.9)
    lat_frac = jax.random.uniform(lat_key, block_shape, jnp.float32, 0.1, 0.9)
    return jnp.concatenate([(1.0 - lon_frac) * (1.0 - lat_frac), (1.0 - lon_frac) * lat_frac, lon_frac * (1.0 - lat_frac), lon_frac * lat_frac], axis=1)


def draw_correlation(key, part):
    off_key, diag_key = jax.random.split(jax.random.fold_in(key, 3))
    off_bound = 0.95 / (OB - 1)
    raw_values = jax.random.uniform(off_key, (TILES, OB, OB), jnp.float32, -off_bound, off_bound)
    symmetric = 0.5 * (raw_values + jnp.swapaxes(raw_values, 1, 2))
    diagonal = jax.random.uniform(diag_key, (TILES, OB, 1), jnp.float32, 1.0, 2.0)
    identity = jnp.eye(OB, dtype=jnp.float32)[None]
    return (symmetric * (1.0 - identity) + diagonal * identity).reshape(TILES * OB, OB)


def level_of(rng, shape, shards, smallest, largest):
    gain, own = 1.0, jax.random.fold_in(rng, 6)
    for position, blocks in shards:
        draws = jnp.exp(jax.random.uniform(jax.random.fold_in(own, position), (blocks,), jnp.float32, smallest / len(shards), largest / len(shards)))
        gain = gain * jnp.repeat(draws, shape[position] // blocks).reshape([-1 if axis == position else 1 for axis in range(len(shape))])
    return gain


def deal_out(stream_key, own, number, rows, amount, top, bound, lean):
    order = jax.random.permutation(stream_key, amount)
    heavy_load, ordinary = portions_of(amount, rows * top, bound, lean, True), portions_of(amount, rows * top, bound, lean, False)
    places = jnp.arange(amount)

    def named(lengths, rotation):
        used = int((lengths > 0).sum())
        fixed = max(1, used // 4)
        moved = fixed + (places - fixed + rotation * (used - fixed)) % max(1, amount - fixed)
        return jnp.zeros((amount,), jnp.int32).at[order[jnp.where(places < fixed, places, moved)]].set(jnp.asarray(lengths, jnp.int32))

    lengths = jnp.where(number % 4 == 0, named(heavy_load, number // 4), named(ordinary, number - number // 4 - 1))
    mixed = jax.random.permutation(jax.random.fold_in(own, 3), amount)
    donor, taker = mixed[0:amount // 2 * 2:2], mixed[1:amount // 2 * 2:2]
    margin = jnp.minimum(lengths[donor] - 1, bound - lengths[taker]) // 2
    margin = jnp.where((donor == order[0]) | (taker == order[0]) | (lengths[taker] == 0), 0, jnp.maximum(margin, 0))
    moved = jax.random.randint(jax.random.fold_in(own, 4), (amount // 2,), 0, 1 << 20) % (margin + 1)
    lengths = lengths.at[donor].add(-moved).at[taker].add(moved)
    members = jnp.searchsorted(jnp.cumsum(lengths), jnp.arange(rows * top), side="right").astype(jnp.int32)
    listing = members.reshape(top, rows).T
    listing = listing[jax.random.permutation(jax.random.fold_in(own, 1), rows)]
    rotation = jax.random.randint(jax.random.fold_in(own, 2), (rows, 1), 0, top)
    return jnp.take_along_axis(listing, (jnp.arange(top)[None, :] + rotation) % top, axis=1)


def portions_of(number_of, total, reach, skew, full):
    portions = [(1 << 20) // math.isqrt(rank ** skew) + 1 for rank in range(1, number_of + 1)]
    largest = reach if full else min(reach, max(-(-total // number_of), total * portions[0] // sum(portions)))
    least = 1 if total - largest >= number_of - 1 else 0
    holding, spare = [largest] + [least] * (number_of - 1), total - largest - least * (number_of - 1)
    while spare > 0:
        free = [i for i in range(1, number_of) if holding[i] < largest] or [i for i in range(1, number_of) if holding[i] < reach]
        pool, left = sum([portions[i] for i in free]), spare
        for i in free:
            more = min(reach - holding[i], max(1, left * portions[i] // pool), spare)
            holding[i] = holding[i] + more
            spare = spare - more
    return np.array(holding)


def gaussian(stream_key, shape, scale, bound, cuts=(), kind=jnp.bfloat16):
    array = scale * jax.random.normal(stream_key, shape, jnp.float32)
    if cuts:
        array = array * level_of(stream_key, shape, cuts, -0.22, 0.18)
    return jnp.clip(array, -bound, bound).astype(kind)


def setup_inputs(seed: int = 0) -> dict:
    key_of = jax.random.split(jax.random.key(seed), 11)
    increment = gaussian(key_of[0], (VARS, LEV, NLON, NLAT), 1.0, 6.0, ((2, 16), (3, 8)), jnp.float32)
    residual = draw_residual(jax.random.fold_in(key_of[10], 71), 0)
    direction = draw_direction(jax.random.fold_in(key_of[10], 71), 0)
    diffusivity = jnp.clip(0.03 + 0.21 * jax.random.uniform(key_of[3], (VARS, LEV, NLON, NLAT), jnp.float32) ** level_of(key_of[3], (VARS, LEV, NLON, NLAT), ((2, 16), (3, 8)), -0.2, 0.2), 0.03, 0.24)
    deviation = jnp.clip(jnp.exp(math.log(2.0) - 1.3862944 * jax.random.uniform(key_of[4], (VARS, LEV, NLON, NLAT), jnp.float32) ** level_of(key_of[4], (VARS, LEV, NLON, NLAT), ((2, 16), (3, 8)), -0.2, 0.2)), 0.5, 2.0)
    stencil = draw_stencil(jax.random.fold_in(key_of[10], 71), 0)
    bilinear = draw_bilinear(jax.random.fold_in(key_of[10], 71), 0)
    obs_weight = jnp.clip(jnp.exp(math.log(6.0) - 1.0986123 * jax.random.uniform(key_of[7], (VARS, TILES * NB, OB), jnp.float32) ** level_of(key_of[7], (VARS, TILES * NB, OB), ((1, 128),), -0.2, 0.2)), 2.0, 6.0)
    block_owner_keys = jax.random.split(jax.random.fold_in(key_of[8], 1), (TILES * NB) // NB)
    block_owner_turns = jax.random.permutation(jax.random.fold_in(key_of[8], 3), (TILES * NB) // NB)
    block_owner = jax.vmap(lambda own, number: deal_out(jax.random.fold_in(key_of[8], 2), own, number, NB, TILES, 1, CAP, 2))(block_owner_keys, block_owner_turns).reshape((TILES * NB, 1))
    correlation = draw_correlation(jax.random.fold_in(key_of[10], 71), 0)
    return {"increment": increment, "residual": residual, "direction": direction, "diffusivity": diffusivity, "deviation": deviation, "stencil": stencil, "bilinear": bilinear, "obs_weight": obs_weight, "block_owner": block_owner, "correlation": correlation}


precise = lax.Precision.HIGHEST


def widen(field):
    lat_wide = jnp.pad(field, ((0, 0), (0, 0), (0, 0), (1, 1)))
    lon_wide = jnp.concatenate([field[:, :, -1:, :], field, field[:, :, :1, :]], axis=2)
    return lat_wide, lon_wide


def face_coeffs(diffusivity):
    lat_wide, lon_wide = widen(diffusivity)
    return (0.5 * (diffusivity + lat_wide[:, :, :, 2:]), 0.5 * (diffusivity + lat_wide[:, :, :, :-2]),
            0.5 * (diffusivity + lon_wide[:, :, 2:, :]), 0.5 * (diffusivity + lon_wide[:, :, :-2, :]))


def diffuse(field, coeffs):
    north_face, south_face, east_face, west_face = coeffs
    for sweep in range(STEPS):
        lat_wide, lon_wide = widen(field)
        field = (field + north_face * (lat_wide[:, :, :, 2:] - field) + south_face * (lat_wide[:, :, :, :-2] - field)
                 + east_face * (lon_wide[:, :, 2:, :] - field) + west_face * (lon_wide[:, :, :-2, :] - field))
    return field


def to_tiles(field):
    parts = field.reshape(VARS, LEV, N_LON, CLON, N_LAT, CLAT)
    parts = jnp.transpose(parts, (4, 2, 0, 1, 3, 5))
    return parts.reshape(N_LAT * N_LON, VARS, LEV * CLON * CLAT)


def from_tiles(tiled):
    parts = tiled.reshape(N_LAT, N_LON, VARS, LEV, CLON, CLAT)
    parts = jnp.transpose(parts, (2, 3, 1, 4, 0, 5))
    return parts.reshape(VARS, LEV, N_LON * CLON, N_LAT * CLAT)


def corner_cells(base_cell):
    return (base_cell, base_cell + 1, base_cell + CLAT, base_cell + CLAT + 1)


def observe(field, stencil, bilinear, obs_weight):
    tiled = to_tiles(field)
    corners = stencil.reshape(TILES, NB, OB)
    weights = bilinear.reshape(TILES, NB, 4, OB)

    def one_tile(flat_cells, base_cell, weights_tile):
        positions = corner_cells(base_cell)
        interpolated = weights_tile[:, 0, :] * flat_cells[:, positions[0]]
        for corner in range(1, 4):
            interpolated = interpolated + weights_tile[:, corner, :] * flat_cells[:, positions[corner]]
        return interpolated

    values = jax.vmap(one_tile)(tiled, corners, weights)
    values = jnp.transpose(values, (1, 0, 2, 3)).reshape(VARS, TILES * NB, OB)
    return obs_weight * values


def correlate(observed, block_owner, correlation):
    matrices = correlation.reshape(TILES, OB, OB)
    per_tile = jnp.transpose(observed.reshape(VARS, TILES, NB, OB), (1, 0, 2, 3))
    owners = block_owner.reshape(TILES, NB)

    def one_tile(args_pair):
        values, targets = args_pair
        chosen = matrices[targets]
        return jnp.einsum("vbk,bik->vbi", values, chosen, precision=precise)

    mixed_values = lax.map(one_tile, (per_tile, owners))
    return jnp.transpose(mixed_values, (1, 0, 2, 3)).reshape(VARS, TILES * NB, OB)


def spread_back(weighted, stencil, bilinear):
    per_tile = jnp.transpose(weighted.reshape(VARS, TILES, NB, OB), (1, 0, 2, 3))
    corners = stencil.reshape(TILES, NB, OB)
    weights = bilinear.reshape(TILES, NB, 4, OB)

    def one_tile(values, base_cell, weights_tile):
        flat_cells = jnp.zeros((VARS, LEV * CLON * CLAT), jnp.float32)
        for corner, positions in enumerate(corner_cells(base_cell)):
            flat_cells = flat_cells.at[:, positions].add(weights_tile[:, corner, :] * values)
        return flat_cells

    return from_tiles(jax.vmap(one_tile)(per_tile, corners, weights))


def reference(increment, residual, direction, diffusivity, deviation, stencil, bilinear, obs_weight, block_owner, correlation):
    coeffs = face_coeffs(diffusivity)

    def hessian(vector):
        state_field = deviation * diffuse(vector, coeffs)
        observed = observe(state_field, stencil, bilinear, obs_weight)
        weighted = obs_weight * correlate(observed, block_owner, correlation)
        spread_field = deviation * spread_back(weighted, stencil, bilinear)
        return vector + diffuse(spread_field, coeffs)

    norm_now = jnp.sum(residual * residual)
    for iteration in range(ITERS):
        image_field = hessian(direction)
        step_size = norm_now / jnp.sum(direction * image_field)
        increment = increment + step_size * direction
        residual = residual - step_size * image_field
        norm_next = jnp.sum(residual * residual)
        direction = residual + (norm_next / norm_now) * direction
        norm_now = norm_next
    return increment, residual, direction
```

```python
import math

import jax
import jax.numpy as jnp
from jax import lax
from jax.sharding import PartitionSpec as P

STEPS = 4
CAP = 2


precise = lax.Precision.HIGHEST


def neighbour_pairs(lat_devices, lon_devices, lat_step, lon_step):
    pairs = []
    for a in range(lat_devices):
        if not 0 <= a + lat_step < lat_devices:
            continue
        for b in range(lon_devices):
            target = (a + lat_step) * lon_devices + (b + lon_step) % lon_devices
            pairs.append((a * lon_devices + b, target))
    return pairs


def widen_halo(value, width):
    lat_devices = lax.axis_size("lat")
    lon_devices = lax.axis_size("lon")
    lon_count, lat_count = value.shape[2], value.shape[3]
    lon_parts = {-1: value[:, :, lon_count - width :], 0: value, 1: value[:, :, :width]}
    rows = []
    for lon_side in (-1, 0, 1):
        row = []
        for lat_side in (-1, 0, 1):
            piece = lon_parts[lon_side]
            if lat_side == -1:
                piece = piece[:, :, :, lat_count - width :]
            elif lat_side == 1:
                piece = piece[:, :, :, :width]
            if lon_side or lat_side:
                pairs = neighbour_pairs(lat_devices, lon_devices, -lat_side, -lon_side)
                piece = lax.ppermute(piece, ("lat", "lon"), pairs)
            row.append(piece)
        rows.append(jnp.concatenate(row, axis=3))
    return jnp.concatenate(rows, axis=2)


def face_coeffs(diffusivity, width):
    wide = widen_halo(diffusivity, width + 1)
    lat_count = diffusivity.shape[3]
    lat_devices = lax.axis_size("lat")
    first = lax.axis_index("lat") * lat_count - width
    cells = first + jnp.arange(lat_count + 2 * width, dtype=jnp.int32)
    inside = ((cells >= 0) & (cells < lat_devices * lat_count)).astype(jnp.float32)
    centre = wide[:, :, 1:-1, 1:-1]
    return (
        inside * (0.5 * (centre + wide[:, :, 1:-1, 2:])),
        inside * (0.5 * (centre + wide[:, :, 1:-1, :-2])),
        inside * (0.5 * (centre + wide[:, :, 2:, 1:-1])),
        inside * (0.5 * (centre + wide[:, :, :-2, 1:-1])),
    )


def diffuse(field, coeffs):
    field = widen_halo(field, STEPS)
    for sweep in range(STEPS):
        lon_end = field.shape[2] - 1
        lat_end = field.shape[3] - 1
        here = field[:, :, 1:lon_end, 1:lat_end]
        edge = sweep + 1
        north_face, south_face, east_face, west_face = (
            c[:, :, edge : c.shape[2] - edge, edge : c.shape[3] - edge] for c in coeffs
        )
        field = (
            here
            + north_face * (field[:, :, 1:lon_end, 2:] - here)
            + south_face * (field[:, :, 1:lon_end, : lat_end - 1] - here)
            + east_face * (field[:, :, 2:, 1:lat_end] - here)
            + west_face * (field[:, :, : lon_end - 1, 1:lat_end] - here)
        )
    return field


def obs_groups(stencil, bilinear):
    block_count, obs_count = stencil.shape
    group = math.gcd(block_count, max(1, 1024 // obs_count))
    steps_count = block_count // group
    bases = stencil.reshape(steps_count, group * obs_count)
    corner_weights = jnp.transpose(bilinear.reshape(steps_count, group, 4, obs_count), (0, 2, 1, 3))
    return (bases, corner_weights.reshape(steps_count, 4, group * obs_count), steps_count)


def lat_weights(lat_base, first_weight, second_weight, lat_count):
    cells = jnp.arange(lat_count, dtype=jnp.int32)[:, None]
    return jnp.where(cells == lat_base[None, :], first_weight[None, :], 0.0) + jnp.where(
        cells == lat_base[None, :] + 1, second_weight[None, :], 0.0
    )


def block_maps(base, weights_four, row_count, lat_count):
    row_base = base // lat_count
    lat_base = base - row_base * lat_count
    rows = jnp.arange(row_count, dtype=jnp.int32)[:, None]
    near_rows = (rows == row_base[None, :]).astype(jnp.float32)
    far_rows = (rows == row_base[None, :] + 1).astype(jnp.float32)
    near_lat = lat_weights(lat_base, weights_four[0], weights_four[1], lat_count)
    far_lat = lat_weights(lat_base, weights_four[2], weights_four[3], lat_count)
    return (near_rows, far_rows, near_lat, far_lat)


def observe(field, stencil, bilinear, obs_weight):
    var_count, level_count, lon_count, lat_count = field.shape
    row_count = level_count * lon_count
    row_field = field.reshape(var_count, row_count, lat_count)
    bases, corner_weights, steps_count = obs_groups(stencil, bilinear)

    def one_group(pair):
        near_rows, far_rows, near_lat, far_lat = block_maps(pair[0], pair[1], row_count, lat_count)
        near_vals = jnp.einsum("vrj,jk->vrk", row_field, near_lat, precision=precise)
        far_vals = jnp.einsum("vrj,jk->vrk", row_field, far_lat, precision=precise)
        return jnp.sum(near_vals * near_rows[None] + far_vals * far_rows[None], axis=1)

    values = lax.map(one_group, (bases, corner_weights))
    values = jnp.transpose(values, (1, 0, 2)).reshape(obs_weight.shape)
    return obs_weight * values


def spread_back(weighted, stencil, bilinear, field_shape):
    var_count, level_count, lon_count, lat_count = field_shape
    row_count = level_count * lon_count
    bases, corner_weights, steps_count = obs_groups(stencil, bilinear)
    grouped = jnp.transpose(weighted.reshape(var_count, steps_count, -1), (1, 0, 2))

    def add_group(total, triple):
        base, weights_four, values = triple
        near_rows, far_rows, near_lat, far_lat = block_maps(
            base, weights_four, row_count, lat_count
        )
        near_part = jnp.einsum(
            "vrk,jk->vrj", near_rows[None] * values[:, None, :], near_lat, precision=precise
        )
        far_part = jnp.einsum(
            "vrk,jk->vrj", far_rows[None] * values[:, None, :], far_lat, precision=precise
        )
        return (total + near_part + far_part, None)

    start = jnp.zeros((var_count, row_count, lat_count), jnp.float32)
    total, unused = lax.scan(add_group, start, (bases, corner_weights, grouped))
    return total.reshape(field_shape)


def slots_of(block_owner, tile_count):
    targets = block_owner[:, 0]
    block_count = targets.shape[0]
    same_owner = (targets[:, None] == jnp.arange(tile_count, dtype=jnp.int32)[None, :]).astype(
        jnp.int32
    )
    order = jnp.arange(block_count, dtype=jnp.int32)
    lower = (order[:, None] > order[None, :]).astype(jnp.int32)
    earlier = jnp.dot(lower, same_owner)
    rank_within = jnp.sum(earlier * same_owner, axis=1)
    return targets * CAP + rank_within


def mix_blocks(values, correlation):
    return jnp.einsum("vsk,ik->vsi", values, correlation, precision=precise)


def shards(
    increment,
    residual,
    direction,
    diffusivity,
    deviation,
    stencil,
    bilinear,
    obs_weight,
    block_owner,
    correlation,
):
    lat_devices = lax.axis_size("lat")
    lon_devices = lax.axis_size("lon")
    tile_count = lat_devices * lon_devices
    coeffs = face_coeffs(diffusivity, STEPS)

    def apply_diffusion(field):
        return diffuse(field, coeffs)

    slots = slots_of(block_owner, tile_count)
    slot_table = (slots[:, None] == jnp.arange(tile_count * CAP, dtype=jnp.int32)[None, :]).astype(
        jnp.float32
    )
    field_shape = direction.shape
    state_field = deviation * apply_diffusion(direction)
    observed = observe(state_field, stencil, bilinear, obs_weight)
    buffer = jnp.einsum("vbk,bs->vsk", observed, slot_table, precision=precise)
    returned = lax.all_to_all(
        mix_blocks(
            lax.all_to_all(buffer, ("lat", "lon"), split_axis=1, concat_axis=1, tiled=True),
            correlation,
        ),
        ("lat", "lon"),
        split_axis=1,
        concat_axis=1,
        tiled=True,
    )
    weighted = obs_weight * jnp.einsum("vsk,bs->vbk", returned, slot_table, precision=precise)
    spread_field = deviation * spread_back(weighted, stencil, bilinear, field_shape)
    image_field = direction + apply_diffusion(spread_field)
    sums = lax.psum(
        jnp.stack(
            [
                jnp.sum(residual * residual),
                jnp.sum(direction * image_field),
                jnp.sum(residual * image_field),
                jnp.sum(image_field * image_field),
            ]
        ),
        ("lat", "lon"),
    )
    norm_now, curvature, cross, image_norm = sums[0], sums[1], sums[2], sums[3]
    step_size = norm_now / curvature
    increment = increment + step_size * direction
    residual = residual - step_size * image_field
    norm_next = norm_now - 2.0 * step_size * cross + step_size * step_size * image_norm
    direction = residual + norm_next / norm_now * direction
    return (increment, residual, direction)


def solution(mesh):
    in_specs = (
        P(None, None, "lon", "lat"),
        P(None, None, "lon", "lat"),
        P(None, None, "lon", "lat"),
        P(None, None, "lon", "lat"),
        P(None, None, "lon", "lat"),
        P(("lat", "lon"), None),
        P(("lat", "lon"), None, None),
        P(None, ("lat", "lon"), None),
        P(("lat", "lon"), None),
        P(("lat", "lon"), None),
    )
    out_specs = (
        P(None, None, "lon", "lat"),
        P(None, None, "lon", "lat"),
        P(None, None, "lon", "lat"),
    )
    return jax.shard_map(shards, mesh=mesh, in_specs=in_specs, out_specs=out_specs, check_vma=False)
```

```python
import functools
import math

import jax
import jax.numpy as jnp
from jax import lax
from jax.experimental import pallas as pl
from jax.sharding import PartitionSpec as P

STEPS = 4
CAP = 2


precise = lax.Precision.HIGHEST


def widen_halo(value, width):
    lat_dim, lon_dim = value.ndim - 1, value.ndim - 2
    for axis, dim, wrap in (("lat", lat_dim, False), ("lon", lon_dim, True)):
        size, length = lax.axis_size(axis), value.shape[dim]
        up = [(i, (i + 1) % size) for i in range(size if wrap else size - 1)]
        down = [(j, i) for i, j in up]
        before = lax.ppermute(lax.slice_in_dim(value, length - width, length, axis=dim), axis, up)
        after = lax.ppermute(lax.slice_in_dim(value, 0, width, axis=dim), axis, down)
        value = jnp.concatenate([before, value, after], axis=dim)
    return value


def face_coeffs(wide, width):
    lat_count = wide.shape[3] - 2 * (width + 1)
    lat_devices = lax.axis_size("lat")
    first = lax.axis_index("lat") * lat_count - width
    cells = first + jnp.arange(lat_count + 2 * width, dtype=jnp.int32)
    inside = ((cells >= 0) & (cells < lat_devices * lat_count)).astype(jnp.float32)
    centre = wide[:, :, 1:-1, 1:-1]
    return (
        inside * (0.5 * (centre + wide[:, :, 1:-1, 2:])),
        inside * (0.5 * (centre + wide[:, :, 1:-1, :-2])),
        inside * (0.5 * (centre + wide[:, :, 2:, 1:-1])),
        inside * (0.5 * (centre + wide[:, :, :-2, 1:-1])),
    )


def diffuse(field, coeffs):
    for sweep in range(STEPS):
        lon_end = field.shape[2] - 1
        lat_end = field.shape[3] - 1
        here = field[:, :, 1:lon_end, 1:lat_end]
        edge = sweep + 1
        north_face, south_face, east_face, west_face = (
            c[:, :, edge : c.shape[2] - edge, edge : c.shape[3] - edge] for c in coeffs
        )
        field = (
            here
            + north_face * (field[:, :, 1:lon_end, 2:] - here)
            + south_face * (field[:, :, 1:lon_end, : lat_end - 1] - here)
            + east_face * (field[:, :, 2:, 1:lat_end] - here)
            + west_face * (field[:, :, : lon_end - 1, 1:lat_end] - here)
        )
    return field


PARTS = 3


def split_parts(value):
    parts = []
    rest = value
    for part in range(PARTS):
        piece = rest.astype(jnp.bfloat16)
        parts.append(piece)
        rest = rest - piece.astype(jnp.float32)
    return parts


def obs_lines(cell_ref, weight_ref, group, lat_count):
    cells = cell_ref[...]
    rows = cells // lat_count
    lats = cells - rows * lat_count
    row_line = jnp.concatenate([rows[g : g + 1, :] for g in range(group)], axis=1)
    lat_line = jnp.concatenate([lats[g : g + 1, :] for g in range(group)], axis=1)
    weights = [
        jnp.concatenate([weight_ref[g, c : c + 1, :] for g in range(group)], axis=1) for c in range(4)
    ]
    return row_line, lat_line, weights


def select_maps(row_line, lat_line, weights, row_count, lat_count):
    width = row_line.shape[1]
    row_ids = lax.broadcasted_iota(jnp.int32, (row_count, width), 0)
    near_rows = (row_ids == row_line).astype(jnp.bfloat16)
    far_rows = (row_ids == row_line + 1).astype(jnp.bfloat16)
    lat_ids = lax.broadcasted_iota(jnp.int32, (lat_count, width), 0)
    near_lat = jnp.where(lat_ids == lat_line, weights[0], 0.0) + jnp.where(
        lat_ids == lat_line + 1, weights[1], 0.0
    )
    far_lat = jnp.where(lat_ids == lat_line, weights[2], 0.0) + jnp.where(
        lat_ids == lat_line + 1, weights[3], 0.0
    )
    return near_rows, far_rows, near_lat, far_lat


def observe_kernel(group, var_count, row_count, lat_count, table_ref, cell_ref, weight_ref, scale_ref, out_ref):
    row_line, lat_line, weights = obs_lines(cell_ref, weight_ref, group, lat_count)
    near_rows, far_rows, near_lat, far_lat = select_maps(row_line, lat_line, weights, row_count, lat_count)
    table = jnp.concatenate(split_parts(table_ref[...]), axis=1)
    near_vals = jnp.dot(table, jnp.concatenate([near_rows] * PARTS, axis=0), preferred_element_type=jnp.float32)
    far_vals = jnp.dot(table, jnp.concatenate([far_rows] * PARTS, axis=0), preferred_element_type=jnp.float32)
    for v in range(var_count):
        span = slice(v * lat_count, (v + 1) * lat_count)
        line = jnp.sum(near_vals[span] * near_lat + far_vals[span] * far_lat, axis=0, keepdims=True)
        for g in range(group):
            out_ref[v, g : g + 1, :] = scale_ref[v, g : g + 1, :] * line[:, g * 128 : (g + 1) * 128]


def spread_kernel(group, var_count, row_count, lat_count, value_ref, cell_ref, weight_ref, out_ref):
    @pl.when(pl.program_id(0) == 0)
    def _():
        out_ref[...] = jnp.zeros_like(out_ref)

    row_line, lat_line, weights = obs_lines(cell_ref, weight_ref, group, lat_count)
    near_rows, far_rows, near_lat, far_lat = select_maps(row_line, lat_line, weights, row_count, lat_count)
    near_parts, far_parts = [], []
    for v in range(var_count):
        line = jnp.concatenate([value_ref[v, g : g + 1, :] for g in range(group)], axis=1)
        near_parts.append(near_lat * line)
        far_parts.append(far_lat * line)
    near_split = split_parts(jnp.concatenate(near_parts, axis=0))
    far_split = split_parts(jnp.concatenate(far_parts, axis=0))
    lhs = jnp.concatenate(near_split + far_split, axis=1)
    rhs = jnp.concatenate([near_rows] * PARTS + [far_rows] * PARTS, axis=1)
    out_ref[...] += lax.dot_general(
        lhs, rhs, (((1,), (1,)), ((), ())), preferred_element_type=jnp.float32
    )


def observe_pallas(field, stencil, bilinear, obs_weight, group=8):
    var_count, level_count, lon_count, lat_count = field.shape
    row_count = level_count * lon_count
    block_count = stencil.shape[0]
    rows_t = jnp.transpose(field.reshape(var_count, row_count, lat_count), (0, 2, 1))
    table = rows_t.reshape(var_count * lat_count, row_count)
    kernel = functools.partial(observe_kernel, group, var_count, row_count, lat_count)
    width = group * stencil.shape[1]
    flops = 2 * 2 * var_count * lat_count * PARTS * row_count * width * (block_count // group)
    return pl.pallas_call(
        kernel,
        grid=(block_count // group,),
        in_specs=[
            pl.BlockSpec(table.shape, lambda i: (0, 0)),
            pl.BlockSpec((group, stencil.shape[1]), lambda i: (i, 0)),
            pl.BlockSpec((group, 4, stencil.shape[1]), lambda i: (i, 0, 0)),
            pl.BlockSpec((var_count, group, stencil.shape[1]), lambda i: (0, i, 0)),
        ],
        out_specs=pl.BlockSpec((var_count, group, stencil.shape[1]), lambda i: (0, i, 0)),
        out_shape=jax.ShapeDtypeStruct(obs_weight.shape, jnp.float32),
        cost_estimate=pl.CostEstimate(flops=flops, transcendentals=0, bytes_accessed=4 * 1024 * 1024),
    )(table, stencil, bilinear, obs_weight)


def spread_pallas(values, stencil, bilinear, field_shape, group=8):
    var_count, level_count, lon_count, lat_count = field_shape
    row_count = level_count * lon_count
    block_count = stencil.shape[0]
    kernel = functools.partial(spread_kernel, group, var_count, row_count, lat_count)
    width = group * stencil.shape[1]
    flops = 2 * 2 * var_count * lat_count * PARTS * row_count * width * (block_count // group)
    total = pl.pallas_call(
        kernel,
        grid=(block_count // group,),
        in_specs=[
            pl.BlockSpec((var_count, group, stencil.shape[1]), lambda i: (0, i, 0)),
            pl.BlockSpec((group, stencil.shape[1]), lambda i: (i, 0)),
            pl.BlockSpec((group, 4, stencil.shape[1]), lambda i: (i, 0, 0)),
        ],
        out_specs=pl.BlockSpec((var_count * lat_count, row_count), lambda i: (0, 0)),
        out_shape=jax.ShapeDtypeStruct((var_count * lat_count, row_count), jnp.float32),
        cost_estimate=pl.CostEstimate(flops=flops, transcendentals=0, bytes_accessed=4 * 1024 * 1024),
    )(values, stencil, bilinear)
    total = jnp.transpose(total.reshape(var_count, lat_count, row_count), (0, 2, 1))
    return total.reshape(field_shape)


def slots_of(block_owner, tile_count):
    targets = block_owner[:, 0]
    block_count = targets.shape[0]
    same_owner = (targets[:, None] == jnp.arange(tile_count, dtype=jnp.int32)[None, :]).astype(
        jnp.int32
    )
    order = jnp.arange(block_count, dtype=jnp.int32)
    lower = (order[:, None] > order[None, :]).astype(jnp.int32)
    earlier = jnp.dot(lower, same_owner)
    rank_within = jnp.sum(earlier * same_owner, axis=1)
    return targets * CAP + rank_within


def mix_blocks(values, correlation):
    return jnp.einsum("vsk,ik->vsi", values, correlation, precision=precise)


def shards(
    increment,
    residual,
    direction,
    diffusivity,
    deviation,
    stencil,
    bilinear,
    obs_weight,
    block_owner,
    correlation,
):
    lat_devices = lax.axis_size("lat")
    lon_devices = lax.axis_size("lon")
    tile_count = lat_devices * lon_devices
    both = widen_halo(jnp.stack([direction, diffusivity]), STEPS + 1)
    coeffs = face_coeffs(both[1], STEPS)

    def apply_diffusion(field):
        return diffuse(widen_halo(field, STEPS), coeffs)

    slots = slots_of(block_owner, tile_count)
    slot_table = (slots[:, None] == jnp.arange(tile_count * CAP, dtype=jnp.int32)[None, :]).astype(
        jnp.float32
    )
    field_shape = direction.shape
    state_field = deviation * diffuse(both[0][:, :, 1:-1, 1:-1], coeffs)
    observed = observe_pallas(state_field, stencil, bilinear, obs_weight)
    buffer = jnp.einsum("vbk,bs->vsk", observed, slot_table, precision=precise)
    returned = lax.all_to_all(
        mix_blocks(
            lax.all_to_all(buffer, ("lat", "lon"), split_axis=1, concat_axis=1, tiled=True),
            correlation,
        ),
        ("lat", "lon"),
        split_axis=1,
        concat_axis=1,
        tiled=True,
    )
    weighted = obs_weight * jnp.einsum("vsk,bs->vbk", returned, slot_table, precision=precise)
    spread_field = deviation * spread_pallas(weighted, stencil, bilinear, field_shape)
    image_field = direction + apply_diffusion(spread_field)
    sums = lax.psum(
        jnp.stack(
            [
                jnp.sum(residual * residual),
                jnp.sum(direction * image_field),
                jnp.sum(residual * image_field),
                jnp.sum(image_field * image_field),
            ]
        ),
        ("lat", "lon"),
    )
    norm_now, curvature, cross, image_norm = sums[0], sums[1], sums[2], sums[3]
    step_size = norm_now / curvature
    increment = increment + step_size * direction
    residual = residual - step_size * image_field
    norm_next = norm_now - 2.0 * step_size * cross + step_size * step_size * image_norm
    direction = residual + norm_next / norm_now * direction
    return (increment, residual, direction)


def solution(mesh):
    in_specs = (
        P(None, None, "lon", "lat"),
        P(None, None, "lon", "lat"),
        P(None, None, "lon", "lat"),
        P(None, None, "lon", "lat"),
        P(None, None, "lon", "lat"),
        P(("lat", "lon"), None),
        P(("lat", "lon"), None, None),
        P(None, ("lat", "lon"), None),
        P(("lat", "lon"), None),
        P(("lat", "lon"), None),
    )
    out_specs = (
        P(None, None, "lon", "lat"),
        P(None, None, "lon", "lat"),
        P(None, None, "lon", "lat"),
    )
    return jax.shard_map(shards, mesh=mesh, in_specs=in_specs, out_specs=out_specs, check_vma=False)
```

```python
import functools
import math

import jax
import jax.numpy as jnp
from jax import lax
from jax.experimental import pallas as pl
from jax.experimental.pallas import tpu as pltpu
from jax.sharding import PartitionSpec as P

STEPS = 4
CAP = 2


precise = lax.Precision.HIGHEST


def widen_halo(value, width):
    lat_dim, lon_dim = value.ndim - 1, value.ndim - 2
    for axis, dim, wrap in (("lat", lat_dim, False), ("lon", lon_dim, True)):
        size, length = lax.axis_size(axis), value.shape[dim]
        up = [(i, (i + 1) % size) for i in range(size if wrap else size - 1)]
        down = [(j, i) for i, j in up]
        before = lax.ppermute(lax.slice_in_dim(value, length - width, length, axis=dim), axis, up)
        after = lax.ppermute(lax.slice_in_dim(value, 0, width, axis=dim), axis, down)
        value = jnp.concatenate([before, value, after], axis=dim)
    return value


def face_coeffs(wide, width):
    lat_count = wide.shape[3] - 2 * (width + 1)
    lat_devices = lax.axis_size("lat")
    first = lax.axis_index("lat") * lat_count - width
    cells = first + jnp.arange(lat_count + 2 * width, dtype=jnp.int32)
    inside = ((cells >= 0) & (cells < lat_devices * lat_count)).astype(jnp.float32)
    centre = wide[:, :, 1:-1, 1:-1]
    return (
        inside * (0.5 * (centre + wide[:, :, 1:-1, 2:])),
        inside * (0.5 * (centre + wide[:, :, 1:-1, :-2])),
        inside * (0.5 * (centre + wide[:, :, 2:, 1:-1])),
        inside * (0.5 * (centre + wide[:, :, :-2, 1:-1])),
    )


def diffuse(field, coeffs):
    for sweep in range(STEPS):
        lon_end = field.shape[2] - 1
        lat_end = field.shape[3] - 1
        here = field[:, :, 1:lon_end, 1:lat_end]
        edge = sweep + 1
        north_face, south_face, east_face, west_face = (
            c[:, :, edge : c.shape[2] - edge, edge : c.shape[3] - edge] for c in coeffs
        )
        field = (
            here
            + north_face * (field[:, :, 1:lon_end, 2:] - here)
            + south_face * (field[:, :, 1:lon_end, : lat_end - 1] - here)
            + east_face * (field[:, :, 2:, 1:lat_end] - here)
            + west_face * (field[:, :, : lon_end - 1, 1:lat_end] - here)
        )
    return field


PARTS = 3


def split_parts(value):
    parts = []
    rest = value
    for part in range(PARTS):
        piece = rest.astype(jnp.bfloat16)
        parts.append(piece)
        rest = rest - piece.astype(jnp.float32)
    return parts


def obs_lines(cell_ref, weight_ref, group, lat_count):
    cells = cell_ref[...]
    rows = cells // lat_count
    lats = cells - rows * lat_count
    row_line = jnp.concatenate([rows[g : g + 1, :] for g in range(group)], axis=1)
    lat_line = jnp.concatenate([lats[g : g + 1, :] for g in range(group)], axis=1)
    weights = [
        jnp.concatenate([weight_ref[g, c : c + 1, :] for g in range(group)], axis=1) for c in range(4)
    ]
    return row_line, lat_line, weights


def select_maps(row_line, lat_line, weights, row_count, lat_count):
    width = row_line.shape[1]
    row_ids = lax.broadcasted_iota(jnp.int32, (row_count, width), 0)
    near_rows = (row_ids == row_line).astype(jnp.bfloat16)
    far_rows = (row_ids == row_line + 1).astype(jnp.bfloat16)
    lat_ids = lax.broadcasted_iota(jnp.int32, (lat_count, width), 0)
    near_lat = jnp.where(lat_ids == lat_line, weights[0], 0.0) + jnp.where(
        lat_ids == lat_line + 1, weights[1], 0.0
    )
    far_lat = jnp.where(lat_ids == lat_line, weights[2], 0.0) + jnp.where(
        lat_ids == lat_line + 1, weights[3], 0.0
    )
    return near_rows, far_rows, near_lat, far_lat


def observe_kernel(group, var_count, row_count, lat_count, table_ref, cell_ref, weight_ref, scale_ref, out_ref):
    row_line, lat_line, weights = obs_lines(cell_ref, weight_ref, group, lat_count)
    near_rows, far_rows, near_lat, far_lat = select_maps(row_line, lat_line, weights, row_count, lat_count)
    table = jnp.concatenate(split_parts(table_ref[...]), axis=1)
    near_vals = jnp.dot(table, jnp.concatenate([near_rows] * PARTS, axis=0), preferred_element_type=jnp.float32)
    far_vals = jnp.dot(table, jnp.concatenate([far_rows] * PARTS, axis=0), preferred_element_type=jnp.float32)
    for v in range(var_count):
        span = slice(v * lat_count, (v + 1) * lat_count)
        line = jnp.sum(near_vals[span] * near_lat + far_vals[span] * far_lat, axis=0, keepdims=True)
        for g in range(group):
            out_ref[v, g : g + 1, :] = scale_ref[v, g : g + 1, :] * line[:, g * 128 : (g + 1) * 128]


def spread_kernel(group, var_count, row_count, lat_count, value_ref, cell_ref, weight_ref, out_ref):
    @pl.when(pl.program_id(0) == 0)
    def _():
        out_ref[...] = jnp.zeros_like(out_ref)

    row_line, lat_line, weights = obs_lines(cell_ref, weight_ref, group, lat_count)
    near_rows, far_rows, near_lat, far_lat = select_maps(row_line, lat_line, weights, row_count, lat_count)
    near_parts, far_parts = [], []
    for v in range(var_count):
        line = jnp.concatenate([value_ref[v, g : g + 1, :] for g in range(group)], axis=1)
        near_parts.append(near_lat * line)
        far_parts.append(far_lat * line)
    near_split = split_parts(jnp.concatenate(near_parts, axis=0))
    far_split = split_parts(jnp.concatenate(far_parts, axis=0))
    lhs = jnp.concatenate(near_split + far_split, axis=1)
    rhs = jnp.concatenate([near_rows] * PARTS + [far_rows] * PARTS, axis=1)
    out_ref[...] += lax.dot_general(
        lhs, rhs, (((1,), (1,)), ((), ())), preferred_element_type=jnp.float32
    )


def observe_pallas(field, stencil, bilinear, obs_weight, group=8):
    var_count, level_count, lon_count, lat_count = field.shape
    row_count = level_count * lon_count
    block_count = stencil.shape[0]
    rows_t = jnp.transpose(field.reshape(var_count, row_count, lat_count), (0, 2, 1))
    table = rows_t.reshape(var_count * lat_count, row_count)
    kernel = functools.partial(observe_kernel, group, var_count, row_count, lat_count)
    width = group * stencil.shape[1]
    flops = 2 * 2 * var_count * lat_count * PARTS * row_count * width * (block_count // group)
    return pl.pallas_call(
        kernel,
        grid=(block_count // group,),
        in_specs=[
            pl.BlockSpec(table.shape, lambda i: (0, 0)),
            pl.BlockSpec((group, stencil.shape[1]), lambda i: (i, 0)),
            pl.BlockSpec((group, 4, stencil.shape[1]), lambda i: (i, 0, 0)),
            pl.BlockSpec((var_count, group, stencil.shape[1]), lambda i: (0, i, 0)),
        ],
        out_specs=pl.BlockSpec((var_count, group, stencil.shape[1]), lambda i: (0, i, 0)),
        out_shape=jax.ShapeDtypeStruct(obs_weight.shape, jnp.float32),
        cost_estimate=pl.CostEstimate(flops=flops, transcendentals=0, bytes_accessed=4 * 1024 * 1024),
    )(table, stencil, bilinear, obs_weight)


def spread_pallas(values, stencil, bilinear, field_shape, group=8):
    var_count, level_count, lon_count, lat_count = field_shape
    row_count = level_count * lon_count
    block_count = stencil.shape[0]
    kernel = functools.partial(spread_kernel, group, var_count, row_count, lat_count)
    width = group * stencil.shape[1]
    flops = 2 * 2 * var_count * lat_count * PARTS * row_count * width * (block_count // group)
    total = pl.pallas_call(
        kernel,
        grid=(block_count // group,),
        in_specs=[
            pl.BlockSpec((var_count, group, stencil.shape[1]), lambda i: (0, i, 0)),
            pl.BlockSpec((group, stencil.shape[1]), lambda i: (i, 0)),
            pl.BlockSpec((group, 4, stencil.shape[1]), lambda i: (i, 0, 0)),
        ],
        out_specs=pl.BlockSpec((var_count * lat_count, row_count), lambda i: (0, 0)),
        out_shape=jax.ShapeDtypeStruct((var_count * lat_count, row_count), jnp.float32),
        cost_estimate=pl.CostEstimate(flops=flops, transcendentals=0, bytes_accessed=4 * 1024 * 1024),
    )(values, stencil, bilinear)
    total = jnp.transpose(total.reshape(var_count, lat_count, row_count), (0, 2, 1))
    return total.reshape(field_shape)


def allreduce_kernel(lat_devices, lon_devices, part_ref, out_ref, lon_buf, lat_buf, lon_send, lon_recv, lat_send, lat_recv):
    mesh_id = pl.DeviceIdType.MESH
    lat_me = lax.axis_index("lat")
    lon_me = lax.axis_index("lon")
    barrier = pltpu.get_barrier_semaphore()
    for peer in range(1, lon_devices):
        pl.semaphore_signal(barrier, inc=1, device_id=(lat_me, (lon_me + peer) % lon_devices), device_id_type=mesh_id)
    for peer in range(1, lat_devices):
        pl.semaphore_signal(barrier, inc=1, device_id=((lat_me + peer) % lat_devices, lon_me), device_id_type=mesh_id)
    pl.semaphore_wait(barrier, lon_devices + lat_devices - 2)

    def gather(buf, send, recv, count, me, target_of, source):
        copies = []
        for peer in range(1, count):
            target = (me + peer) % count
            copy = pltpu.make_async_remote_copy(
                src_ref=source,
                dst_ref=buf.at[me],
                send_sem=send.at[target],
                recv_sem=recv.at[me],
                device_id=target_of(target),
                device_id_type=mesh_id,
            )
            copy.start()
            copies.append((peer, copy))
        for peer, copy in copies:
            copy.wait_send()
        for peer in range(1, count):
            source_index = (me + count - peer) % count
            pltpu.make_async_remote_copy(
                src_ref=source,
                dst_ref=buf.at[source_index],
                send_sem=send.at[source_index],
                recv_sem=recv.at[source_index],
                device_id=target_of(source_index),
                device_id_type=mesh_id,
            ).wait_recv()

    gather(lon_buf, lon_send, lon_recv, lon_devices, lon_me, lambda t: (lat_me, t), part_ref)
    lon_buf[lon_me] = part_ref[...]
    total = lon_buf[0]
    for i in range(1, lon_devices):
        total = total + lon_buf[i]
    out_ref[...] = total
    gather(lat_buf, lat_send, lat_recv, lat_devices, lat_me, lambda t: (t, lon_me), out_ref)
    lat_buf[lat_me] = out_ref[...]
    total = lat_buf[0]
    for i in range(1, lat_devices):
        total = total + lat_buf[i]
    out_ref[...] = total


def allreduce_pallas(part):
    lat_devices = lax.axis_size("lat")
    lon_devices = lax.axis_size("lon")
    kernel = functools.partial(allreduce_kernel, lat_devices, lon_devices)
    return pl.pallas_call(
        kernel,
        in_specs=[pl.BlockSpec(memory_space=pltpu.VMEM)],
        out_specs=pl.BlockSpec(memory_space=pltpu.VMEM),
        out_shape=jax.ShapeDtypeStruct(part.shape, jnp.float32),
        scratch_shapes=[
            pltpu.VMEM((lon_devices,) + part.shape, jnp.float32),
            pltpu.VMEM((lat_devices,) + part.shape, jnp.float32),
            pltpu.SemaphoreType.DMA((lon_devices,)),
            pltpu.SemaphoreType.DMA((lon_devices,)),
            pltpu.SemaphoreType.DMA((lat_devices,)),
            pltpu.SemaphoreType.DMA((lat_devices,)),
        ],
        compiler_params=pltpu.CompilerParams(collective_id=0, has_side_effects=True),
    )(part)


def slots_of(block_owner, tile_count):
    targets = block_owner[:, 0]
    block_count = targets.shape[0]
    same_owner = (targets[:, None] == jnp.arange(tile_count, dtype=jnp.int32)[None, :]).astype(
        jnp.int32
    )
    order = jnp.arange(block_count, dtype=jnp.int32)
    lower = (order[:, None] > order[None, :]).astype(jnp.int32)
    earlier = jnp.dot(lower, same_owner)
    rank_within = jnp.sum(earlier * same_owner, axis=1)
    return targets * CAP + rank_within


def mix_blocks(values, correlation):
    return jnp.einsum("vsk,ik->vsi", values, correlation, precision=precise)


def shards(
    increment,
    residual,
    direction,
    diffusivity,
    deviation,
    stencil,
    bilinear,
    obs_weight,
    block_owner,
    correlation,
):
    lat_devices = lax.axis_size("lat")
    lon_devices = lax.axis_size("lon")
    tile_count = lat_devices * lon_devices
    both = widen_halo(jnp.stack([direction, diffusivity]), STEPS + 1)
    coeffs = face_coeffs(both[1], STEPS)

    def apply_diffusion(field):
        return diffuse(widen_halo(field, STEPS), coeffs)

    slots = slots_of(block_owner, tile_count)
    slot_table = (slots[:, None] == jnp.arange(tile_count * CAP, dtype=jnp.int32)[None, :]).astype(
        jnp.float32
    )
    field_shape = direction.shape
    state_field = deviation * diffuse(both[0][:, :, 1:-1, 1:-1], coeffs)
    observed = observe_pallas(state_field, stencil, bilinear, obs_weight)
    buffer = jnp.einsum("vbk,bs->vsk", observed, slot_table, precision=precise)
    returned = lax.all_to_all(
        mix_blocks(
            lax.all_to_all(buffer, ("lat", "lon"), split_axis=1, concat_axis=1, tiled=True),
            correlation,
        ),
        ("lat", "lon"),
        split_axis=1,
        concat_axis=1,
        tiled=True,
    )
    weighted = obs_weight * jnp.einsum("vsk,bs->vbk", returned, slot_table, precision=precise)
    spread_field = deviation * spread_pallas(weighted, stencil, bilinear, field_shape)
    image_field = direction + apply_diffusion(spread_field)
    local_sums = jnp.stack(
        [
            jnp.sum(residual * residual),
            jnp.sum(direction * image_field),
            jnp.sum(residual * image_field),
            jnp.sum(image_field * image_field),
        ]
    )
    sums = allreduce_pallas(jnp.zeros((8, 128), jnp.float32).at[0, :4].set(local_sums))[0]
    norm_now, curvature, cross, image_norm = sums[0], sums[1], sums[2], sums[3]
    step_size = norm_now / curvature
    increment = increment + step_size * direction
    residual = residual - step_size * image_field
    norm_next = norm_now - 2.0 * step_size * cross + step_size * step_size * image_norm
    direction = residual + norm_next / norm_now * direction
    return (increment, residual, direction)


def solution(mesh):
    in_specs = (
        P(None, None, "lon", "lat"),
        P(None, None, "lon", "lat"),
        P(None, None, "lon", "lat"),
        P(None, None, "lon", "lat"),
        P(None, None, "lon", "lat"),
        P(("lat", "lon"), None),
        P(("lat", "lon"), None, None),
        P(None, ("lat", "lon"), None),
        P(("lat", "lon"), None),
        P(("lat", "lon"), None),
    )
    out_specs = (
        P(None, None, "lon", "lat"),
        P(None, None, "lon", "lat"),
        P(None, None, "lon", "lat"),
    )
    return jax.shard_map(shards, mesh=mesh, in_specs=in_specs, out_specs=out_specs, check_vma=False)
```

```python
import functools
import math

import jax
import jax.numpy as jnp
from jax import lax
from jax.experimental import pallas as pl
from jax.experimental.pallas import tpu as pltpu
from jax.sharding import PartitionSpec as P

STEPS = 4
CAP = 2


precise = lax.Precision.HIGHEST


def face_coeffs(wide, width):
    lat_count = wide.shape[3] - 2 * (width + 1)
    lat_devices = lax.axis_size("lat")
    first = lax.axis_index("lat") * lat_count - width
    cells = first + jnp.arange(lat_count + 2 * width, dtype=jnp.int32)
    inside = ((cells >= 0) & (cells < lat_devices * lat_count)).astype(jnp.float32)
    centre = wide[:, :, 1:-1, 1:-1]
    return (
        inside * (0.5 * (centre + wide[:, :, 1:-1, 2:])),
        inside * (0.5 * (centre + wide[:, :, 1:-1, :-2])),
        inside * (0.5 * (centre + wide[:, :, 2:, 1:-1])),
        inside * (0.5 * (centre + wide[:, :, :-2, 1:-1])),
    )


def diffuse(field, coeffs):
    for sweep in range(STEPS):
        lon_end = field.shape[2] - 1
        lat_end = field.shape[3] - 1
        here = field[:, :, 1:lon_end, 1:lat_end]
        edge = sweep + 1
        north_face, south_face, east_face, west_face = (
            c[:, :, edge : c.shape[2] - edge, edge : c.shape[3] - edge] for c in coeffs
        )
        field = (
            here
            + north_face * (field[:, :, 1:lon_end, 2:] - here)
            + south_face * (field[:, :, 1:lon_end, : lat_end - 1] - here)
            + east_face * (field[:, :, 2:, 1:lat_end] - here)
            + west_face * (field[:, :, : lon_end - 1, 1:lat_end] - here)
        )
    return field


PARTS = 3


def split_parts(value):
    parts = []
    rest = value
    for part in range(PARTS):
        piece = rest.astype(jnp.bfloat16)
        parts.append(piece)
        rest = rest - piece.astype(jnp.float32)
    return parts


def obs_lines(cell_ref, weight_ref, group, lat_count):
    cells = cell_ref[...]
    rows = cells // lat_count
    lats = cells - rows * lat_count
    row_line = jnp.concatenate([rows[g : g + 1, :] for g in range(group)], axis=1)
    lat_line = jnp.concatenate([lats[g : g + 1, :] for g in range(group)], axis=1)
    weights = [
        jnp.concatenate([weight_ref[g, c : c + 1, :] for g in range(group)], axis=1) for c in range(4)
    ]
    return row_line, lat_line, weights


def select_maps(row_line, lat_line, weights, row_count, lat_count):
    width = row_line.shape[1]
    row_ids = lax.broadcasted_iota(jnp.int32, (row_count, width), 0)
    near_rows = (row_ids == row_line).astype(jnp.bfloat16)
    far_rows = (row_ids == row_line + 1).astype(jnp.bfloat16)
    lat_ids = lax.broadcasted_iota(jnp.int32, (lat_count, width), 0)
    near_lat = jnp.where(lat_ids == lat_line, weights[0], 0.0) + jnp.where(
        lat_ids == lat_line + 1, weights[1], 0.0
    )
    far_lat = jnp.where(lat_ids == lat_line, weights[2], 0.0) + jnp.where(
        lat_ids == lat_line + 1, weights[3], 0.0
    )
    return near_rows, far_rows, near_lat, far_lat


def observe_kernel(group, var_count, row_count, lat_count, table_ref, cell_ref, weight_ref, scale_ref, out_ref):
    row_line, lat_line, weights = obs_lines(cell_ref, weight_ref, group, lat_count)
    near_rows, far_rows, near_lat, far_lat = select_maps(row_line, lat_line, weights, row_count, lat_count)
    table = jnp.concatenate(split_parts(table_ref[...]), axis=1)
    near_vals = jnp.dot(table, jnp.concatenate([near_rows] * PARTS, axis=0), preferred_element_type=jnp.float32)
    far_vals = jnp.dot(table, jnp.concatenate([far_rows] * PARTS, axis=0), preferred_element_type=jnp.float32)
    for v in range(var_count):
        span = slice(v * lat_count, (v + 1) * lat_count)
        line = jnp.sum(near_vals[span] * near_lat + far_vals[span] * far_lat, axis=0, keepdims=True)
        for g in range(group):
            out_ref[v, g : g + 1, :] = scale_ref[v, g : g + 1, :] * line[:, g * 128 : (g + 1) * 128]


def spread_kernel(group, var_count, row_count, lat_count, value_ref, cell_ref, weight_ref, out_ref):
    @pl.when(pl.program_id(0) == 0)
    def _():
        out_ref[...] = jnp.zeros_like(out_ref)

    row_line, lat_line, weights = obs_lines(cell_ref, weight_ref, group, lat_count)
    near_rows, far_rows, near_lat, far_lat = select_maps(row_line, lat_line, weights, row_count, lat_count)
    near_parts, far_parts = [], []
    for v in range(var_count):
        line = jnp.concatenate([value_ref[v, g : g + 1, :] for g in range(group)], axis=1)
        near_parts.append(near_lat * line)
        far_parts.append(far_lat * line)
    near_split = split_parts(jnp.concatenate(near_parts, axis=0))
    far_split = split_parts(jnp.concatenate(far_parts, axis=0))
    lhs = jnp.concatenate(near_split + far_split, axis=1)
    rhs = jnp.concatenate([near_rows] * PARTS + [far_rows] * PARTS, axis=1)
    out_ref[...] += lax.dot_general(
        lhs, rhs, (((1,), (1,)), ((), ())), preferred_element_type=jnp.float32
    )


def observe_pallas(field, stencil, bilinear, obs_weight, group=8):
    var_count, level_count, lon_count, lat_count = field.shape
    row_count = level_count * lon_count
    block_count = stencil.shape[0]
    rows_t = jnp.transpose(field.reshape(var_count, row_count, lat_count), (0, 2, 1))
    table = rows_t.reshape(var_count * lat_count, row_count)
    kernel = functools.partial(observe_kernel, group, var_count, row_count, lat_count)
    width = group * stencil.shape[1]
    flops = 2 * 2 * var_count * lat_count * PARTS * row_count * width * (block_count // group)
    return pl.pallas_call(
        kernel,
        grid=(block_count // group,),
        in_specs=[
            pl.BlockSpec(table.shape, lambda i: (0, 0)),
            pl.BlockSpec((group, stencil.shape[1]), lambda i: (i, 0)),
            pl.BlockSpec((group, 4, stencil.shape[1]), lambda i: (i, 0, 0)),
            pl.BlockSpec((var_count, group, stencil.shape[1]), lambda i: (0, i, 0)),
        ],
        out_specs=pl.BlockSpec((var_count, group, stencil.shape[1]), lambda i: (0, i, 0)),
        out_shape=jax.ShapeDtypeStruct(obs_weight.shape, jnp.float32),
        cost_estimate=pl.CostEstimate(flops=flops, transcendentals=0, bytes_accessed=4 * 1024 * 1024),
    )(table, stencil, bilinear, obs_weight)


def spread_pallas(values, stencil, bilinear, field_shape, group=8):
    var_count, level_count, lon_count, lat_count = field_shape
    row_count = level_count * lon_count
    block_count = stencil.shape[0]
    kernel = functools.partial(spread_kernel, group, var_count, row_count, lat_count)
    width = group * stencil.shape[1]
    flops = 2 * 2 * var_count * lat_count * PARTS * row_count * width * (block_count // group)
    total = pl.pallas_call(
        kernel,
        grid=(block_count // group,),
        in_specs=[
            pl.BlockSpec((var_count, group, stencil.shape[1]), lambda i: (0, i, 0)),
            pl.BlockSpec((group, stencil.shape[1]), lambda i: (i, 0)),
            pl.BlockSpec((group, 4, stencil.shape[1]), lambda i: (i, 0, 0)),
        ],
        out_specs=pl.BlockSpec((var_count * lat_count, row_count), lambda i: (0, 0)),
        out_shape=jax.ShapeDtypeStruct((var_count * lat_count, row_count), jnp.float32),
        cost_estimate=pl.CostEstimate(flops=flops, transcendentals=0, bytes_accessed=4 * 1024 * 1024),
    )(values, stencil, bilinear)
    total = jnp.transpose(total.reshape(var_count, lat_count, row_count), (0, 2, 1))
    return total.reshape(field_shape)


SIDES = tuple((lat_side, lon_side) for lat_side in (-1, 0, 1) for lon_side in (-1, 0, 1) if lat_side or lon_side)


def halo_kernel(lat_devices, lon_devices, *refs):
    count = len(SIDES)
    send_refs, out_refs = refs[:count], refs[count : 2 * count]
    held_refs = refs[2 * count : 3 * count]
    send_sems, recv_sems = refs[3 * count], refs[3 * count + 1]
    mesh_id = pl.DeviceIdType.MESH
    lat_me = lax.axis_index("lat")
    lon_me = lax.axis_index("lon")

    def lat_ok(index):
        return jnp.logical_and(index >= 0, index < lat_devices)

    def remote(k, lat_to, lon_to):
        return pltpu.make_async_remote_copy(
            src_ref=send_refs[k],
            dst_ref=held_refs[k],
            send_sem=send_sems.at[k],
            recv_sem=recv_sems.at[k],
            device_id=(lat_to, lon_to),
            device_id_type=mesh_id,
        )

    barrier = pltpu.get_barrier_semaphore()
    for lat_side, lon_side in SIDES:
        peer_lat = lat_me + lat_side

        @pl.when(lat_ok(peer_lat))
        def _():
            pl.semaphore_signal(
                barrier, inc=1, device_id=(peer_lat, (lon_me + lon_side + lon_devices) % lon_devices), device_id_type=mesh_id
            )

    edges = (lat_devices - 1 - lat_me) // max(lat_devices - 1, 1) + lat_me // max(lat_devices - 1, 1)
    pl.semaphore_wait(barrier, len(SIDES) - 3 * edges)

    for k, (lat_side, lon_side) in enumerate(SIDES):
        lat_to = lat_me - lat_side
        lon_to = (lon_me - lon_side + lon_devices) % lon_devices

        @pl.when(lat_ok(lat_to))
        def _():
            remote(k, lat_to, lon_to).start()

    for k, (lat_side, lon_side) in enumerate(SIDES):
        lat_to = lat_me - lat_side
        lon_to = (lon_me - lon_side + lon_devices) % lon_devices

        @pl.when(lat_ok(lat_to))
        def _():
            remote(k, lat_to, lon_to).wait_send()

    for k, (lat_side, lon_side) in enumerate(SIDES):
        lat_from = lat_me + lat_side
        lon_from = (lon_me + lon_side + lon_devices) % lon_devices

        @pl.when(lat_ok(lat_from))
        def _():
            remote(k, lat_from, lon_from).wait_recv()
            out_refs[k][...] = held_refs[k][...]

        @pl.when(jnp.logical_not(lat_ok(lat_from)))
        def _():
            out_refs[k][...] = jnp.zeros_like(out_refs[k])


def span(side, count, width):
    return {-1: slice(count - width, count), 0: slice(0, count), 1: slice(0, width)}[side]


def pack_piece(value, side, width):
    lat_side, lon_side = side
    planes, lon_count, lat_count = value.shape
    piece = value[:, span(lon_side, lon_count, width), span(lat_side, lat_count, width)]
    if lon_side == 0:
        return jnp.transpose(piece, (2, 0, 1)).reshape(width, planes * lon_count)
    if lat_side == 0:
        return piece.reshape(planes * width, lat_count)
    return jnp.transpose(piece, (1, 2, 0)).reshape(width * width, planes)


def unpack_piece(packed, side, width, planes, lon_count, lat_count):
    lat_side, lon_side = side
    if lon_side == 0:
        return jnp.transpose(packed.reshape(width, planes, lon_count), (1, 2, 0))
    if lat_side == 0:
        return packed.reshape(planes, width, lat_count)
    return jnp.transpose(packed.reshape(width, width, planes), (2, 0, 1))


def halo_pallas(value, width, collective):
    lat_devices = lax.axis_size("lat")
    lon_devices = lax.axis_size("lon")
    lead = value.shape[:-2]
    lon_count, lat_count = value.shape[-2:]
    flat = value.reshape((-1, lon_count, lat_count))
    planes = flat.shape[0]
    packed = [pack_piece(flat, side, width) for side in SIDES]
    kernel = functools.partial(halo_kernel, lat_devices, lon_devices)
    vmem = pl.BlockSpec(memory_space=pltpu.VMEM)
    received = pl.pallas_call(
        kernel,
        in_specs=[vmem] * len(SIDES),
        out_specs=[vmem] * len(SIDES),
        out_shape=[jax.ShapeDtypeStruct(p.shape, p.dtype) for p in packed],
        scratch_shapes=[pltpu.VMEM(p.shape, p.dtype) for p in packed]
        + [pltpu.SemaphoreType.DMA((len(SIDES),)), pltpu.SemaphoreType.DMA((len(SIDES),))],
        compiler_params=pltpu.CompilerParams(collective_id=collective, has_side_effects=True),
    )(*packed)
    pieces = {side: unpack_piece(r, side, width, planes, lon_count, lat_count) for side, r in zip(SIDES, received)}
    pieces[(0, 0)] = flat
    rows = [
        jnp.concatenate([pieces[(lat_side, lon_side)] for lat_side in (-1, 0, 1)], axis=2)
        for lon_side in (-1, 0, 1)
    ]
    wide = jnp.concatenate(rows, axis=1)
    return wide.reshape(lead + (lon_count + 2 * width, lat_count + 2 * width))


def allreduce_kernel(lat_devices, lon_devices, part_ref, out_ref, lon_buf, lat_buf, lon_send, lon_recv, lat_send, lat_recv):
    mesh_id = pl.DeviceIdType.MESH
    lat_me = lax.axis_index("lat")
    lon_me = lax.axis_index("lon")
    barrier = pltpu.get_barrier_semaphore()
    for peer in range(1, lon_devices):
        pl.semaphore_signal(barrier, inc=1, device_id=(lat_me, (lon_me + peer) % lon_devices), device_id_type=mesh_id)
    for peer in range(1, lat_devices):
        pl.semaphore_signal(barrier, inc=1, device_id=((lat_me + peer) % lat_devices, lon_me), device_id_type=mesh_id)
    pl.semaphore_wait(barrier, lon_devices + lat_devices - 2)

    def gather(buf, send, recv, count, me, target_of, source):
        copies = []
        for peer in range(1, count):
            target = (me + peer) % count
            copy = pltpu.make_async_remote_copy(
                src_ref=source,
                dst_ref=buf.at[me],
                send_sem=send.at[target],
                recv_sem=recv.at[me],
                device_id=target_of(target),
                device_id_type=mesh_id,
            )
            copy.start()
            copies.append((peer, copy))
        for peer, copy in copies:
            copy.wait_send()
        for peer in range(1, count):
            source_index = (me + count - peer) % count
            pltpu.make_async_remote_copy(
                src_ref=source,
                dst_ref=buf.at[source_index],
                send_sem=send.at[source_index],
                recv_sem=recv.at[source_index],
                device_id=target_of(source_index),
                device_id_type=mesh_id,
            ).wait_recv()

    gather(lon_buf, lon_send, lon_recv, lon_devices, lon_me, lambda t: (lat_me, t), part_ref)
    lon_buf[lon_me] = part_ref[...]
    total = lon_buf[0]
    for i in range(1, lon_devices):
        total = total + lon_buf[i]
    out_ref[...] = total
    gather(lat_buf, lat_send, lat_recv, lat_devices, lat_me, lambda t: (t, lon_me), out_ref)
    lat_buf[lat_me] = out_ref[...]
    total = lat_buf[0]
    for i in range(1, lat_devices):
        total = total + lat_buf[i]
    out_ref[...] = total


def allreduce_pallas(part):
    lat_devices = lax.axis_size("lat")
    lon_devices = lax.axis_size("lon")
    kernel = functools.partial(allreduce_kernel, lat_devices, lon_devices)
    return pl.pallas_call(
        kernel,
        in_specs=[pl.BlockSpec(memory_space=pltpu.VMEM)],
        out_specs=pl.BlockSpec(memory_space=pltpu.VMEM),
        out_shape=jax.ShapeDtypeStruct(part.shape, jnp.float32),
        scratch_shapes=[
            pltpu.VMEM((lon_devices,) + part.shape, jnp.float32),
            pltpu.VMEM((lat_devices,) + part.shape, jnp.float32),
            pltpu.SemaphoreType.DMA((lon_devices,)),
            pltpu.SemaphoreType.DMA((lon_devices,)),
            pltpu.SemaphoreType.DMA((lat_devices,)),
            pltpu.SemaphoreType.DMA((lat_devices,)),
        ],
        compiler_params=pltpu.CompilerParams(collective_id=0, has_side_effects=True),
    )(part)


def slots_of(block_owner, tile_count):
    targets = block_owner[:, 0]
    block_count = targets.shape[0]
    same_owner = (targets[:, None] == jnp.arange(tile_count, dtype=jnp.int32)[None, :]).astype(
        jnp.int32
    )
    order = jnp.arange(block_count, dtype=jnp.int32)
    lower = (order[:, None] > order[None, :]).astype(jnp.int32)
    earlier = jnp.dot(lower, same_owner)
    rank_within = jnp.sum(earlier * same_owner, axis=1)
    return targets * CAP + rank_within


def mix_blocks(values, correlation):
    return jnp.einsum("vsk,ik->vsi", values, correlation, precision=precise)


def shards(
    increment,
    residual,
    direction,
    diffusivity,
    deviation,
    stencil,
    bilinear,
    obs_weight,
    block_owner,
    correlation,
):
    lat_devices = lax.axis_size("lat")
    lon_devices = lax.axis_size("lon")
    tile_count = lat_devices * lon_devices
    both = halo_pallas(jnp.stack([direction, diffusivity]), STEPS + 1, 1)
    coeffs = face_coeffs(both[1], STEPS)

    def apply_diffusion(field):
        return diffuse(halo_pallas(field, STEPS, 2), coeffs)

    slots = slots_of(block_owner, tile_count)
    slot_table = (slots[:, None] == jnp.arange(tile_count * CAP, dtype=jnp.int32)[None, :]).astype(
        jnp.float32
    )
    field_shape = direction.shape
    state_field = deviation * diffuse(both[0][:, :, 1:-1, 1:-1], coeffs)
    observed = observe_pallas(state_field, stencil, bilinear, obs_weight)
    buffer = jnp.einsum("vbk,bs->vsk", observed, slot_table, precision=precise)
    returned = lax.all_to_all(
        mix_blocks(
            lax.all_to_all(buffer, ("lat", "lon"), split_axis=1, concat_axis=1, tiled=True),
            correlation,
        ),
        ("lat", "lon"),
        split_axis=1,
        concat_axis=1,
        tiled=True,
    )
    weighted = obs_weight * jnp.einsum("vsk,bs->vbk", returned, slot_table, precision=precise)
    spread_field = deviation * spread_pallas(weighted, stencil, bilinear, field_shape)
    image_field = direction + apply_diffusion(spread_field)
    local_sums = jnp.stack(
        [
            jnp.sum(residual * residual),
            jnp.sum(direction * image_field),
            jnp.sum(residual * image_field),
            jnp.sum(image_field * image_field),
        ]
    )
    sums = allreduce_pallas(jnp.zeros((8, 128), jnp.float32).at[0, :4].set(local_sums))[0]
    norm_now, curvature, cross, image_norm = sums[0], sums[1], sums[2], sums[3]
    step_size = norm_now / curvature
    increment = increment + step_size * direction
    residual = residual - step_size * image_field
    norm_next = norm_now - 2.0 * step_size * cross + step_size * step_size * image_norm
    direction = residual + norm_next / norm_now * direction
    return (increment, residual, direction)


def solution(mesh):
    in_specs = (
        P(None, None, "lon", "lat"),
        P(None, None, "lon", "lat"),
        P(None, None, "lon", "lat"),
        P(None, None, "lon", "lat"),
        P(None, None, "lon", "lat"),
        P(("lat", "lon"), None),
        P(("lat", "lon"), None, None),
        P(None, ("lat", "lon"), None),
        P(("lat", "lon"), None),
        P(("lat", "lon"), None),
    )
    out_specs = (
        P(None, None, "lon", "lat"),
        P(None, None, "lon", "lat"),
        P(None, None, "lon", "lat"),
    )
    return jax.shard_map(shards, mesh=mesh, in_specs=in_specs, out_specs=out_specs, check_vma=False)
```

```python
import functools
import math

import jax
import jax.numpy as jnp
from jax import lax
from jax.experimental import pallas as pl
from jax.experimental.pallas import tpu as pltpu
from jax.sharding import PartitionSpec as P

STEPS = 4
CAP = 2


precise = lax.Precision.HIGHEST


def widen_halo(value, width):
    lat_dim, lon_dim = value.ndim - 1, value.ndim - 2
    for axis, dim, wrap in (("lat", lat_dim, False), ("lon", lon_dim, True)):
        size, length = lax.axis_size(axis), value.shape[dim]
        up = [(i, (i + 1) % size) for i in range(size if wrap else size - 1)]
        down = [(j, i) for i, j in up]
        before = lax.ppermute(lax.slice_in_dim(value, length - width, length, axis=dim), axis, up)
        after = lax.ppermute(lax.slice_in_dim(value, 0, width, axis=dim), axis, down)
        value = jnp.concatenate([before, value, after], axis=dim)
    return value


def face_coeffs(wide, width):
    lat_count = wide.shape[3] - 2 * (width + 1)
    lat_devices = lax.axis_size("lat")
    first = lax.axis_index("lat") * lat_count - width
    cells = first + jnp.arange(lat_count + 2 * width, dtype=jnp.int32)
    inside = ((cells >= 0) & (cells < lat_devices * lat_count)).astype(jnp.float32)
    centre = wide[:, :, 1:-1, 1:-1]
    return (
        inside * (0.5 * (centre + wide[:, :, 1:-1, 2:])),
        inside * (0.5 * (centre + wide[:, :, 1:-1, :-2])),
        inside * (0.5 * (centre + wide[:, :, 2:, 1:-1])),
        inside * (0.5 * (centre + wide[:, :, :-2, 1:-1])),
    )


def diffuse(field, coeffs):
    for sweep in range(STEPS):
        lon_end = field.shape[2] - 1
        lat_end = field.shape[3] - 1
        here = field[:, :, 1:lon_end, 1:lat_end]
        edge = sweep + 1
        north_face, south_face, east_face, west_face = (
            c[:, :, edge : c.shape[2] - edge, edge : c.shape[3] - edge] for c in coeffs
        )
        field = (
            here
            + north_face * (field[:, :, 1:lon_end, 2:] - here)
            + south_face * (field[:, :, 1:lon_end, : lat_end - 1] - here)
            + east_face * (field[:, :, 2:, 1:lat_end] - here)
            + west_face * (field[:, :, : lon_end - 1, 1:lat_end] - here)
        )
    return field


PARTS = 2


def split_parts(value):
    parts = []
    rest = value
    for part in range(PARTS):
        piece = rest.astype(jnp.bfloat16)
        parts.append(piece)
        rest = rest - piece.astype(jnp.float32)
    return parts


def obs_lines(cell_ref, weight_ref, group, lat_count):
    cells = cell_ref[...]
    rows = cells // lat_count
    lats = cells - rows * lat_count
    row_line = jnp.concatenate([rows[g : g + 1, :] for g in range(group)], axis=1)
    lat_line = jnp.concatenate([lats[g : g + 1, :] for g in range(group)], axis=1)
    weights = [
        jnp.concatenate([weight_ref[g, c : c + 1, :] for g in range(group)], axis=1) for c in range(4)
    ]
    return row_line, lat_line, weights


def select_maps(row_line, lat_line, weights, row_count, lat_count):
    width = row_line.shape[1]
    row_ids = lax.broadcasted_iota(jnp.int32, (row_count, width), 0)
    near_rows = (row_ids == row_line).astype(jnp.bfloat16)
    far_rows = (row_ids == row_line + 1).astype(jnp.bfloat16)
    lat_ids = lax.broadcasted_iota(jnp.int32, (lat_count, width), 0)
    near_lat = jnp.where(lat_ids == lat_line, weights[0], 0.0) + jnp.where(
        lat_ids == lat_line + 1, weights[1], 0.0
    )
    far_lat = jnp.where(lat_ids == lat_line, weights[2], 0.0) + jnp.where(
        lat_ids == lat_line + 1, weights[3], 0.0
    )
    return near_rows, far_rows, near_lat, far_lat


def observe_kernel(group, var_count, row_count, lat_count, table_ref, cell_ref, weight_ref, scale_ref, out_ref):
    row_line, lat_line, weights = obs_lines(cell_ref, weight_ref, group, lat_count)
    near_rows, far_rows, near_lat, far_lat = select_maps(row_line, lat_line, weights, row_count, lat_count)
    table = jnp.concatenate(split_parts(table_ref[...]), axis=1)
    near_vals = jnp.dot(table, jnp.concatenate([near_rows] * PARTS, axis=0), preferred_element_type=jnp.float32)
    far_vals = jnp.dot(table, jnp.concatenate([far_rows] * PARTS, axis=0), preferred_element_type=jnp.float32)
    for v in range(var_count):
        span = slice(v * lat_count, (v + 1) * lat_count)
        line = jnp.sum(near_vals[span] * near_lat + far_vals[span] * far_lat, axis=0, keepdims=True)
        for g in range(group):
            out_ref[v, g : g + 1, :] = scale_ref[v, g : g + 1, :] * line[:, g * 128 : (g + 1) * 128]


def spread_kernel(group, var_count, row_count, lat_count, value_ref, cell_ref, weight_ref, out_ref):
    @pl.when(pl.program_id(0) == 0)
    def _():
        out_ref[...] = jnp.zeros_like(out_ref)

    row_line, lat_line, weights = obs_lines(cell_ref, weight_ref, group, lat_count)
    near_rows, far_rows, near_lat, far_lat = select_maps(row_line, lat_line, weights, row_count, lat_count)
    near_parts, far_parts = [], []
    for v in range(var_count):
        line = jnp.concatenate([value_ref[v, g : g + 1, :] for g in range(group)], axis=1)
        near_parts.append(near_lat * line)
        far_parts.append(far_lat * line)
    near_split = split_parts(jnp.concatenate(near_parts, axis=0))
    far_split = split_parts(jnp.concatenate(far_parts, axis=0))
    lhs = jnp.concatenate(near_split + far_split, axis=1)
    rhs = jnp.concatenate([near_rows] * PARTS + [far_rows] * PARTS, axis=1)
    out_ref[...] += lax.dot_general(
        lhs, rhs, (((1,), (1,)), ((), ())), preferred_element_type=jnp.float32
    )


def observe_pallas(field, stencil, bilinear, obs_weight, group=8):
    var_count, level_count, lon_count, lat_count = field.shape
    row_count = level_count * lon_count
    block_count = stencil.shape[0]
    rows_t = jnp.transpose(field.reshape(var_count, row_count, lat_count), (0, 2, 1))
    table = rows_t.reshape(var_count * lat_count, row_count)
    kernel = functools.partial(observe_kernel, group, var_count, row_count, lat_count)
    width = group * stencil.shape[1]
    flops = 2 * 2 * var_count * lat_count * PARTS * row_count * width * (block_count // group)
    return pl.pallas_call(
        kernel,
        grid=(block_count // group,),
        in_specs=[
            pl.BlockSpec(table.shape, lambda i: (0, 0)),
            pl.BlockSpec((group, stencil.shape[1]), lambda i: (i, 0)),
            pl.BlockSpec((group, 4, stencil.shape[1]), lambda i: (i, 0, 0)),
            pl.BlockSpec((var_count, group, stencil.shape[1]), lambda i: (0, i, 0)),
        ],
        out_specs=pl.BlockSpec((var_count, group, stencil.shape[1]), lambda i: (0, i, 0)),
        out_shape=jax.ShapeDtypeStruct(obs_weight.shape, jnp.float32),
        cost_estimate=pl.CostEstimate(flops=flops, transcendentals=0, bytes_accessed=4 * 1024 * 1024),
    )(table, stencil, bilinear, obs_weight)


def spread_pallas(values, stencil, bilinear, field_shape, group=8):
    var_count, level_count, lon_count, lat_count = field_shape
    row_count = level_count * lon_count
    block_count = stencil.shape[0]
    kernel = functools.partial(spread_kernel, group, var_count, row_count, lat_count)
    width = group * stencil.shape[1]
    flops = 2 * 2 * var_count * lat_count * PARTS * row_count * width * (block_count // group)
    total = pl.pallas_call(
        kernel,
        grid=(block_count // group,),
        in_specs=[
            pl.BlockSpec((var_count, group, stencil.shape[1]), lambda i: (0, i, 0)),
            pl.BlockSpec((group, stencil.shape[1]), lambda i: (i, 0)),
            pl.BlockSpec((group, 4, stencil.shape[1]), lambda i: (i, 0, 0)),
        ],
        out_specs=pl.BlockSpec((var_count * lat_count, row_count), lambda i: (0, 0)),
        out_shape=jax.ShapeDtypeStruct((var_count * lat_count, row_count), jnp.float32),
        cost_estimate=pl.CostEstimate(flops=flops, transcendentals=0, bytes_accessed=4 * 1024 * 1024),
    )(values, stencil, bilinear)
    total = jnp.transpose(total.reshape(var_count, lat_count, row_count), (0, 2, 1))
    return total.reshape(field_shape)


def allreduce_kernel(lat_devices, lon_devices, part_ref, out_ref, lon_buf, lat_buf, lon_send, lon_recv, lat_send, lat_recv):
    mesh_id = pl.DeviceIdType.MESH
    lat_me = lax.axis_index("lat")
    lon_me = lax.axis_index("lon")
    barrier = pltpu.get_barrier_semaphore()
    for peer in range(1, lon_devices):
        pl.semaphore_signal(barrier, inc=1, device_id=(lat_me, (lon_me + peer) % lon_devices), device_id_type=mesh_id)
    for peer in range(1, lat_devices):
        pl.semaphore_signal(barrier, inc=1, device_id=((lat_me + peer) % lat_devices, lon_me), device_id_type=mesh_id)
    pl.semaphore_wait(barrier, lon_devices + lat_devices - 2)

    def gather(buf, send, recv, count, me, target_of, source):
        copies = []
        for peer in range(1, count):
            target = (me + peer) % count
            copy = pltpu.make_async_remote_copy(
                src_ref=source,
                dst_ref=buf.at[me],
                send_sem=send.at[target],
                recv_sem=recv.at[me],
                device_id=target_of(target),
                device_id_type=mesh_id,
            )
            copy.start()
            copies.append((peer, copy))
        for peer, copy in copies:
            copy.wait_send()
        for peer in range(1, count):
            source_index = (me + count - peer) % count
            pltpu.make_async_remote_copy(
                src_ref=source,
                dst_ref=buf.at[source_index],
                send_sem=send.at[source_index],
                recv_sem=recv.at[source_index],
                device_id=target_of(source_index),
                device_id_type=mesh_id,
            ).wait_recv()

    gather(lon_buf, lon_send, lon_recv, lon_devices, lon_me, lambda t: (lat_me, t), part_ref)
    lon_buf[lon_me] = part_ref[...]
    total = lon_buf[0]
    for i in range(1, lon_devices):
        total = total + lon_buf[i]
    out_ref[...] = total
    gather(lat_buf, lat_send, lat_recv, lat_devices, lat_me, lambda t: (t, lon_me), out_ref)
    lat_buf[lat_me] = out_ref[...]
    total = lat_buf[0]
    for i in range(1, lat_devices):
        total = total + lat_buf[i]
    out_ref[...] = total


def allreduce_pallas(part):
    lat_devices = lax.axis_size("lat")
    lon_devices = lax.axis_size("lon")
    kernel = functools.partial(allreduce_kernel, lat_devices, lon_devices)
    return pl.pallas_call(
        kernel,
        in_specs=[pl.BlockSpec(memory_space=pltpu.VMEM)],
        out_specs=pl.BlockSpec(memory_space=pltpu.VMEM),
        out_shape=jax.ShapeDtypeStruct(part.shape, jnp.float32),
        scratch_shapes=[
            pltpu.VMEM((lon_devices,) + part.shape, jnp.float32),
            pltpu.VMEM((lat_devices,) + part.shape, jnp.float32),
            pltpu.SemaphoreType.DMA((lon_devices,)),
            pltpu.SemaphoreType.DMA((lon_devices,)),
            pltpu.SemaphoreType.DMA((lat_devices,)),
            pltpu.SemaphoreType.DMA((lat_devices,)),
        ],
        compiler_params=pltpu.CompilerParams(collective_id=0, has_side_effects=True),
    )(part)


def slots_of(block_owner, tile_count):
    targets = block_owner[:, 0]
    block_count = targets.shape[0]
    same_owner = (targets[:, None] == jnp.arange(tile_count, dtype=jnp.int32)[None, :]).astype(
        jnp.int32
    )
    order = jnp.arange(block_count, dtype=jnp.int32)
    lower = (order[:, None] > order[None, :]).astype(jnp.int32)
    earlier = jnp.dot(lower, same_owner)
    rank_within = jnp.sum(earlier * same_owner, axis=1)
    return targets * CAP + rank_within


def mix_blocks(values, correlation):
    return jnp.einsum("vsk,ik->vsi", values, correlation, precision=precise)


def shards(
    increment,
    residual,
    direction,
    diffusivity,
    deviation,
    stencil,
    bilinear,
    obs_weight,
    block_owner,
    correlation,
):
    lat_devices = lax.axis_size("lat")
    lon_devices = lax.axis_size("lon")
    tile_count = lat_devices * lon_devices
    both = widen_halo(jnp.stack([direction, diffusivity]), STEPS + 1)
    coeffs = face_coeffs(both[1], STEPS)

    def apply_diffusion(field):
        return diffuse(widen_halo(field, STEPS), coeffs)

    slots = slots_of(block_owner, tile_count)
    slot_table = (slots[:, None] == jnp.arange(tile_count * CAP, dtype=jnp.int32)[None, :]).astype(
        jnp.float32
    )
    field_shape = direction.shape
    state_field = deviation * diffuse(both[0][:, :, 1:-1, 1:-1], coeffs)
    observed = observe_pallas(state_field, stencil, bilinear, obs_weight)
    buffer = jnp.einsum("vbk,bs->vsk", observed, slot_table, precision=precise)
    returned = lax.all_to_all(
        mix_blocks(
            lax.all_to_all(buffer, ("lat", "lon"), split_axis=1, concat_axis=1, tiled=True),
            correlation,
        ),
        ("lat", "lon"),
        split_axis=1,
        concat_axis=1,
        tiled=True,
    )
    weighted = obs_weight * jnp.einsum("vsk,bs->vbk", returned, slot_table, precision=precise)
    spread_field = deviation * spread_pallas(weighted, stencil, bilinear, field_shape)
    image_field = direction + apply_diffusion(spread_field)
    local_sums = jnp.stack(
        [
            jnp.sum(residual * residual),
            jnp.sum(direction * image_field),
            jnp.sum(residual * image_field),
            jnp.sum(image_field * image_field),
        ]
    )
    sums = allreduce_pallas(jnp.zeros((8, 128), jnp.float32).at[0, :4].set(local_sums))[0]
    norm_now, curvature, cross, image_norm = sums[0], sums[1], sums[2], sums[3]
    step_size = norm_now / curvature
    increment = increment + step_size * direction
    residual = residual - step_size * image_field
    norm_next = norm_now - 2.0 * step_size * cross + step_size * step_size * image_norm
    direction = residual + norm_next / norm_now * direction
    return (increment, residual, direction)


def solution(mesh):
    in_specs = (
        P(None, None, "lon", "lat"),
        P(None, None, "lon", "lat"),
        P(None, None, "lon", "lat"),
        P(None, None, "lon", "lat"),
        P(None, None, "lon", "lat"),
        P(("lat", "lon"), None),
        P(("lat", "lon"), None, None),
        P(None, ("lat", "lon"), None),
        P(("lat", "lon"), None),
        P(("lat", "lon"), None),
    )
    out_specs = (
        P(None, None, "lon", "lat"),
        P(None, None, "lon", "lat"),
        P(None, None, "lon", "lat"),
    )
    return jax.shard_map(shards, mesh=mesh, in_specs=in_specs, out_specs=out_specs, check_vma=False)
```

```python
import functools
import math

import jax
import jax.numpy as jnp
from jax import lax
from jax.experimental import pallas as pl
from jax.experimental.pallas import tpu as pltpu
from jax.sharding import PartitionSpec as P

STEPS = 4
CAP = 2


precise = lax.Precision.HIGHEST


def widen_halo(value, width):
    lat_dim, lon_dim = value.ndim - 1, value.ndim - 2
    for axis, dim, wrap in (("lat", lat_dim, False), ("lon", lon_dim, True)):
        size, length = lax.axis_size(axis), value.shape[dim]
        up = [(i, (i + 1) % size) for i in range(size if wrap else size - 1)]
        down = [(j, i) for i, j in up]
        before = lax.ppermute(lax.slice_in_dim(value, length - width, length, axis=dim), axis, up)
        after = lax.ppermute(lax.slice_in_dim(value, 0, width, axis=dim), axis, down)
        value = jnp.concatenate([before, value, after], axis=dim)
    return value


def face_coeffs(wide, width):
    lat_count = wide.shape[3] - 2 * (width + 1)
    lat_devices = lax.axis_size("lat")
    first = lax.axis_index("lat") * lat_count - width
    cells = first + jnp.arange(lat_count + 2 * width, dtype=jnp.int32)
    inside = ((cells >= 0) & (cells < lat_devices * lat_count)).astype(jnp.float32)
    centre = wide[:, :, 1:-1, 1:-1]
    return (
        inside * (0.5 * (centre + wide[:, :, 1:-1, 2:])),
        inside * (0.5 * (centre + wide[:, :, 1:-1, :-2])),
        inside * (0.5 * (centre + wide[:, :, 2:, 1:-1])),
        inside * (0.5 * (centre + wide[:, :, :-2, 1:-1])),
    )


def diffuse(field, coeffs):
    for sweep in range(STEPS):
        lon_end = field.shape[2] - 1
        lat_end = field.shape[3] - 1
        here = field[:, :, 1:lon_end, 1:lat_end]
        edge = sweep + 1
        north_face, south_face, east_face, west_face = (
            c[:, :, edge : c.shape[2] - edge, edge : c.shape[3] - edge] for c in coeffs
        )
        field = (
            here
            + north_face * (field[:, :, 1:lon_end, 2:] - here)
            + south_face * (field[:, :, 1:lon_end, : lat_end - 1] - here)
            + east_face * (field[:, :, 2:, 1:lat_end] - here)
            + west_face * (field[:, :, : lon_end - 1, 1:lat_end] - here)
        )
    return field


PARTS = 2


def split_parts(value):
    parts = []
    rest = value
    for part in range(PARTS):
        piece = rest.astype(jnp.bfloat16)
        parts.append(piece)
        rest = rest - piece.astype(jnp.float32)
    return parts


def obs_lines(cell_ref, weight_ref, group, lat_count):
    cells = cell_ref[...]
    rows = cells // lat_count
    lats = cells - rows * lat_count
    row_line = jnp.concatenate([rows[g : g + 1, :] for g in range(group)], axis=1)
    lat_line = jnp.concatenate([lats[g : g + 1, :] for g in range(group)], axis=1)
    weights = [
        jnp.concatenate([weight_ref[g, c : c + 1, :] for g in range(group)], axis=1) for c in range(4)
    ]
    return row_line, lat_line, weights


def select_maps(row_line, lat_line, weights, row_count, lat_count):
    width = row_line.shape[1]
    row_ids = lax.broadcasted_iota(jnp.int32, (row_count, width), 0)
    near_rows = (row_ids == row_line).astype(jnp.bfloat16)
    lat_ids = lax.broadcasted_iota(jnp.int32, (lat_count, width), 0)
    at_first = lat_ids == lat_line
    at_second = lat_ids == lat_line + 1
    near_lat = jnp.where(at_first, weights[0], 0.0) + jnp.where(at_second, weights[1], 0.0)
    far_lat = jnp.where(at_first, weights[2], 0.0) + jnp.where(at_second, weights[3], 0.0)
    return near_rows, near_lat, far_lat


def observe_kernel(group, var_count, row_count, lat_count, table_ref, cell_ref, weight_ref, scale_ref, out_ref):
    row_line, lat_line, weights = obs_lines(cell_ref, weight_ref, group, lat_count)
    near_rows, near_lat, far_lat = select_maps(row_line, lat_line, weights, row_count, lat_count)
    table = jnp.concatenate(split_parts(table_ref[...]), axis=1)
    picked = jnp.dot(table, jnp.concatenate([near_rows] * PARTS, axis=0), preferred_element_type=jnp.float32)
    half = var_count * lat_count
    for v in range(var_count):
        near_span = slice(v * lat_count, (v + 1) * lat_count)
        far_span = slice(half + v * lat_count, half + (v + 1) * lat_count)
        line = jnp.sum(picked[near_span] * near_lat + picked[far_span] * far_lat, axis=0, keepdims=True)
        for g in range(group):
            out_ref[v, g : g + 1, :] = scale_ref[v, g : g + 1, :] * line[:, g * 128 : (g + 1) * 128]


def spread_kernel(group, var_count, row_count, lat_count, value_ref, cell_ref, weight_ref, out_ref):
    @pl.when(pl.program_id(0) == 0)
    def _():
        out_ref[...] = jnp.zeros_like(out_ref)

    row_line, lat_line, weights = obs_lines(cell_ref, weight_ref, group, lat_count)
    near_rows, near_lat, far_lat = select_maps(row_line, lat_line, weights, row_count, lat_count)
    near_parts, far_parts = [], []
    for v in range(var_count):
        line = jnp.concatenate([value_ref[v, g : g + 1, :] for g in range(group)], axis=1)
        near_parts.append(near_lat * line)
        far_parts.append(far_lat * line)
    lhs = jnp.concatenate(split_parts(jnp.concatenate(near_parts + far_parts, axis=0)), axis=1)
    rhs = jnp.concatenate([near_rows] * PARTS, axis=1)
    out_ref[...] += lax.dot_general(
        lhs, rhs, (((1,), (1,)), ((), ())), preferred_element_type=jnp.float32
    )


def observe_pallas(field, stencil, bilinear, obs_weight, group=16):
    var_count, level_count, lon_count, lat_count = field.shape
    row_count = level_count * lon_count
    block_count = stencil.shape[0]
    rows_t = jnp.transpose(field.reshape(var_count, row_count, lat_count), (0, 2, 1))
    shifted = jnp.concatenate([rows_t[:, :, 1:], jnp.zeros_like(rows_t[:, :, :1])], axis=2)
    table = jnp.concatenate([rows_t, shifted], axis=0).reshape(2 * var_count * lat_count, row_count)
    kernel = functools.partial(observe_kernel, group, var_count, row_count, lat_count)
    width = group * stencil.shape[1]
    flops = 2 * 2 * var_count * lat_count * PARTS * row_count * width * (block_count // group)
    return pl.pallas_call(
        kernel,
        grid=(block_count // group,),
        in_specs=[
            pl.BlockSpec(table.shape, lambda i: (0, 0)),
            pl.BlockSpec((group, stencil.shape[1]), lambda i: (i, 0)),
            pl.BlockSpec((group, 4, stencil.shape[1]), lambda i: (i, 0, 0)),
            pl.BlockSpec((var_count, group, stencil.shape[1]), lambda i: (0, i, 0)),
        ],
        out_specs=pl.BlockSpec((var_count, group, stencil.shape[1]), lambda i: (0, i, 0)),
        out_shape=jax.ShapeDtypeStruct(obs_weight.shape, jnp.float32),
        cost_estimate=pl.CostEstimate(flops=flops, transcendentals=0, bytes_accessed=4 * 1024 * 1024),
    )(table, stencil, bilinear, obs_weight)


def spread_pallas(values, stencil, bilinear, field_shape, group=16):
    var_count, level_count, lon_count, lat_count = field_shape
    row_count = level_count * lon_count
    block_count = stencil.shape[0]
    kernel = functools.partial(spread_kernel, group, var_count, row_count, lat_count)
    width = group * stencil.shape[1]
    flops = 2 * 2 * var_count * lat_count * PARTS * row_count * width * (block_count // group)
    total = pl.pallas_call(
        kernel,
        grid=(block_count // group,),
        in_specs=[
            pl.BlockSpec((var_count, group, stencil.shape[1]), lambda i: (0, i, 0)),
            pl.BlockSpec((group, stencil.shape[1]), lambda i: (i, 0)),
            pl.BlockSpec((group, 4, stencil.shape[1]), lambda i: (i, 0, 0)),
        ],
        out_specs=pl.BlockSpec((2 * var_count * lat_count, row_count), lambda i: (0, 0)),
        out_shape=jax.ShapeDtypeStruct((2 * var_count * lat_count, row_count), jnp.float32),
        cost_estimate=pl.CostEstimate(flops=flops, transcendentals=0, bytes_accessed=4 * 1024 * 1024),
    )(values, stencil, bilinear)
    total = total.reshape(2, var_count, lat_count, row_count)
    far = jnp.concatenate([jnp.zeros_like(total[1, :, :, :1]), total[1, :, :, :-1]], axis=2)
    total = jnp.transpose(total[0] + far, (0, 2, 1))
    return total.reshape(field_shape)


def allreduce_kernel(lat_devices, lon_devices, part_ref, out_ref, lon_buf, lat_buf, lon_send, lon_recv, lat_send, lat_recv):
    mesh_id = pl.DeviceIdType.MESH
    lat_me = lax.axis_index("lat")
    lon_me = lax.axis_index("lon")
    barrier = pltpu.get_barrier_semaphore()
    for peer in range(1, lon_devices):
        pl.semaphore_signal(barrier, inc=1, device_id=(lat_me, (lon_me + peer) % lon_devices), device_id_type=mesh_id)
    for peer in range(1, lat_devices):
        pl.semaphore_signal(barrier, inc=1, device_id=((lat_me + peer) % lat_devices, lon_me), device_id_type=mesh_id)
    pl.semaphore_wait(barrier, lon_devices + lat_devices - 2)

    def gather(buf, send, recv, count, me, target_of, source):
        copies = []
        for peer in range(1, count):
            target = (me + peer) % count
            copy = pltpu.make_async_remote_copy(
                src_ref=source,
                dst_ref=buf.at[me],
                send_sem=send.at[target],
                recv_sem=recv.at[me],
                device_id=target_of(target),
                device_id_type=mesh_id,
            )
            copy.start()
            copies.append((peer, copy))
        for peer, copy in copies:
            copy.wait_send()
        for peer in range(1, count):
            source_index = (me + count - peer) % count
            pltpu.make_async_remote_copy(
                src_ref=source,
                dst_ref=buf.at[source_index],
                send_sem=send.at[source_index],
                recv_sem=recv.at[source_index],
                device_id=target_of(source_index),
                device_id_type=mesh_id,
            ).wait_recv()

    gather(lon_buf, lon_send, lon_recv, lon_devices, lon_me, lambda t: (lat_me, t), part_ref)
    lon_buf[lon_me] = part_ref[...]
    total = lon_buf[0]
    for i in range(1, lon_devices):
        total = total + lon_buf[i]
    out_ref[...] = total
    gather(lat_buf, lat_send, lat_recv, lat_devices, lat_me, lambda t: (t, lon_me), out_ref)
    lat_buf[lat_me] = out_ref[...]
    total = lat_buf[0]
    for i in range(1, lat_devices):
        total = total + lat_buf[i]
    out_ref[...] = total


def allreduce_pallas(part):
    lat_devices = lax.axis_size("lat")
    lon_devices = lax.axis_size("lon")
    kernel = functools.partial(allreduce_kernel, lat_devices, lon_devices)
    return pl.pallas_call(
        kernel,
        in_specs=[pl.BlockSpec(memory_space=pltpu.VMEM)],
        out_specs=pl.BlockSpec(memory_space=pltpu.VMEM),
        out_shape=jax.ShapeDtypeStruct(part.shape, jnp.float32),
        scratch_shapes=[
            pltpu.VMEM((lon_devices,) + part.shape, jnp.float32),
            pltpu.VMEM((lat_devices,) + part.shape, jnp.float32),
            pltpu.SemaphoreType.DMA((lon_devices,)),
            pltpu.SemaphoreType.DMA((lon_devices,)),
            pltpu.SemaphoreType.DMA((lat_devices,)),
            pltpu.SemaphoreType.DMA((lat_devices,)),
        ],
        compiler_params=pltpu.CompilerParams(collective_id=0, has_side_effects=True),
    )(part)


def slots_of(block_owner, tile_count):
    targets = block_owner[:, 0]
    block_count = targets.shape[0]
    same_owner = (targets[:, None] == jnp.arange(tile_count, dtype=jnp.int32)[None, :]).astype(
        jnp.int32
    )
    order = jnp.arange(block_count, dtype=jnp.int32)
    lower = (order[:, None] > order[None, :]).astype(jnp.int32)
    earlier = jnp.dot(lower, same_owner)
    rank_within = jnp.sum(earlier * same_owner, axis=1)
    return targets * CAP + rank_within


def mix_blocks(values, correlation):
    return jnp.einsum("vsk,ik->vsi", values, correlation, precision=precise)


def shards(
    increment,
    residual,
    direction,
    diffusivity,
    deviation,
    stencil,
    bilinear,
    obs_weight,
    block_owner,
    correlation,
):
    lat_devices = lax.axis_size("lat")
    lon_devices = lax.axis_size("lon")
    tile_count = lat_devices * lon_devices
    both = widen_halo(jnp.stack([direction, diffusivity]), STEPS + 1)
    coeffs = face_coeffs(both[1], STEPS)

    def apply_diffusion(field):
        return diffuse(widen_halo(field, STEPS), coeffs)

    slots = slots_of(block_owner, tile_count)
    slot_table = (slots[:, None] == jnp.arange(tile_count * CAP, dtype=jnp.int32)[None, :]).astype(
        jnp.float32
    )
    field_shape = direction.shape
    state_field = deviation * diffuse(both[0][:, :, 1:-1, 1:-1], coeffs)
    observed = observe_pallas(state_field, stencil, bilinear, obs_weight)
    buffer = jnp.einsum("vbk,bs->vsk", observed, slot_table, precision=precise)
    returned = lax.all_to_all(
        mix_blocks(
            lax.all_to_all(buffer, ("lat", "lon"), split_axis=1, concat_axis=1, tiled=True),
            correlation,
        ),
        ("lat", "lon"),
        split_axis=1,
        concat_axis=1,
        tiled=True,
    )
    weighted = obs_weight * jnp.einsum("vsk,bs->vbk", returned, slot_table, precision=precise)
    spread_field = deviation * spread_pallas(weighted, stencil, bilinear, field_shape)
    image_field = direction + apply_diffusion(spread_field)
    local_sums = jnp.stack(
        [
            jnp.sum(residual * residual),
            jnp.sum(direction * image_field),
            jnp.sum(residual * image_field),
            jnp.sum(image_field * image_field),
        ]
    )
    sums = allreduce_pallas(jnp.zeros((8, 128), jnp.float32).at[0, :4].set(local_sums))[0]
    norm_now, curvature, cross, image_norm = sums[0], sums[1], sums[2], sums[3]
    step_size = norm_now / curvature
    increment = increment + step_size * direction
    residual = residual - step_size * image_field
    norm_next = norm_now - 2.0 * step_size * cross + step_size * step_size * image_norm
    direction = residual + norm_next / norm_now * direction
    return (increment, residual, direction)


def solution(mesh):
    in_specs = (
        P(None, None, "lon", "lat"),
        P(None, None, "lon", "lat"),
        P(None, None, "lon", "lat"),
        P(None, None, "lon", "lat"),
        P(None, None, "lon", "lat"),
        P(("lat", "lon"), None),
        P(("lat", "lon"), None, None),
        P(None, ("lat", "lon"), None),
        P(("lat", "lon"), None),
        P(("lat", "lon"), None),
    )
    out_specs = (
        P(None, None, "lon", "lat"),
        P(None, None, "lon", "lat"),
        P(None, None, "lon", "lat"),
    )
    return jax.shard_map(shards, mesh=mesh, in_specs=in_specs, out_specs=out_specs, check_vma=False)
```

```python
import functools
import math

import jax
import jax.numpy as jnp
from jax import lax
from jax.experimental import pallas as pl
from jax.experimental.pallas import tpu as pltpu
from jax.sharding import PartitionSpec as P

STEPS = 4
CAP = 2


precise = lax.Precision.HIGHEST


def widen_halo(value, width):
    lat_dim, lon_dim = value.ndim - 1, value.ndim - 2
    for axis, dim, wrap in (("lat", lat_dim, False), ("lon", lon_dim, True)):
        size, length = lax.axis_size(axis), value.shape[dim]
        up = [(i, (i + 1) % size) for i in range(size if wrap else size - 1)]
        down = [(j, i) for i, j in up]
        before = lax.ppermute(lax.slice_in_dim(value, length - width, length, axis=dim), axis, up)
        after = lax.ppermute(lax.slice_in_dim(value, 0, width, axis=dim), axis, down)
        value = jnp.concatenate([before, value, after], axis=dim)
    return value


def face_coeffs(wide, width):
    lat_count = wide.shape[3] - 2 * (width + 1)
    lat_devices = lax.axis_size("lat")
    first = lax.axis_index("lat") * lat_count - width
    cells = first + jnp.arange(lat_count + 2 * width, dtype=jnp.int32)
    inside = ((cells >= 0) & (cells < lat_devices * lat_count)).astype(jnp.float32)
    centre = wide[:, :, 1:-1, 1:-1]
    return (
        inside * (0.5 * (centre + wide[:, :, 1:-1, 2:])),
        inside * (0.5 * (centre + wide[:, :, 1:-1, :-2])),
        inside * (0.5 * (centre + wide[:, :, 2:, 1:-1])),
        inside * (0.5 * (centre + wide[:, :, :-2, 1:-1])),
    )


def diffuse(field, coeffs):
    for sweep in range(STEPS):
        lon_end = field.shape[2] - 1
        lat_end = field.shape[3] - 1
        here = field[:, :, 1:lon_end, 1:lat_end]
        edge = sweep + 1
        north_face, south_face, east_face, west_face = (
            c[:, :, edge : c.shape[2] - edge, edge : c.shape[3] - edge] for c in coeffs
        )
        field = (
            here
            + north_face * (field[:, :, 1:lon_end, 2:] - here)
            + south_face * (field[:, :, 1:lon_end, : lat_end - 1] - here)
            + east_face * (field[:, :, 2:, 1:lat_end] - here)
            + west_face * (field[:, :, : lon_end - 1, 1:lat_end] - here)
        )
    return field


PARTS = 2


def split_parts(value):
    parts = []
    rest = value
    for part in range(PARTS):
        piece = rest.astype(jnp.bfloat16)
        parts.append(piece)
        rest = rest - piece.astype(jnp.float32)
    return parts


def obs_lines(cell_ref, weight_ref, group, lat_count):
    cells = cell_ref[...]
    rows = cells // lat_count
    lats = cells - rows * lat_count
    row_line = jnp.concatenate([rows[g : g + 1, :] for g in range(group)], axis=1)
    lat_line = jnp.concatenate([lats[g : g + 1, :] for g in range(group)], axis=1)
    weights = [
        jnp.concatenate([weight_ref[g, c : c + 1, :] for g in range(group)], axis=1) for c in range(4)
    ]
    return row_line, lat_line, weights


def select_maps(row_line, lat_line, weights, row_count, lat_count):
    width = row_line.shape[1]
    row_ids = lax.broadcasted_iota(jnp.int32, (row_count, width), 0)
    near_rows = (row_ids == row_line).astype(jnp.bfloat16)
    lat_ids = lax.broadcasted_iota(jnp.int32, (lat_count, width), 0)
    at_first = lat_ids == lat_line
    at_second = lat_ids == lat_line + 1
    near_lat = jnp.where(at_first, weights[0], 0.0) + jnp.where(at_second, weights[1], 0.0)
    far_lat = jnp.where(at_first, weights[2], 0.0) + jnp.where(at_second, weights[3], 0.0)
    return near_rows, near_lat, far_lat


def observe_kernel(group, var_count, row_count, lat_count, table_ref, cell_ref, weight_ref, scale_ref, out_ref):
    row_line, lat_line, weights = obs_lines(cell_ref, weight_ref, group, lat_count)
    near_rows, near_lat, far_lat = select_maps(row_line, lat_line, weights, row_count, lat_count)
    table = jnp.concatenate(split_parts(table_ref[...]), axis=1)
    picked = jnp.dot(table, jnp.concatenate([near_rows] * PARTS, axis=0), preferred_element_type=jnp.float32)
    half = var_count * lat_count
    for v in range(var_count):
        near_span = slice(v * lat_count, (v + 1) * lat_count)
        far_span = slice(half + v * lat_count, half + (v + 1) * lat_count)
        line = jnp.sum(picked[near_span] * near_lat + picked[far_span] * far_lat, axis=0, keepdims=True)
        for g in range(group):
            out_ref[v, g : g + 1, :] = scale_ref[v, g : g + 1, :] * line[:, g * 128 : (g + 1) * 128]


def spread_kernel(group, var_count, row_count, lat_count, value_ref, cell_ref, weight_ref, out_ref, total_ref):
    step = pl.program_id(0)

    @pl.when(step == 0)
    def _():
        total_ref[...] = jnp.zeros_like(total_ref)

    row_line, lat_line, weights = obs_lines(cell_ref, weight_ref, group, lat_count)
    near_rows, near_lat, far_lat = select_maps(row_line, lat_line, weights, row_count, lat_count)
    near_parts, far_parts = [], []
    for v in range(var_count):
        line = jnp.concatenate([value_ref[v, g : g + 1, :] for g in range(group)], axis=1)
        near_parts.append(near_lat * line)
        far_parts.append(far_lat * line)
    rhs = jnp.concatenate(split_parts(jnp.concatenate(near_parts + far_parts, axis=0)), axis=1)
    lhs = jnp.concatenate([near_rows] * PARTS, axis=1)
    total_ref[...] += lax.dot_general(
        lhs, rhs, (((1,), (1,)), ((), ())), preferred_element_type=jnp.float32
    )

    @pl.when(step == pl.num_programs(0) - 1)
    def _():
        total = total_ref[...]
        half = var_count * lat_count
        summed = total[:, :half] + pltpu.roll(total[:, half:], 1, 0)
        for v in range(var_count):
            out_ref[v] = summed[:, v * lat_count : (v + 1) * lat_count]


def observe_pallas(field, stencil, bilinear, obs_weight, group=16):
    var_count, level_count, lon_count, lat_count = field.shape
    row_count = level_count * lon_count
    block_count = stencil.shape[0]
    rows_t = jnp.transpose(field.reshape(var_count, row_count, lat_count), (0, 2, 1))
    shifted = jnp.concatenate([rows_t[:, :, 1:], jnp.zeros_like(rows_t[:, :, :1])], axis=2)
    table = jnp.concatenate([rows_t, shifted], axis=0).reshape(2 * var_count * lat_count, row_count)
    kernel = functools.partial(observe_kernel, group, var_count, row_count, lat_count)
    width = group * stencil.shape[1]
    flops = 2 * 2 * var_count * lat_count * PARTS * row_count * width * (block_count // group)
    return pl.pallas_call(
        kernel,
        grid=(block_count // group,),
        in_specs=[
            pl.BlockSpec(table.shape, lambda i: (0, 0)),
            pl.BlockSpec((group, stencil.shape[1]), lambda i: (i, 0)),
            pl.BlockSpec((group, 4, stencil.shape[1]), lambda i: (i, 0, 0)),
            pl.BlockSpec((var_count, group, stencil.shape[1]), lambda i: (0, i, 0)),
        ],
        out_specs=pl.BlockSpec((var_count, group, stencil.shape[1]), lambda i: (0, i, 0)),
        out_shape=jax.ShapeDtypeStruct(obs_weight.shape, jnp.float32),
        cost_estimate=pl.CostEstimate(flops=flops, transcendentals=0, bytes_accessed=4 * 1024 * 1024),
    )(table, stencil, bilinear, obs_weight)


def spread_pallas(values, stencil, bilinear, field_shape, group=16):
    var_count, level_count, lon_count, lat_count = field_shape
    row_count = level_count * lon_count
    block_count = stencil.shape[0]
    kernel = functools.partial(spread_kernel, group, var_count, row_count, lat_count)
    width = group * stencil.shape[1]
    flops = 2 * 2 * var_count * lat_count * PARTS * row_count * width * (block_count // group)
    total = pl.pallas_call(
        kernel,
        grid=(block_count // group,),
        in_specs=[
            pl.BlockSpec((var_count, group, stencil.shape[1]), lambda i: (0, i, 0)),
            pl.BlockSpec((group, stencil.shape[1]), lambda i: (i, 0)),
            pl.BlockSpec((group, 4, stencil.shape[1]), lambda i: (i, 0, 0)),
        ],
        out_specs=pl.BlockSpec((var_count, row_count, lat_count), lambda i: (0, 0, 0)),
        out_shape=jax.ShapeDtypeStruct((var_count, row_count, lat_count), jnp.float32),
        scratch_shapes=[pltpu.VMEM((row_count, 2 * var_count * lat_count), jnp.float32)],
        cost_estimate=pl.CostEstimate(flops=flops, transcendentals=0, bytes_accessed=4 * 1024 * 1024),
    )(values, stencil, bilinear)
    return total.reshape(field_shape)


def allreduce_kernel(lat_devices, lon_devices, part_ref, out_ref, lon_buf, lat_buf, lon_send, lon_recv, lat_send, lat_recv):
    mesh_id = pl.DeviceIdType.MESH
    lat_me = lax.axis_index("lat")
    lon_me = lax.axis_index("lon")
    barrier = pltpu.get_barrier_semaphore()
    for peer in range(1, lon_devices):
        pl.semaphore_signal(barrier, inc=1, device_id=(lat_me, (lon_me + peer) % lon_devices), device_id_type=mesh_id)
    for peer in range(1, lat_devices):
        pl.semaphore_signal(barrier, inc=1, device_id=((lat_me + peer) % lat_devices, lon_me), device_id_type=mesh_id)
    pl.semaphore_wait(barrier, lon_devices + lat_devices - 2)

    def gather(buf, send, recv, count, me, target_of, source):
        copies = []
        for peer in range(1, count):
            target = (me + peer) % count
            copy = pltpu.make_async_remote_copy(
                src_ref=source,
                dst_ref=buf.at[me],
                send_sem=send.at[target],
                recv_sem=recv.at[me],
                device_id=target_of(target),
                device_id_type=mesh_id,
            )
            copy.start()
            copies.append((peer, copy))
        for peer, copy in copies:
            copy.wait_send()
        for peer in range(1, count):
            source_index = (me + count - peer) % count
            pltpu.make_async_remote_copy(
                src_ref=source,
                dst_ref=buf.at[source_index],
                send_sem=send.at[source_index],
                recv_sem=recv.at[source_index],
                device_id=target_of(source_index),
                device_id_type=mesh_id,
            ).wait_recv()

    gather(lon_buf, lon_send, lon_recv, lon_devices, lon_me, lambda t: (lat_me, t), part_ref)
    lon_buf[lon_me] = part_ref[...]
    total = lon_buf[0]
    for i in range(1, lon_devices):
        total = total + lon_buf[i]
    out_ref[...] = total
    gather(lat_buf, lat_send, lat_recv, lat_devices, lat_me, lambda t: (t, lon_me), out_ref)
    lat_buf[lat_me] = out_ref[...]
    total = lat_buf[0]
    for i in range(1, lat_devices):
        total = total + lat_buf[i]
    out_ref[...] = total


def allreduce_pallas(part):
    lat_devices = lax.axis_size("lat")
    lon_devices = lax.axis_size("lon")
    kernel = functools.partial(allreduce_kernel, lat_devices, lon_devices)
    return pl.pallas_call(
        kernel,
        in_specs=[pl.BlockSpec(memory_space=pltpu.VMEM)],
        out_specs=pl.BlockSpec(memory_space=pltpu.VMEM),
        out_shape=jax.ShapeDtypeStruct(part.shape, jnp.float32),
        scratch_shapes=[
            pltpu.VMEM((lon_devices,) + part.shape, jnp.float32),
            pltpu.VMEM((lat_devices,) + part.shape, jnp.float32),
            pltpu.SemaphoreType.DMA((lon_devices,)),
            pltpu.SemaphoreType.DMA((lon_devices,)),
            pltpu.SemaphoreType.DMA((lat_devices,)),
            pltpu.SemaphoreType.DMA((lat_devices,)),
        ],
        compiler_params=pltpu.CompilerParams(collective_id=0, has_side_effects=True),
    )(part)


def slots_of(block_owner, tile_count):
    targets = block_owner[:, 0]
    block_count = targets.shape[0]
    same_owner = (targets[:, None] == jnp.arange(tile_count, dtype=jnp.int32)[None, :]).astype(
        jnp.int32
    )
    order = jnp.arange(block_count, dtype=jnp.int32)
    lower = (order[:, None] > order[None, :]).astype(jnp.int32)
    earlier = jnp.dot(lower, same_owner)
    rank_within = jnp.sum(earlier * same_owner, axis=1)
    return targets * CAP + rank_within


def mix_blocks(values, correlation):
    return jnp.einsum("vsk,ik->vsi", values, correlation, precision=precise)


def shards(
    increment,
    residual,
    direction,
    diffusivity,
    deviation,
    stencil,
    bilinear,
    obs_weight,
    block_owner,
    correlation,
):
    lat_devices = lax.axis_size("lat")
    lon_devices = lax.axis_size("lon")
    tile_count = lat_devices * lon_devices
    both = widen_halo(jnp.stack([direction, diffusivity]), STEPS + 1)
    coeffs = face_coeffs(both[1], STEPS)

    def apply_diffusion(field):
        return diffuse(widen_halo(field, STEPS), coeffs)

    slots = slots_of(block_owner, tile_count)
    slot_table = (slots[:, None] == jnp.arange(tile_count * CAP, dtype=jnp.int32)[None, :]).astype(
        jnp.float32
    )
    field_shape = direction.shape
    state_field = deviation * diffuse(both[0][:, :, 1:-1, 1:-1], coeffs)
    observed = observe_pallas(state_field, stencil, bilinear, obs_weight)
    buffer = jnp.einsum("vbk,bs->vsk", observed, slot_table, precision=precise)
    returned = lax.all_to_all(
        mix_blocks(
            lax.all_to_all(buffer, ("lat", "lon"), split_axis=1, concat_axis=1, tiled=True),
            correlation,
        ),
        ("lat", "lon"),
        split_axis=1,
        concat_axis=1,
        tiled=True,
    )
    weighted = obs_weight * jnp.einsum("vsk,bs->vbk", returned, slot_table, precision=precise)
    spread_field = deviation * spread_pallas(weighted, stencil, bilinear, field_shape)
    image_field = direction + apply_diffusion(spread_field)
    local_sums = jnp.stack(
        [
            jnp.sum(residual * residual),
            jnp.sum(direction * image_field),
            jnp.sum(residual * image_field),
            jnp.sum(image_field * image_field),
        ]
    )
    sums = allreduce_pallas(jnp.zeros((8, 128), jnp.float32).at[0, :4].set(local_sums))[0]
    norm_now, curvature, cross, image_norm = sums[0], sums[1], sums[2], sums[3]
    step_size = norm_now / curvature
    increment = increment + step_size * direction
    residual = residual - step_size * image_field
    norm_next = norm_now - 2.0 * step_size * cross + step_size * step_size * image_norm
    direction = residual + norm_next / norm_now * direction
    return (increment, residual, direction)


def solution(mesh):
    in_specs = (
        P(None, None, "lon", "lat"),
        P(None, None, "lon", "lat"),
        P(None, None, "lon", "lat"),
        P(None, None, "lon", "lat"),
        P(None, None, "lon", "lat"),
        P(("lat", "lon"), None),
        P(("lat", "lon"), None, None),
        P(None, ("lat", "lon"), None),
        P(("lat", "lon"), None),
        P(("lat", "lon"), None),
    )
    out_specs = (
        P(None, None, "lon", "lat"),
        P(None, None, "lon", "lat"),
        P(None, None, "lon", "lat"),
    )
    return jax.shard_map(shards, mesh=mesh, in_specs=in_specs, out_specs=out_specs, check_vma=False)
```

```python
import functools
import math

import jax
import jax.numpy as jnp
from jax import lax
from jax.experimental import pallas as pl
from jax.experimental.pallas import tpu as pltpu
from jax.sharding import PartitionSpec as P

STEPS = 4
CAP = 2


precise = lax.Precision.HIGHEST


def widen_halo(value, width):
    lat_dim, lon_dim = value.ndim - 1, value.ndim - 2
    for axis, dim, wrap in (("lat", lat_dim, False), ("lon", lon_dim, True)):
        size, length = lax.axis_size(axis), value.shape[dim]
        up = [(i, (i + 1) % size) for i in range(size if wrap else size - 1)]
        down = [(j, i) for i, j in up]
        before = lax.ppermute(lax.slice_in_dim(value, length - width, length, axis=dim), axis, up)
        after = lax.ppermute(lax.slice_in_dim(value, 0, width, axis=dim), axis, down)
        value = jnp.concatenate([before, value, after], axis=dim)
    return value


def face_coeffs(wide, width):
    lat_count = wide.shape[3] - 2 * (width + 1)
    lat_devices = lax.axis_size("lat")
    first = lax.axis_index("lat") * lat_count - width
    cells = first + jnp.arange(lat_count + 2 * width, dtype=jnp.int32)
    inside = ((cells >= 0) & (cells < lat_devices * lat_count)).astype(jnp.float32)
    centre = wide[:, :, 1:-1, 1:-1]
    return (
        inside * (0.5 * (centre + wide[:, :, 1:-1, 2:])),
        inside * (0.5 * (centre + wide[:, :, 1:-1, :-2])),
        inside * (0.5 * (centre + wide[:, :, 2:, 1:-1])),
        inside * (0.5 * (centre + wide[:, :, :-2, 1:-1])),
    )


def diffuse_kernel(steps, field_ref, north_ref, south_ref, east_ref, west_ref, out_ref):
    field = field_ref[...]
    rows, lanes = field.shape[1], field.shape[2]
    north, south, east, west = north_ref[...], south_ref[...], east_ref[...], west_ref[...]
    for sweep in range(steps):
        field = (
            field
            + north * (pltpu.roll(field, lanes - 1, 2) - field)
            + south * (pltpu.roll(field, 1, 2) - field)
            + east * (pltpu.roll(field, rows - 1, 1) - field)
            + west * (pltpu.roll(field, 1, 1) - field)
        )
    field = pltpu.roll(pltpu.roll(field, lanes - steps, 2), rows - steps, 1)
    out_ref[...] = field[:, : out_ref.shape[1], : out_ref.shape[2]]


def pad_lanes(value):
    planes, rows, lanes = value.shape
    return jnp.pad(value, ((0, 0), (0, 0), (0, -lanes % 128)))


def padded_coeffs(coeffs):
    return tuple(pad_lanes(c.reshape((-1,) + c.shape[-2:])) for c in coeffs)


def diffuse(field, coeffs, planes_per_step=50):
    lead = field.shape[:-2]
    flat = pad_lanes(field.reshape((-1,) + field.shape[-2:]))
    planes, rows, lanes = flat.shape
    lon_count, lat_count = rows - 2 * STEPS, field.shape[-1] - 2 * STEPS
    spec = pl.BlockSpec((planes_per_step, rows, lanes), lambda i: (i, 0, 0))
    out = pl.pallas_call(
        functools.partial(diffuse_kernel, STEPS),
        grid=(planes // planes_per_step,),
        in_specs=[spec] * 5,
        out_specs=pl.BlockSpec((planes_per_step, lon_count, lat_count), lambda i: (i, 0, 0)),
        out_shape=jax.ShapeDtypeStruct((planes, lon_count, lat_count), field.dtype),
        cost_estimate=pl.CostEstimate(
            flops=14 * STEPS * planes * rows * lanes, transcendentals=0, bytes_accessed=24 * planes * rows * lanes
        ),
    )(flat, *coeffs)
    return out.reshape(lead + (lon_count, lat_count))


PARTS = 2


def split_parts(value):
    parts = []
    rest = value
    for part in range(PARTS):
        piece = rest.astype(jnp.bfloat16)
        parts.append(piece)
        rest = rest - piece.astype(jnp.float32)
    return parts


def obs_lines(cell_ref, weight_ref, group, lat_count):
    cells = cell_ref[...]
    rows = cells // lat_count
    lats = cells - rows * lat_count
    row_line = jnp.concatenate([rows[g : g + 1, :] for g in range(group)], axis=1)
    lat_line = jnp.concatenate([lats[g : g + 1, :] for g in range(group)], axis=1)
    weights = [
        jnp.concatenate([weight_ref[g, c : c + 1, :] for g in range(group)], axis=1) for c in range(4)
    ]
    return row_line, lat_line, weights


def select_maps(row_line, lat_line, weights, row_count, lat_count):
    width = row_line.shape[1]
    row_ids = lax.broadcasted_iota(jnp.int32, (row_count, width), 0)
    near_rows = (row_ids == row_line).astype(jnp.bfloat16)
    lat_ids = lax.broadcasted_iota(jnp.int32, (lat_count, width), 0)
    at_first = lat_ids == lat_line
    at_second = lat_ids == lat_line + 1
    near_lat = jnp.where(at_first, weights[0], 0.0) + jnp.where(at_second, weights[1], 0.0)
    far_lat = jnp.where(at_first, weights[2], 0.0) + jnp.where(at_second, weights[3], 0.0)
    return near_rows, near_lat, far_lat


def observe_kernel(group, var_count, row_count, lat_count, table_ref, cell_ref, weight_ref, scale_ref, out_ref):
    row_line, lat_line, weights = obs_lines(cell_ref, weight_ref, group, lat_count)
    near_rows, near_lat, far_lat = select_maps(row_line, lat_line, weights, row_count, lat_count)
    table = jnp.concatenate(split_parts(table_ref[...]), axis=1)
    picked = jnp.dot(table, jnp.concatenate([near_rows] * PARTS, axis=0), preferred_element_type=jnp.float32)
    half = var_count * lat_count
    for v in range(var_count):
        near_span = slice(v * lat_count, (v + 1) * lat_count)
        far_span = slice(half + v * lat_count, half + (v + 1) * lat_count)
        line = jnp.sum(picked[near_span] * near_lat + picked[far_span] * far_lat, axis=0, keepdims=True)
        for g in range(group):
            out_ref[v, g : g + 1, :] = scale_ref[v, g : g + 1, :] * line[:, g * 128 : (g + 1) * 128]


def spread_kernel(group, var_count, row_count, lat_count, value_ref, cell_ref, weight_ref, out_ref, total_ref):
    step = pl.program_id(0)

    @pl.when(step == 0)
    def _():
        total_ref[...] = jnp.zeros_like(total_ref)

    row_line, lat_line, weights = obs_lines(cell_ref, weight_ref, group, lat_count)
    near_rows, near_lat, far_lat = select_maps(row_line, lat_line, weights, row_count, lat_count)
    near_parts, far_parts = [], []
    for v in range(var_count):
        line = jnp.concatenate([value_ref[v, g : g + 1, :] for g in range(group)], axis=1)
        near_parts.append(near_lat * line)
        far_parts.append(far_lat * line)
    rhs = jnp.concatenate(split_parts(jnp.concatenate(near_parts + far_parts, axis=0)), axis=1)
    lhs = jnp.concatenate([near_rows] * PARTS, axis=1)
    total_ref[...] += lax.dot_general(
        lhs, rhs, (((1,), (1,)), ((), ())), preferred_element_type=jnp.float32
    )

    @pl.when(step == pl.num_programs(0) - 1)
    def _():
        total = total_ref[...]
        half = var_count * lat_count
        summed = total[:, :half] + pltpu.roll(total[:, half:], 1, 0)
        for v in range(var_count):
            out_ref[v] = summed[:, v * lat_count : (v + 1) * lat_count]


def observe_pallas(field, stencil, bilinear, obs_weight, group=16):
    var_count, level_count, lon_count, lat_count = field.shape
    row_count = level_count * lon_count
    block_count = stencil.shape[0]
    rows_t = jnp.transpose(field.reshape(var_count, row_count, lat_count), (0, 2, 1))
    shifted = jnp.concatenate([rows_t[:, :, 1:], jnp.zeros_like(rows_t[:, :, :1])], axis=2)
    table = jnp.concatenate([rows_t, shifted], axis=0).reshape(2 * var_count * lat_count, row_count)
    kernel = functools.partial(observe_kernel, group, var_count, row_count, lat_count)
    width = group * stencil.shape[1]
    flops = 2 * 2 * var_count * lat_count * PARTS * row_count * width * (block_count // group)
    return pl.pallas_call(
        kernel,
        grid=(block_count // group,),
        in_specs=[
            pl.BlockSpec(table.shape, lambda i: (0, 0)),
            pl.BlockSpec((group, stencil.shape[1]), lambda i: (i, 0)),
            pl.BlockSpec((group, 4, stencil.shape[1]), lambda i: (i, 0, 0)),
            pl.BlockSpec((var_count, group, stencil.shape[1]), lambda i: (0, i, 0)),
        ],
        out_specs=pl.BlockSpec((var_count, group, stencil.shape[1]), lambda i: (0, i, 0)),
        out_shape=jax.ShapeDtypeStruct(obs_weight.shape, jnp.float32),
        cost_estimate=pl.CostEstimate(flops=flops, transcendentals=0, bytes_accessed=4 * 1024 * 1024),
    )(table, stencil, bilinear, obs_weight)


def spread_pallas(values, stencil, bilinear, field_shape, group=16):
    var_count, level_count, lon_count, lat_count = field_shape
    row_count = level_count * lon_count
    block_count = stencil.shape[0]
    kernel = functools.partial(spread_kernel, group, var_count, row_count, lat_count)
    width = group * stencil.shape[1]
    flops = 2 * 2 * var_count * lat_count * PARTS * row_count * width * (block_count // group)
    total = pl.pallas_call(
        kernel,
        grid=(block_count // group,),
        in_specs=[
            pl.BlockSpec((var_count, group, stencil.shape[1]), lambda i: (0, i, 0)),
            pl.BlockSpec((group, stencil.shape[1]), lambda i: (i, 0)),
            pl.BlockSpec((group, 4, stencil.shape[1]), lambda i: (i, 0, 0)),
        ],
        out_specs=pl.BlockSpec((var_count, row_count, lat_count), lambda i: (0, 0, 0)),
        out_shape=jax.ShapeDtypeStruct((var_count, row_count, lat_count), jnp.float32),
        scratch_shapes=[pltpu.VMEM((row_count, 2 * var_count * lat_count), jnp.float32)],
        cost_estimate=pl.CostEstimate(flops=flops, transcendentals=0, bytes_accessed=4 * 1024 * 1024),
    )(values, stencil, bilinear)
    return total.reshape(field_shape)


def allreduce_kernel(lat_devices, lon_devices, part_ref, out_ref, lon_buf, lat_buf, lon_send, lon_recv, lat_send, lat_recv):
    mesh_id = pl.DeviceIdType.MESH
    lat_me = lax.axis_index("lat")
    lon_me = lax.axis_index("lon")
    barrier = pltpu.get_barrier_semaphore()
    for peer in range(1, lon_devices):
        pl.semaphore_signal(barrier, inc=1, device_id=(lat_me, (lon_me + peer) % lon_devices), device_id_type=mesh_id)
    for peer in range(1, lat_devices):
        pl.semaphore_signal(barrier, inc=1, device_id=((lat_me + peer) % lat_devices, lon_me), device_id_type=mesh_id)
    pl.semaphore_wait(barrier, lon_devices + lat_devices - 2)

    def gather(buf, send, recv, count, me, target_of, source):
        copies = []
        for peer in range(1, count):
            target = (me + peer) % count
            copy = pltpu.make_async_remote_copy(
                src_ref=source,
                dst_ref=buf.at[me],
                send_sem=send.at[target],
                recv_sem=recv.at[me],
                device_id=target_of(target),
                device_id_type=mesh_id,
            )
            copy.start()
            copies.append((peer, copy))
        for peer, copy in copies:
            copy.wait_send()
        for peer in range(1, count):
            source_index = (me + count - peer) % count
            pltpu.make_async_remote_copy(
                src_ref=source,
                dst_ref=buf.at[source_index],
                send_sem=send.at[source_index],
                recv_sem=recv.at[source_index],
                device_id=target_of(source_index),
                device_id_type=mesh_id,
            ).wait_recv()

    gather(lon_buf, lon_send, lon_recv, lon_devices, lon_me, lambda t: (lat_me, t), part_ref)
    lon_buf[lon_me] = part_ref[...]
    total = lon_buf[0]
    for i in range(1, lon_devices):
        total = total + lon_buf[i]
    out_ref[...] = total
    gather(lat_buf, lat_send, lat_recv, lat_devices, lat_me, lambda t: (t, lon_me), out_ref)
    lat_buf[lat_me] = out_ref[...]
    total = lat_buf[0]
    for i in range(1, lat_devices):
        total = total + lat_buf[i]
    out_ref[...] = total


def allreduce_pallas(part):
    lat_devices = lax.axis_size("lat")
    lon_devices = lax.axis_size("lon")
    kernel = functools.partial(allreduce_kernel, lat_devices, lon_devices)
    return pl.pallas_call(
        kernel,
        in_specs=[pl.BlockSpec(memory_space=pltpu.VMEM)],
        out_specs=pl.BlockSpec(memory_space=pltpu.VMEM),
        out_shape=jax.ShapeDtypeStruct(part.shape, jnp.float32),
        scratch_shapes=[
            pltpu.VMEM((lon_devices,) + part.shape, jnp.float32),
            pltpu.VMEM((lat_devices,) + part.shape, jnp.float32),
            pltpu.SemaphoreType.DMA((lon_devices,)),
            pltpu.SemaphoreType.DMA((lon_devices,)),
            pltpu.SemaphoreType.DMA((lat_devices,)),
            pltpu.SemaphoreType.DMA((lat_devices,)),
        ],
        compiler_params=pltpu.CompilerParams(collective_id=0, has_side_effects=True),
    )(part)


def slots_of(block_owner, tile_count):
    targets = block_owner[:, 0]
    block_count = targets.shape[0]
    same_owner = (targets[:, None] == jnp.arange(tile_count, dtype=jnp.int32)[None, :]).astype(
        jnp.int32
    )
    order = jnp.arange(block_count, dtype=jnp.int32)
    lower = (order[:, None] > order[None, :]).astype(jnp.int32)
    earlier = jnp.dot(lower, same_owner)
    rank_within = jnp.sum(earlier * same_owner, axis=1)
    return targets * CAP + rank_within


def mix_blocks(values, correlation):
    return jnp.einsum("vsk,ik->vsi", values, correlation, precision=precise)


def shards(
    increment,
    residual,
    direction,
    diffusivity,
    deviation,
    stencil,
    bilinear,
    obs_weight,
    block_owner,
    correlation,
):
    lat_devices = lax.axis_size("lat")
    lon_devices = lax.axis_size("lon")
    tile_count = lat_devices * lon_devices
    both = widen_halo(jnp.stack([direction, diffusivity]), STEPS + 1)
    coeffs = padded_coeffs(face_coeffs(both[1], STEPS))

    def apply_diffusion(field):
        return diffuse(widen_halo(field, STEPS), coeffs)

    slots = slots_of(block_owner, tile_count)
    slot_table = (slots[:, None] == jnp.arange(tile_count * CAP, dtype=jnp.int32)[None, :]).astype(
        jnp.float32
    )
    field_shape = direction.shape
    state_field = deviation * diffuse(both[0][:, :, 1:-1, 1:-1], coeffs)
    observed = observe_pallas(state_field, stencil, bilinear, obs_weight)
    buffer = jnp.einsum("vbk,bs->vsk", observed, slot_table, precision=precise)
    returned = lax.all_to_all(
        mix_blocks(
            lax.all_to_all(buffer, ("lat", "lon"), split_axis=1, concat_axis=1, tiled=True),
            correlation,
        ),
        ("lat", "lon"),
        split_axis=1,
        concat_axis=1,
        tiled=True,
    )
    weighted = obs_weight * jnp.einsum("vsk,bs->vbk", returned, slot_table, precision=precise)
    spread_field = deviation * spread_pallas(weighted, stencil, bilinear, field_shape)
    image_field = direction + apply_diffusion(spread_field)
    local_sums = jnp.stack(
        [
            jnp.sum(residual * residual),
            jnp.sum(direction * image_field),
            jnp.sum(residual * image_field),
            jnp.sum(image_field * image_field),
        ]
    )
    sums = allreduce_pallas(jnp.zeros((8, 128), jnp.float32).at[0, :4].set(local_sums))[0]
    norm_now, curvature, cross, image_norm = sums[0], sums[1], sums[2], sums[3]
    step_size = norm_now / curvature
    increment = increment + step_size * direction
    residual = residual - step_size * image_field
    norm_next = norm_now - 2.0 * step_size * cross + step_size * step_size * image_norm
    direction = residual + norm_next / norm_now * direction
    return (increment, residual, direction)


def solution(mesh):
    in_specs = (
        P(None, None, "lon", "lat"),
        P(None, None, "lon", "lat"),
        P(None, None, "lon", "lat"),
        P(None, None, "lon", "lat"),
        P(None, None, "lon", "lat"),
        P(("lat", "lon"), None),
        P(("lat", "lon"), None, None),
        P(None, ("lat", "lon"), None),
        P(("lat", "lon"), None),
        P(("lat", "lon"), None),
    )
    out_specs = (
        P(None, None, "lon", "lat"),
        P(None, None, "lon", "lat"),
        P(None, None, "lon", "lat"),
    )
    return jax.shard_map(shards, mesh=mesh, in_specs=in_specs, out_specs=out_specs, check_vma=False)
```

```python
import functools
import math

import jax
import jax.numpy as jnp
from jax import lax
from jax.experimental import pallas as pl
from jax.experimental.pallas import tpu as pltpu
from jax.sharding import PartitionSpec as P

STEPS = 4
CAP = 2


precise = lax.Precision.HIGHEST


def widen_halo(value, width):
    lat_dim, lon_dim = value.ndim - 1, value.ndim - 2
    for axis, dim, wrap in (("lat", lat_dim, False), ("lon", lon_dim, True)):
        size, length = lax.axis_size(axis), value.shape[dim]
        up = [(i, (i + 1) % size) for i in range(size if wrap else size - 1)]
        down = [(j, i) for i, j in up]
        before = lax.ppermute(lax.slice_in_dim(value, length - width, length, axis=dim), axis, up)
        after = lax.ppermute(lax.slice_in_dim(value, 0, width, axis=dim), axis, down)
        value = jnp.concatenate([before, value, after], axis=dim)
    return value


def face_coeffs(wide, width):
    lat_count = wide.shape[3] - 2 * (width + 1)
    lat_devices = lax.axis_size("lat")
    first = lax.axis_index("lat") * lat_count - width
    cells = first + jnp.arange(lat_count + 2 * width, dtype=jnp.int32)
    inside = ((cells >= 0) & (cells < lat_devices * lat_count)).astype(jnp.float32)
    centre = wide[:, :, 1:-1, 1:-1]
    return (
        inside * (0.5 * (centre + wide[:, :, 1:-1, 2:])),
        inside * (0.5 * (centre + wide[:, :, 1:-1, :-2])),
        inside * (0.5 * (centre + wide[:, :, 2:, 1:-1])),
        inside * (0.5 * (centre + wide[:, :, :-2, 1:-1])),
    )


def diffuse_kernel(steps, field_ref, north_ref, south_ref, east_ref, west_ref, out_ref):
    field = field_ref[...]
    rows, lanes = field.shape[1], field.shape[2]
    north, south, east, west = north_ref[...], south_ref[...], east_ref[...], west_ref[...]
    keep = 1.0 - (north + south + east + west)
    for sweep in range(steps):
        field = (
            keep * field
            + north * pltpu.roll(field, lanes - 1, 2)
            + south * pltpu.roll(field, 1, 2)
            + east * pltpu.roll(field, rows - 1, 1)
            + west * pltpu.roll(field, 1, 1)
        )
    field = pltpu.roll(pltpu.roll(field, lanes - steps, 2), rows - steps, 1)
    out_ref[...] = field[:, : out_ref.shape[1], : out_ref.shape[2]]


def pad_lanes(value):
    planes, rows, lanes = value.shape
    return jnp.pad(value, ((0, 0), (0, 0), (0, -lanes % 128)))


def padded_coeffs(coeffs):
    return tuple(pad_lanes(c.reshape((-1,) + c.shape[-2:])) for c in coeffs)


def diffuse(field, coeffs, planes_per_step=50):
    lead = field.shape[:-2]
    flat = pad_lanes(field.reshape((-1,) + field.shape[-2:]))
    planes, rows, lanes = flat.shape
    lon_count, lat_count = rows - 2 * STEPS, field.shape[-1] - 2 * STEPS
    spec = pl.BlockSpec((planes_per_step, rows, lanes), lambda i: (i, 0, 0))
    out = pl.pallas_call(
        functools.partial(diffuse_kernel, STEPS),
        grid=(planes // planes_per_step,),
        in_specs=[spec] * 5,
        out_specs=pl.BlockSpec((planes_per_step, lon_count, lat_count), lambda i: (i, 0, 0)),
        out_shape=jax.ShapeDtypeStruct((planes, lon_count, lat_count), field.dtype),
        cost_estimate=pl.CostEstimate(
            flops=14 * STEPS * planes * rows * lanes, transcendentals=0, bytes_accessed=24 * planes * rows * lanes
        ),
    )(flat, *coeffs)
    return out.reshape(lead + (lon_count, lat_count))


PARTS = 2


def split_parts(value):
    parts = []
    rest = value
    for part in range(PARTS):
        piece = rest.astype(jnp.bfloat16)
        parts.append(piece)
        rest = rest - piece.astype(jnp.float32)
    return parts


def obs_lines(cell_ref, weight_ref, group, lat_count):
    cells = cell_ref[...]
    rows = cells // lat_count
    lats = cells - rows * lat_count
    row_line = jnp.concatenate([rows[g : g + 1, :] for g in range(group)], axis=1)
    lat_line = jnp.concatenate([lats[g : g + 1, :] for g in range(group)], axis=1)
    weights = [
        jnp.concatenate([weight_ref[g, c : c + 1, :] for g in range(group)], axis=1) for c in range(4)
    ]
    return row_line, lat_line, weights


def select_maps(row_line, lat_line, weights, row_count, lat_count):
    width = row_line.shape[1]
    row_ids = lax.broadcasted_iota(jnp.int32, (row_count, width), 0)
    near_rows = (row_ids == row_line).astype(jnp.bfloat16)
    lat_ids = lax.broadcasted_iota(jnp.int32, (lat_count, width), 0)
    at_first = lat_ids == lat_line
    at_second = lat_ids == lat_line + 1
    near_lat = jnp.where(at_first, weights[0], 0.0) + jnp.where(at_second, weights[1], 0.0)
    far_lat = jnp.where(at_first, weights[2], 0.0) + jnp.where(at_second, weights[3], 0.0)
    return near_rows, near_lat, far_lat


def observe_kernel(group, var_count, row_count, lat_count, table_ref, cell_ref, weight_ref, scale_ref, out_ref):
    row_line, lat_line, weights = obs_lines(cell_ref, weight_ref, group, lat_count)
    near_rows, near_lat, far_lat = select_maps(row_line, lat_line, weights, row_count, lat_count)
    table = jnp.concatenate(split_parts(table_ref[...]), axis=1)
    picked = jnp.dot(table, jnp.concatenate([near_rows] * PARTS, axis=0), preferred_element_type=jnp.float32)
    half = var_count * lat_count
    for v in range(var_count):
        near_span = slice(v * lat_count, (v + 1) * lat_count)
        far_span = slice(half + v * lat_count, half + (v + 1) * lat_count)
        line = jnp.sum(picked[near_span] * near_lat + picked[far_span] * far_lat, axis=0, keepdims=True)
        for g in range(group):
            out_ref[v, g : g + 1, :] = scale_ref[v, g : g + 1, :] * line[:, g * 128 : (g + 1) * 128]


def spread_kernel(group, var_count, row_count, lat_count, value_ref, cell_ref, weight_ref, out_ref, total_ref):
    step = pl.program_id(0)

    @pl.when(step == 0)
    def _():
        total_ref[...] = jnp.zeros_like(total_ref)

    row_line, lat_line, weights = obs_lines(cell_ref, weight_ref, group, lat_count)
    near_rows, near_lat, far_lat = select_maps(row_line, lat_line, weights, row_count, lat_count)
    near_parts, far_parts = [], []
    for v in range(var_count):
        line = jnp.concatenate([value_ref[v, g : g + 1, :] for g in range(group)], axis=1)
        near_parts.append(near_lat * line)
        far_parts.append(far_lat * line)
    rhs = jnp.concatenate(split_parts(jnp.concatenate(near_parts + far_parts, axis=0)), axis=1)
    lhs = jnp.concatenate([near_rows] * PARTS, axis=1)
    total_ref[...] += lax.dot_general(
        lhs, rhs, (((1,), (1,)), ((), ())), preferred_element_type=jnp.float32
    )

    @pl.when(step == pl.num_programs(0) - 1)
    def _():
        total = total_ref[...]
        half = var_count * lat_count
        summed = total[:, :half] + pltpu.roll(total[:, half:], 1, 0)
        for v in range(var_count):
            out_ref[v] = summed[:, v * lat_count : (v + 1) * lat_count]


def observe_pallas(field, stencil, bilinear, obs_weight, group=16):
    var_count, level_count, lon_count, lat_count = field.shape
    row_count = level_count * lon_count
    block_count = stencil.shape[0]
    rows_t = jnp.transpose(field.reshape(var_count, row_count, lat_count), (0, 2, 1))
    shifted = jnp.concatenate([rows_t[:, :, 1:], jnp.zeros_like(rows_t[:, :, :1])], axis=2)
    table = jnp.concatenate([rows_t, shifted], axis=0).reshape(2 * var_count * lat_count, row_count)
    kernel = functools.partial(observe_kernel, group, var_count, row_count, lat_count)
    width = group * stencil.shape[1]
    flops = 2 * 2 * var_count * lat_count * PARTS * row_count * width * (block_count // group)
    return pl.pallas_call(
        kernel,
        grid=(block_count // group,),
        in_specs=[
            pl.BlockSpec(table.shape, lambda i: (0, 0)),
            pl.BlockSpec((group, stencil.shape[1]), lambda i: (i, 0)),
            pl.BlockSpec((group, 4, stencil.shape[1]), lambda i: (i, 0, 0)),
            pl.BlockSpec((var_count, group, stencil.shape[1]), lambda i: (0, i, 0)),
        ],
        out_specs=pl.BlockSpec((var_count, group, stencil.shape[1]), lambda i: (0, i, 0)),
        out_shape=jax.ShapeDtypeStruct(obs_weight.shape, jnp.float32),
        cost_estimate=pl.CostEstimate(flops=flops, transcendentals=0, bytes_accessed=4 * 1024 * 1024),
    )(table, stencil, bilinear, obs_weight)


def spread_pallas(values, stencil, bilinear, field_shape, group=16):
    var_count, level_count, lon_count, lat_count = field_shape
    row_count = level_count * lon_count
    block_count = stencil.shape[0]
    kernel = functools.partial(spread_kernel, group, var_count, row_count, lat_count)
    width = group * stencil.shape[1]
    flops = 2 * 2 * var_count * lat_count * PARTS * row_count * width * (block_count // group)
    total = pl.pallas_call(
        kernel,
        grid=(block_count // group,),
        in_specs=[
            pl.BlockSpec((var_count, group, stencil.shape[1]), lambda i: (0, i, 0)),
            pl.BlockSpec((group, stencil.shape[1]), lambda i: (i, 0)),
            pl.BlockSpec((group, 4, stencil.shape[1]), lambda i: (i, 0, 0)),
        ],
        out_specs=pl.BlockSpec((var_count, row_count, lat_count), lambda i: (0, 0, 0)),
        out_shape=jax.ShapeDtypeStruct((var_count, row_count, lat_count), jnp.float32),
        scratch_shapes=[pltpu.VMEM((row_count, 2 * var_count * lat_count), jnp.float32)],
        cost_estimate=pl.CostEstimate(flops=flops, transcendentals=0, bytes_accessed=4 * 1024 * 1024),
    )(values, stencil, bilinear)
    return total.reshape(field_shape)


def allreduce_kernel(lat_devices, lon_devices, part_ref, out_ref, lon_buf, lat_buf, lon_send, lon_recv, lat_send, lat_recv):
    mesh_id = pl.DeviceIdType.MESH
    lat_me = lax.axis_index("lat")
    lon_me = lax.axis_index("lon")
    barrier = pltpu.get_barrier_semaphore()
    for peer in range(1, lon_devices):
        pl.semaphore_signal(barrier, inc=1, device_id=(lat_me, (lon_me + peer) % lon_devices), device_id_type=mesh_id)
    for peer in range(1, lat_devices):
        pl.semaphore_signal(barrier, inc=1, device_id=((lat_me + peer) % lat_devices, lon_me), device_id_type=mesh_id)
    pl.semaphore_wait(barrier, lon_devices + lat_devices - 2)

    def gather(buf, send, recv, count, me, target_of, source):
        copies = []
        for peer in range(1, count):
            target = (me + peer) % count
            copy = pltpu.make_async_remote_copy(
                src_ref=source,
                dst_ref=buf.at[me],
                send_sem=send.at[target],
                recv_sem=recv.at[me],
                device_id=target_of(target),
                device_id_type=mesh_id,
            )
            copy.start()
            copies.append((peer, copy))
        for peer, copy in copies:
            copy.wait_send()
        for peer in range(1, count):
            source_index = (me + count - peer) % count
            pltpu.make_async_remote_copy(
                src_ref=source,
                dst_ref=buf.at[source_index],
                send_sem=send.at[source_index],
                recv_sem=recv.at[source_index],
                device_id=target_of(source_index),
                device_id_type=mesh_id,
            ).wait_recv()

    gather(lon_buf, lon_send, lon_recv, lon_devices, lon_me, lambda t: (lat_me, t), part_ref)
    lon_buf[lon_me] = part_ref[...]
    total = lon_buf[0]
    for i in range(1, lon_devices):
        total = total + lon_buf[i]
    out_ref[...] = total
    gather(lat_buf, lat_send, lat_recv, lat_devices, lat_me, lambda t: (t, lon_me), out_ref)
    lat_buf[lat_me] = out_ref[...]
    total = lat_buf[0]
    for i in range(1, lat_devices):
        total = total + lat_buf[i]
    out_ref[...] = total


def allreduce_pallas(part):
    lat_devices = lax.axis_size("lat")
    lon_devices = lax.axis_size("lon")
    kernel = functools.partial(allreduce_kernel, lat_devices, lon_devices)
    return pl.pallas_call(
        kernel,
        in_specs=[pl.BlockSpec(memory_space=pltpu.VMEM)],
        out_specs=pl.BlockSpec(memory_space=pltpu.VMEM),
        out_shape=jax.ShapeDtypeStruct(part.shape, jnp.float32),
        scratch_shapes=[
            pltpu.VMEM((lon_devices,) + part.shape, jnp.float32),
            pltpu.VMEM((lat_devices,) + part.shape, jnp.float32),
            pltpu.SemaphoreType.DMA((lon_devices,)),
            pltpu.SemaphoreType.DMA((lon_devices,)),
            pltpu.SemaphoreType.DMA((lat_devices,)),
            pltpu.SemaphoreType.DMA((lat_devices,)),
        ],
        compiler_params=pltpu.CompilerParams(collective_id=0, has_side_effects=True),
    )(part)


def slots_of(block_owner, tile_count):
    targets = block_owner[:, 0]
    block_count = targets.shape[0]
    same_owner = (targets[:, None] == jnp.arange(tile_count, dtype=jnp.int32)[None, :]).astype(
        jnp.int32
    )
    order = jnp.arange(block_count, dtype=jnp.int32)
    lower = (order[:, None] > order[None, :]).astype(jnp.int32)
    earlier = jnp.dot(lower, same_owner)
    rank_within = jnp.sum(earlier * same_owner, axis=1)
    return targets * CAP + rank_within


def mix_blocks(values, correlation):
    return jnp.einsum("vsk,ik->vsi", values, correlation, precision=precise)


def shards(
    increment,
    residual,
    direction,
    diffusivity,
    deviation,
    stencil,
    bilinear,
    obs_weight,
    block_owner,
    correlation,
):
    lat_devices = lax.axis_size("lat")
    lon_devices = lax.axis_size("lon")
    tile_count = lat_devices * lon_devices
    both = widen_halo(jnp.stack([direction, diffusivity]), STEPS + 1)
    coeffs = padded_coeffs(face_coeffs(both[1], STEPS))

    def apply_diffusion(field):
        return diffuse(widen_halo(field, STEPS), coeffs)

    slots = slots_of(block_owner, tile_count)
    slot_table = (slots[:, None] == jnp.arange(tile_count * CAP, dtype=jnp.int32)[None, :]).astype(
        jnp.float32
    )
    field_shape = direction.shape
    state_field = deviation * diffuse(both[0][:, :, 1:-1, 1:-1], coeffs)
    observed = observe_pallas(state_field, stencil, bilinear, obs_weight)
    buffer = jnp.einsum("vbk,bs->vsk", observed, slot_table, precision=precise)
    returned = lax.all_to_all(
        mix_blocks(
            lax.all_to_all(buffer, ("lat", "lon"), split_axis=1, concat_axis=1, tiled=True),
            correlation,
        ),
        ("lat", "lon"),
        split_axis=1,
        concat_axis=1,
        tiled=True,
    )
    weighted = obs_weight * jnp.einsum("vsk,bs->vbk", returned, slot_table, precision=precise)
    spread_field = deviation * spread_pallas(weighted, stencil, bilinear, field_shape)
    image_field = direction + apply_diffusion(spread_field)
    local_sums = jnp.stack(
        [
            jnp.sum(residual * residual),
            jnp.sum(direction * image_field),
            jnp.sum(residual * image_field),
            jnp.sum(image_field * image_field),
        ]
    )
    sums = allreduce_pallas(jnp.zeros((8, 128), jnp.float32).at[0, :4].set(local_sums))[0]
    norm_now, curvature, cross, image_norm = sums[0], sums[1], sums[2], sums[3]
    step_size = norm_now / curvature
    increment = increment + step_size * direction
    residual = residual - step_size * image_field
    norm_next = norm_now - 2.0 * step_size * cross + step_size * step_size * image_norm
    direction = residual + norm_next / norm_now * direction
    return (increment, residual, direction)


def solution(mesh):
    in_specs = (
        P(None, None, "lon", "lat"),
        P(None, None, "lon", "lat"),
        P(None, None, "lon", "lat"),
        P(None, None, "lon", "lat"),
        P(None, None, "lon", "lat"),
        P(("lat", "lon"), None),
        P(("lat", "lon"), None, None),
        P(None, ("lat", "lon"), None),
        P(("lat", "lon"), None),
        P(("lat", "lon"), None),
    )
    out_specs = (
        P(None, None, "lon", "lat"),
        P(None, None, "lon", "lat"),
        P(None, None, "lon", "lat"),
    )
    return jax.shard_map(shards, mesh=mesh, in_specs=in_specs, out_specs=out_specs, check_vma=False)
```

```python
import functools
import math

import jax
import jax.numpy as jnp
from jax import lax
from jax.experimental import pallas as pl
from jax.experimental.pallas import tpu as pltpu
from jax.sharding import PartitionSpec as P

STEPS = 4
CAP = 2


precise = lax.Precision.HIGHEST


def widen_halo(value, width):
    lat_dim, lon_dim = value.ndim - 1, value.ndim - 2
    for axis, dim, wrap in (("lat", lat_dim, False), ("lon", lon_dim, True)):
        size, length = lax.axis_size(axis), value.shape[dim]
        up = [(i, (i + 1) % size) for i in range(size if wrap else size - 1)]
        down = [(j, i) for i, j in up]
        before = lax.ppermute(lax.slice_in_dim(value, length - width, length, axis=dim), axis, up)
        after = lax.ppermute(lax.slice_in_dim(value, 0, width, axis=dim), axis, down)
        value = jnp.concatenate([before, value, after], axis=dim)
    return value


def face_coeffs(wide, width):
    lat_count = wide.shape[3] - 2 * (width + 1)
    lat_devices = lax.axis_size("lat")
    first = lax.axis_index("lat") * lat_count - width
    cells = first + jnp.arange(lat_count + 2 * width, dtype=jnp.int32)
    inside = ((cells >= 0) & (cells < lat_devices * lat_count)).astype(jnp.float32)
    centre = wide[:, :, 1:-1, 1:-1]
    return (
        inside * (0.5 * (centre + wide[:, :, 1:-1, 2:])),
        inside * (0.5 * (centre + wide[:, :, 1:-1, :-2])),
        inside * (0.5 * (centre + wide[:, :, 2:, 1:-1])),
        inside * (0.5 * (centre + wide[:, :, :-2, 1:-1])),
    )


def diffuse_kernel(steps, field_ref, north_ref, south_ref, east_ref, west_ref, out_ref):
    rows, lanes = field_ref.shape[1], field_ref.shape[2]

    def one_plane(plane, carry):
        field = field_ref[plane]
        north, south, east, west = north_ref[plane], south_ref[plane], east_ref[plane], west_ref[plane]
        for sweep in range(steps):
            field = (
                field
                + north * (pltpu.roll(field, lanes - 1, 1) - field)
                + south * (pltpu.roll(field, 1, 1) - field)
                + east * (pltpu.roll(field, rows - 1, 0) - field)
                + west * (pltpu.roll(field, 1, 0) - field)
            )
        field = pltpu.roll(pltpu.roll(field, lanes - steps, 1), rows - steps, 0)
        out_ref[plane] = field[: out_ref.shape[1], : out_ref.shape[2]]
        return carry

    lax.fori_loop(0, field_ref.shape[0], one_plane, 0)


def pad_lanes(value):
    planes, rows, lanes = value.shape
    return jnp.pad(value, ((0, 0), (0, 0), (0, -lanes % 128)))


def padded_coeffs(coeffs):
    return tuple(pad_lanes(c.reshape((-1,) + c.shape[-2:])) for c in coeffs)


def diffuse(field, coeffs, planes_per_step=50):
    lead = field.shape[:-2]
    flat = pad_lanes(field.reshape((-1,) + field.shape[-2:]))
    planes, rows, lanes = flat.shape
    lon_count, lat_count = rows - 2 * STEPS, field.shape[-1] - 2 * STEPS
    spec = pl.BlockSpec((planes_per_step, rows, lanes), lambda i: (i, 0, 0))
    out = pl.pallas_call(
        functools.partial(diffuse_kernel, STEPS),
        grid=(planes // planes_per_step,),
        in_specs=[spec] * 5,
        out_specs=pl.BlockSpec((planes_per_step, lon_count, lat_count), lambda i: (i, 0, 0)),
        out_shape=jax.ShapeDtypeStruct((planes, lon_count, lat_count), field.dtype),
        cost_estimate=pl.CostEstimate(
            flops=14 * STEPS * planes * rows * lanes, transcendentals=0, bytes_accessed=24 * planes * rows * lanes
        ),
    )(flat, *coeffs)
    return out.reshape(lead + (lon_count, lat_count))


PARTS = 2


def split_parts(value):
    parts = []
    rest = value
    for part in range(PARTS):
        piece = rest.astype(jnp.bfloat16)
        parts.append(piece)
        rest = rest - piece.astype(jnp.float32)
    return parts


def obs_lines(cell_ref, weight_ref, group, lat_count):
    cells = cell_ref[...]
    rows = cells // lat_count
    lats = cells - rows * lat_count
    row_line = jnp.concatenate([rows[g : g + 1, :] for g in range(group)], axis=1)
    lat_line = jnp.concatenate([lats[g : g + 1, :] for g in range(group)], axis=1)
    weights = [
        jnp.concatenate([weight_ref[g, c : c + 1, :] for g in range(group)], axis=1) for c in range(4)
    ]
    return row_line, lat_line, weights


def select_maps(row_line, lat_line, weights, row_count, lat_count):
    width = row_line.shape[1]
    row_ids = lax.broadcasted_iota(jnp.int32, (row_count, width), 0)
    near_rows = (row_ids == row_line).astype(jnp.bfloat16)
    lat_ids = lax.broadcasted_iota(jnp.int32, (lat_count, width), 0)
    at_first = lat_ids == lat_line
    at_second = lat_ids == lat_line + 1
    near_lat = jnp.where(at_first, weights[0], 0.0) + jnp.where(at_second, weights[1], 0.0)
    far_lat = jnp.where(at_first, weights[2], 0.0) + jnp.where(at_second, weights[3], 0.0)
    return near_rows, near_lat, far_lat


def observe_kernel(group, var_count, row_count, lat_count, table_ref, cell_ref, weight_ref, scale_ref, out_ref):
    row_line, lat_line, weights = obs_lines(cell_ref, weight_ref, group, lat_count)
    near_rows, near_lat, far_lat = select_maps(row_line, lat_line, weights, row_count, lat_count)
    table = jnp.concatenate(split_parts(table_ref[...]), axis=1)
    picked = jnp.dot(table, jnp.concatenate([near_rows] * PARTS, axis=0), preferred_element_type=jnp.float32)
    half = var_count * lat_count
    for v in range(var_count):
        near_span = slice(v * lat_count, (v + 1) * lat_count)
        far_span = slice(half + v * lat_count, half + (v + 1) * lat_count)
        line = jnp.sum(picked[near_span] * near_lat + picked[far_span] * far_lat, axis=0, keepdims=True)
        for g in range(group):
            out_ref[v, g : g + 1, :] = scale_ref[v, g : g + 1, :] * line[:, g * 128 : (g + 1) * 128]


def spread_kernel(group, var_count, row_count, lat_count, value_ref, cell_ref, weight_ref, out_ref, total_ref):
    step = pl.program_id(0)

    @pl.when(step == 0)
    def _():
        total_ref[...] = jnp.zeros_like(total_ref)

    row_line, lat_line, weights = obs_lines(cell_ref, weight_ref, group, lat_count)
    near_rows, near_lat, far_lat = select_maps(row_line, lat_line, weights, row_count, lat_count)
    near_parts, far_parts = [], []
    for v in range(var_count):
        line = jnp.concatenate([value_ref[v, g : g + 1, :] for g in range(group)], axis=1)
        near_parts.append(near_lat * line)
        far_parts.append(far_lat * line)
    rhs = jnp.concatenate(split_parts(jnp.concatenate(near_parts + far_parts, axis=0)), axis=1)
    lhs = jnp.concatenate([near_rows] * PARTS, axis=1)
    total_ref[...] += lax.dot_general(
        lhs, rhs, (((1,), (1,)), ((), ())), preferred_element_type=jnp.float32
    )

    @pl.when(step == pl.num_programs(0) - 1)
    def _():
        total = total_ref[...]
        half = var_count * lat_count
        summed = total[:, :half] + pltpu.roll(total[:, half:], 1, 0)
        for v in range(var_count):
            out_ref[v] = summed[:, v * lat_count : (v + 1) * lat_count]


def observe_pallas(field, stencil, bilinear, obs_weight, group=16):
    var_count, level_count, lon_count, lat_count = field.shape
    row_count = level_count * lon_count
    block_count = stencil.shape[0]
    rows_t = jnp.transpose(field.reshape(var_count, row_count, lat_count), (0, 2, 1))
    shifted = jnp.concatenate([rows_t[:, :, 1:], jnp.zeros_like(rows_t[:, :, :1])], axis=2)
    table = jnp.concatenate([rows_t, shifted], axis=0).reshape(2 * var_count * lat_count, row_count)
    kernel = functools.partial(observe_kernel, group, var_count, row_count, lat_count)
    width = group * stencil.shape[1]
    flops = 2 * 2 * var_count * lat_count * PARTS * row_count * width * (block_count // group)
    return pl.pallas_call(
        kernel,
        grid=(block_count // group,),
        in_specs=[
            pl.BlockSpec(table.shape, lambda i: (0, 0)),
            pl.BlockSpec((group, stencil.shape[1]), lambda i: (i, 0)),
            pl.BlockSpec((group, 4, stencil.shape[1]), lambda i: (i, 0, 0)),
            pl.BlockSpec((var_count, group, stencil.shape[1]), lambda i: (0, i, 0)),
        ],
        out_specs=pl.BlockSpec((var_count, group, stencil.shape[1]), lambda i: (0, i, 0)),
        out_shape=jax.ShapeDtypeStruct(obs_weight.shape, jnp.float32),
        cost_estimate=pl.CostEstimate(flops=flops, transcendentals=0, bytes_accessed=4 * 1024 * 1024),
    )(table, stencil, bilinear, obs_weight)


def spread_pallas(values, stencil, bilinear, field_shape, group=16):
    var_count, level_count, lon_count, lat_count = field_shape
    row_count = level_count * lon_count
    block_count = stencil.shape[0]
    kernel = functools.partial(spread_kernel, group, var_count, row_count, lat_count)
    width = group * stencil.shape[1]
    flops = 2 * 2 * var_count * lat_count * PARTS * row_count * width * (block_count // group)
    total = pl.pallas_call(
        kernel,
        grid=(block_count // group,),
        in_specs=[
            pl.BlockSpec((var_count, group, stencil.shape[1]), lambda i: (0, i, 0)),
            pl.BlockSpec((group, stencil.shape[1]), lambda i: (i, 0)),
            pl.BlockSpec((group, 4, stencil.shape[1]), lambda i: (i, 0, 0)),
        ],
        out_specs=pl.BlockSpec((var_count, row_count, lat_count), lambda i: (0, 0, 0)),
        out_shape=jax.ShapeDtypeStruct((var_count, row_count, lat_count), jnp.float32),
        scratch_shapes=[pltpu.VMEM((row_count, 2 * var_count * lat_count), jnp.float32)],
        cost_estimate=pl.CostEstimate(flops=flops, transcendentals=0, bytes_accessed=4 * 1024 * 1024),
    )(values, stencil, bilinear)
    return total.reshape(field_shape)


def allreduce_kernel(lat_devices, lon_devices, part_ref, out_ref, lon_buf, lat_buf, lon_send, lon_recv, lat_send, lat_recv):
    mesh_id = pl.DeviceIdType.MESH
    lat_me = lax.axis_index("lat")
    lon_me = lax.axis_index("lon")
    barrier = pltpu.get_barrier_semaphore()
    for peer in range(1, lon_devices):
        pl.semaphore_signal(barrier, inc=1, device_id=(lat_me, (lon_me + peer) % lon_devices), device_id_type=mesh_id)
    for peer in range(1, lat_devices):
        pl.semaphore_signal(barrier, inc=1, device_id=((lat_me + peer) % lat_devices, lon_me), device_id_type=mesh_id)
    pl.semaphore_wait(barrier, lon_devices + lat_devices - 2)

    def gather(buf, send, recv, count, me, target_of, source):
        copies = []
        for peer in range(1, count):
            target = (me + peer) % count
            copy = pltpu.make_async_remote_copy(
                src_ref=source,
                dst_ref=buf.at[me],
                send_sem=send.at[target],
                recv_sem=recv.at[me],
                device_id=target_of(target),
                device_id_type=mesh_id,
            )
            copy.start()
            copies.append((peer, copy))
        for peer, copy in copies:
            copy.wait_send()
        for peer in range(1, count):
            source_index = (me + count - peer) % count
            pltpu.make_async_remote_copy(
                src_ref=source,
                dst_ref=buf.at[source_index],
                send_sem=send.at[source_index],
                recv_sem=recv.at[source_index],
                device_id=target_of(source_index),
                device_id_type=mesh_id,
            ).wait_recv()

    gather(lon_buf, lon_send, lon_recv, lon_devices, lon_me, lambda t: (lat_me, t), part_ref)
    lon_buf[lon_me] = part_ref[...]
    total = lon_buf[0]
    for i in range(1, lon_devices):
        total = total + lon_buf[i]
    out_ref[...] = total
    gather(lat_buf, lat_send, lat_recv, lat_devices, lat_me, lambda t: (t, lon_me), out_ref)
    lat_buf[lat_me] = out_ref[...]
    total = lat_buf[0]
    for i in range(1, lat_devices):
        total = total + lat_buf[i]
    out_ref[...] = total


def allreduce_pallas(part):
    lat_devices = lax.axis_size("lat")
    lon_devices = lax.axis_size("lon")
    kernel = functools.partial(allreduce_kernel, lat_devices, lon_devices)
    return pl.pallas_call(
        kernel,
        in_specs=[pl.BlockSpec(memory_space=pltpu.VMEM)],
        out_specs=pl.BlockSpec(memory_space=pltpu.VMEM),
        out_shape=jax.ShapeDtypeStruct(part.shape, jnp.float32),
        scratch_shapes=[
            pltpu.VMEM((lon_devices,) + part.shape, jnp.float32),
            pltpu.VMEM((lat_devices,) + part.shape, jnp.float32),
            pltpu.SemaphoreType.DMA((lon_devices,)),
            pltpu.SemaphoreType.DMA((lon_devices,)),
            pltpu.SemaphoreType.DMA((lat_devices,)),
            pltpu.SemaphoreType.DMA((lat_devices,)),
        ],
        compiler_params=pltpu.CompilerParams(collective_id=0, has_side_effects=True),
    )(part)


def slots_of(block_owner, tile_count):
    targets = block_owner[:, 0]
    block_count = targets.shape[0]
    same_owner = (targets[:, None] == jnp.arange(tile_count, dtype=jnp.int32)[None, :]).astype(
        jnp.int32
    )
    order = jnp.arange(block_count, dtype=jnp.int32)
    lower = (order[:, None] > order[None, :]).astype(jnp.int32)
    earlier = jnp.dot(lower, same_owner)
    rank_within = jnp.sum(earlier * same_owner, axis=1)
    return targets * CAP + rank_within


def mix_blocks(values, correlation):
    return jnp.einsum("vsk,ik->vsi", values, correlation, precision=precise)


def shards(
    increment,
    residual,
    direction,
    diffusivity,
    deviation,
    stencil,
    bilinear,
    obs_weight,
    block_owner,
    correlation,
):
    lat_devices = lax.axis_size("lat")
    lon_devices = lax.axis_size("lon")
    tile_count = lat_devices * lon_devices
    both = widen_halo(jnp.stack([direction, diffusivity]), STEPS + 1)
    coeffs = padded_coeffs(face_coeffs(both[1], STEPS))

    def apply_diffusion(field):
        return diffuse(widen_halo(field, STEPS), coeffs)

    slots = slots_of(block_owner, tile_count)
    slot_table = (slots[:, None] == jnp.arange(tile_count * CAP, dtype=jnp.int32)[None, :]).astype(
        jnp.float32
    )
    field_shape = direction.shape
    state_field = deviation * diffuse(both[0][:, :, 1:-1, 1:-1], coeffs)
    observed = observe_pallas(state_field, stencil, bilinear, obs_weight)
    buffer = jnp.einsum("vbk,bs->vsk", observed, slot_table, precision=precise)
    returned = lax.all_to_all(
        mix_blocks(
            lax.all_to_all(buffer, ("lat", "lon"), split_axis=1, concat_axis=1, tiled=True),
            correlation,
        ),
        ("lat", "lon"),
        split_axis=1,
        concat_axis=1,
        tiled=True,
    )
    weighted = obs_weight * jnp.einsum("vsk,bs->vbk", returned, slot_table, precision=precise)
    spread_field = deviation * spread_pallas(weighted, stencil, bilinear, field_shape)
    image_field = direction + apply_diffusion(spread_field)
    local_sums = jnp.stack(
        [
            jnp.sum(residual * residual),
            jnp.sum(direction * image_field),
            jnp.sum(residual * image_field),
            jnp.sum(image_field * image_field),
        ]
    )
    sums = allreduce_pallas(jnp.zeros((8, 128), jnp.float32).at[0, :4].set(local_sums))[0]
    norm_now, curvature, cross, image_norm = sums[0], sums[1], sums[2], sums[3]
    step_size = norm_now / curvature
    increment = increment + step_size * direction
    residual = residual - step_size * image_field
    norm_next = norm_now - 2.0 * step_size * cross + step_size * step_size * image_norm
    direction = residual + norm_next / norm_now * direction
    return (increment, residual, direction)


def solution(mesh):
    in_specs = (
        P(None, None, "lon", "lat"),
        P(None, None, "lon", "lat"),
        P(None, None, "lon", "lat"),
        P(None, None, "lon", "lat"),
        P(None, None, "lon", "lat"),
        P(("lat", "lon"), None),
        P(("lat", "lon"), None, None),
        P(None, ("lat", "lon"), None),
        P(("lat", "lon"), None),
        P(("lat", "lon"), None),
    )
    out_specs = (
        P(None, None, "lon", "lat"),
        P(None, None, "lon", "lat"),
        P(None, None, "lon", "lat"),
    )
    return jax.shard_map(shards, mesh=mesh, in_specs=in_specs, out_specs=out_specs, check_vma=False)
```

```python
import functools
import math

import jax
import jax.numpy as jnp
from jax import lax
from jax.experimental import pallas as pl
from jax.experimental.pallas import tpu as pltpu
from jax.sharding import PartitionSpec as P

STEPS = 4
CAP = 2


precise = lax.Precision.HIGHEST


def widen_halo(value, width):
    lat_dim, lon_dim = value.ndim - 1, value.ndim - 2
    for axis, dim, wrap in (("lat", lat_dim, False), ("lon", lon_dim, True)):
        size, length = lax.axis_size(axis), value.shape[dim]
        up = [(i, (i + 1) % size) for i in range(size if wrap else size - 1)]
        down = [(j, i) for i, j in up]
        before = lax.ppermute(lax.slice_in_dim(value, length - width, length, axis=dim), axis, up)
        after = lax.ppermute(lax.slice_in_dim(value, 0, width, axis=dim), axis, down)
        value = jnp.concatenate([before, value, after], axis=dim)
    return value


def face_coeffs(wide, width):
    lat_count = wide.shape[3] - 2 * (width + 1)
    lat_devices = lax.axis_size("lat")
    first = lax.axis_index("lat") * lat_count - width
    cells = first + jnp.arange(lat_count + 2 * width, dtype=jnp.int32)
    inside = ((cells >= 0) & (cells < lat_devices * lat_count)).astype(jnp.float32)
    centre = wide[:, :, 1:-1, 1:-1]
    return (
        inside * (0.5 * (centre + wide[:, :, 1:-1, 2:])),
        inside * (0.5 * (centre + wide[:, :, 1:-1, :-2])),
        inside * (0.5 * (centre + wide[:, :, 2:, 1:-1])),
        inside * (0.5 * (centre + wide[:, :, :-2, 1:-1])),
    )


def diffuse_kernel(steps, field_ref, north_ref, south_ref, east_ref, west_ref, out_ref):
    field = field_ref[...]
    rows, lanes = field.shape[1], field.shape[2]
    north, south, east, west = north_ref[...], south_ref[...], east_ref[...], west_ref[...]
    for sweep in range(steps):
        field = (
            field
            + north * (pltpu.roll(field, lanes - 1, 2) - field)
            + south * (pltpu.roll(field, 1, 2) - field)
            + east * (pltpu.roll(field, rows - 1, 1) - field)
            + west * (pltpu.roll(field, 1, 1) - field)
        )
    field = pltpu.roll(pltpu.roll(field, lanes - steps, 2), rows - steps, 1)
    out_ref[...] = field[:, : out_ref.shape[1], : out_ref.shape[2]]


def pad_lanes(value):
    planes, rows, lanes = value.shape
    return jnp.pad(value, ((0, 0), (0, 0), (0, -lanes % 128)))


def padded_coeffs(coeffs):
    return tuple(pad_lanes(c.reshape((-1,) + c.shape[-2:])) for c in coeffs)


def diffuse(field, coeffs, planes_per_step=50):
    lead = field.shape[:-2]
    flat = pad_lanes(field.reshape((-1,) + field.shape[-2:]))
    planes, rows, lanes = flat.shape
    lon_count, lat_count = rows - 2 * STEPS, field.shape[-1] - 2 * STEPS
    spec = pl.BlockSpec((planes_per_step, rows, lanes), lambda i: (i, 0, 0))
    out = pl.pallas_call(
        functools.partial(diffuse_kernel, STEPS),
        grid=(planes // planes_per_step,),
        in_specs=[spec] * 5,
        out_specs=pl.BlockSpec((planes_per_step, lon_count, lat_count), lambda i: (i, 0, 0)),
        out_shape=jax.ShapeDtypeStruct((planes, lon_count, lat_count), field.dtype),
        cost_estimate=pl.CostEstimate(
            flops=14 * STEPS * planes * rows * lanes, transcendentals=0, bytes_accessed=24 * planes * rows * lanes
        ),
    )(flat, *coeffs)
    return out.reshape(lead + (lon_count, lat_count))


PARTS = 2


def split_parts(value):
    parts = []
    rest = value
    for part in range(PARTS):
        piece = rest.astype(jnp.bfloat16)
        parts.append(piece)
        rest = rest - piece.astype(jnp.float32)
    return parts


def obs_lines(cell_ref, weight_ref, group, lat_count):
    cells = cell_ref[...]
    rows = cells // lat_count
    lats = cells - rows * lat_count
    row_line = jnp.concatenate([rows[g : g + 1, :] for g in range(group)], axis=1)
    lat_line = jnp.concatenate([lats[g : g + 1, :] for g in range(group)], axis=1)
    weights = [
        jnp.concatenate([weight_ref[g, c : c + 1, :] for g in range(group)], axis=1) for c in range(4)
    ]
    return row_line, lat_line, weights


def select_maps(row_line, lat_line, weights, row_count, lat_count):
    width = row_line.shape[1]
    row_ids = lax.broadcasted_iota(jnp.int32, (row_count, width), 0)
    near_rows = (row_ids == row_line).astype(jnp.bfloat16)
    lat_ids = lax.broadcasted_iota(jnp.int32, (lat_count, width), 0)
    at_first = lat_ids == lat_line
    at_second = lat_ids == lat_line + 1
    near_lat = jnp.where(at_first, weights[0], 0.0) + jnp.where(at_second, weights[1], 0.0)
    far_lat = jnp.where(at_first, weights[2], 0.0) + jnp.where(at_second, weights[3], 0.0)
    return near_rows, near_lat, far_lat


def observe_kernel(group, var_count, row_count, lat_count, table_ref, cell_ref, weight_ref, scale_ref, out_ref):
    row_line, lat_line, weights = obs_lines(cell_ref, weight_ref, group, lat_count)
    near_rows, near_lat, far_lat = select_maps(row_line, lat_line, weights, row_count, lat_count)
    table = jnp.concatenate(split_parts(table_ref[...]), axis=1)
    picked = jnp.dot(table, jnp.concatenate([near_rows] * PARTS, axis=0), preferred_element_type=jnp.float32)
    half = var_count * lat_count
    for v in range(var_count):
        near_span = slice(v * lat_count, (v + 1) * lat_count)
        far_span = slice(half + v * lat_count, half + (v + 1) * lat_count)
        line = jnp.sum(picked[near_span] * near_lat + picked[far_span] * far_lat, axis=0, keepdims=True)
        for g in range(group):
            out_ref[v, g : g + 1, :] = scale_ref[v, g : g + 1, :] * line[:, g * 128 : (g + 1) * 128]


def spread_kernel(group, var_count, row_count, lat_count, value_ref, cell_ref, weight_ref, out_ref, total_ref):
    step = pl.program_id(0)

    @pl.when(step == 0)
    def _():
        total_ref[...] = jnp.zeros_like(total_ref)

    row_line, lat_line, weights = obs_lines(cell_ref, weight_ref, group, lat_count)
    near_rows, near_lat, far_lat = select_maps(row_line, lat_line, weights, row_count, lat_count)
    near_parts, far_parts = [], []
    for v in range(var_count):
        line = jnp.concatenate([value_ref[v, g : g + 1, :] for g in range(group)], axis=1)
        near_parts.append(near_lat * line)
        far_parts.append(far_lat * line)
    rhs = jnp.concatenate(split_parts(jnp.concatenate(near_parts + far_parts, axis=0)), axis=1)
    lhs = jnp.concatenate([near_rows] * PARTS, axis=1)
    total_ref[...] += lax.dot_general(
        lhs, rhs, (((1,), (1,)), ((), ())), preferred_element_type=jnp.float32
    )

    @pl.when(step == pl.num_programs(0) - 1)
    def _():
        total = total_ref[...]
        half = var_count * lat_count
        summed = total[:, :half] + pltpu.roll(total[:, half:], 1, 0)
        for v in range(var_count):
            out_ref[v] = summed[:, v * lat_count : (v + 1) * lat_count]


def observe_pallas(field, stencil, bilinear, obs_weight, group=32):
    var_count, level_count, lon_count, lat_count = field.shape
    row_count = level_count * lon_count
    block_count = stencil.shape[0]
    rows_t = jnp.transpose(field.reshape(var_count, row_count, lat_count), (0, 2, 1))
    shifted = jnp.concatenate([rows_t[:, :, 1:], jnp.zeros_like(rows_t[:, :, :1])], axis=2)
    table = jnp.concatenate([rows_t, shifted], axis=0).reshape(2 * var_count * lat_count, row_count)
    kernel = functools.partial(observe_kernel, group, var_count, row_count, lat_count)
    width = group * stencil.shape[1]
    flops = 2 * 2 * var_count * lat_count * PARTS * row_count * width * (block_count // group)
    return pl.pallas_call(
        kernel,
        grid=(block_count // group,),
        in_specs=[
            pl.BlockSpec(table.shape, lambda i: (0, 0)),
            pl.BlockSpec((group, stencil.shape[1]), lambda i: (i, 0)),
            pl.BlockSpec((group, 4, stencil.shape[1]), lambda i: (i, 0, 0)),
            pl.BlockSpec((var_count, group, stencil.shape[1]), lambda i: (0, i, 0)),
        ],
        out_specs=pl.BlockSpec((var_count, group, stencil.shape[1]), lambda i: (0, i, 0)),
        out_shape=jax.ShapeDtypeStruct(obs_weight.shape, jnp.float32),
        cost_estimate=pl.CostEstimate(flops=flops, transcendentals=0, bytes_accessed=4 * 1024 * 1024),
    )(table, stencil, bilinear, obs_weight)


def spread_pallas(values, stencil, bilinear, field_shape, group=32):
    var_count, level_count, lon_count, lat_count = field_shape
    row_count = level_count * lon_count
    block_count = stencil.shape[0]
    kernel = functools.partial(spread_kernel, group, var_count, row_count, lat_count)
    width = group * stencil.shape[1]
    flops = 2 * 2 * var_count * lat_count * PARTS * row_count * width * (block_count // group)
    total = pl.pallas_call(
        kernel,
        grid=(block_count // group,),
        in_specs=[
            pl.BlockSpec((var_count, group, stencil.shape[1]), lambda i: (0, i, 0)),
            pl.BlockSpec((group, stencil.shape[1]), lambda i: (i, 0)),
            pl.BlockSpec((group, 4, stencil.shape[1]), lambda i: (i, 0, 0)),
        ],
        out_specs=pl.BlockSpec((var_count, row_count, lat_count), lambda i: (0, 0, 0)),
        out_shape=jax.ShapeDtypeStruct((var_count, row_count, lat_count), jnp.float32),
        scratch_shapes=[pltpu.VMEM((row_count, 2 * var_count * lat_count), jnp.float32)],
        cost_estimate=pl.CostEstimate(flops=flops, transcendentals=0, bytes_accessed=4 * 1024 * 1024),
    )(values, stencil, bilinear)
    return total.reshape(field_shape)


def allreduce_kernel(lat_devices, lon_devices, part_ref, out_ref, lon_buf, lat_buf, lon_send, lon_recv, lat_send, lat_recv):
    mesh_id = pl.DeviceIdType.MESH
    lat_me = lax.axis_index("lat")
    lon_me = lax.axis_index("lon")
    barrier = pltpu.get_barrier_semaphore()
    for peer in range(1, lon_devices):
        pl.semaphore_signal(barrier, inc=1, device_id=(lat_me, (lon_me + peer) % lon_devices), device_id_type=mesh_id)
    for peer in range(1, lat_devices):
        pl.semaphore_signal(barrier, inc=1, device_id=((lat_me + peer) % lat_devices, lon_me), device_id_type=mesh_id)
    pl.semaphore_wait(barrier, lon_devices + lat_devices - 2)

    def gather(buf, send, recv, count, me, target_of, source):
        copies = []
        for peer in range(1, count):
            target = (me + peer) % count
            copy = pltpu.make_async_remote_copy(
                src_ref=source,
                dst_ref=buf.at[me],
                send_sem=send.at[target],
                recv_sem=recv.at[me],
                device_id=target_of(target),
                device_id_type=mesh_id,
            )
            copy.start()
            copies.append((peer, copy))
        for peer, copy in copies:
            copy.wait_send()
        for peer in range(1, count):
            source_index = (me + count - peer) % count
            pltpu.make_async_remote_copy(
                src_ref=source,
                dst_ref=buf.at[source_index],
                send_sem=send.at[source_index],
                recv_sem=recv.at[source_index],
                device_id=target_of(source_index),
                device_id_type=mesh_id,
            ).wait_recv()

    gather(lon_buf, lon_send, lon_recv, lon_devices, lon_me, lambda t: (lat_me, t), part_ref)
    lon_buf[lon_me] = part_ref[...]
    total = lon_buf[0]
    for i in range(1, lon_devices):
        total = total + lon_buf[i]
    out_ref[...] = total
    gather(lat_buf, lat_send, lat_recv, lat_devices, lat_me, lambda t: (t, lon_me), out_ref)
    lat_buf[lat_me] = out_ref[...]
    total = lat_buf[0]
    for i in range(1, lat_devices):
        total = total + lat_buf[i]
    out_ref[...] = total


def allreduce_pallas(part):
    lat_devices = lax.axis_size("lat")
    lon_devices = lax.axis_size("lon")
    kernel = functools.partial(allreduce_kernel, lat_devices, lon_devices)
    return pl.pallas_call(
        kernel,
        in_specs=[pl.BlockSpec(memory_space=pltpu.VMEM)],
        out_specs=pl.BlockSpec(memory_space=pltpu.VMEM),
        out_shape=jax.ShapeDtypeStruct(part.shape, jnp.float32),
        scratch_shapes=[
            pltpu.VMEM((lon_devices,) + part.shape, jnp.float32),
            pltpu.VMEM((lat_devices,) + part.shape, jnp.float32),
            pltpu.SemaphoreType.DMA((lon_devices,)),
            pltpu.SemaphoreType.DMA((lon_devices,)),
            pltpu.SemaphoreType.DMA((lat_devices,)),
            pltpu.SemaphoreType.DMA((lat_devices,)),
        ],
        compiler_params=pltpu.CompilerParams(collective_id=0, has_side_effects=True),
    )(part)


def slots_of(block_owner, tile_count):
    targets = block_owner[:, 0]
    block_count = targets.shape[0]
    same_owner = (targets[:, None] == jnp.arange(tile_count, dtype=jnp.int32)[None, :]).astype(
        jnp.int32
    )
    order = jnp.arange(block_count, dtype=jnp.int32)
    lower = (order[:, None] > order[None, :]).astype(jnp.int32)
    earlier = jnp.dot(lower, same_owner)
    rank_within = jnp.sum(earlier * same_owner, axis=1)
    return targets * CAP + rank_within


def mix_blocks(values, correlation):
    return jnp.einsum("vsk,ik->vsi", values, correlation, precision=precise)


def shards(
    increment,
    residual,
    direction,
    diffusivity,
    deviation,
    stencil,
    bilinear,
    obs_weight,
    block_owner,
    correlation,
):
    lat_devices = lax.axis_size("lat")
    lon_devices = lax.axis_size("lon")
    tile_count = lat_devices * lon_devices
    both = widen_halo(jnp.stack([direction, diffusivity]), STEPS + 1)
    coeffs = padded_coeffs(face_coeffs(both[1], STEPS))

    def apply_diffusion(field):
        return diffuse(widen_halo(field, STEPS), coeffs)

    slots = slots_of(block_owner, tile_count)
    slot_table = (slots[:, None] == jnp.arange(tile_count * CAP, dtype=jnp.int32)[None, :]).astype(
        jnp.float32
    )
    field_shape = direction.shape
    state_field = deviation * diffuse(both[0][:, :, 1:-1, 1:-1], coeffs)
    observed = observe_pallas(state_field, stencil, bilinear, obs_weight)
    buffer = jnp.einsum("vbk,bs->vsk", observed, slot_table, precision=precise)
    returned = lax.all_to_all(
        mix_blocks(
            lax.all_to_all(buffer, ("lat", "lon"), split_axis=1, concat_axis=1, tiled=True),
            correlation,
        ),
        ("lat", "lon"),
        split_axis=1,
        concat_axis=1,
        tiled=True,
    )
    weighted = obs_weight * jnp.einsum("vsk,bs->vbk", returned, slot_table, precision=precise)
    spread_field = deviation * spread_pallas(weighted, stencil, bilinear, field_shape)
    image_field = direction + apply_diffusion(spread_field)
    local_sums = jnp.stack(
        [
            jnp.sum(residual * residual),
            jnp.sum(direction * image_field),
            jnp.sum(residual * image_field),
            jnp.sum(image_field * image_field),
        ]
    )
    sums = allreduce_pallas(jnp.zeros((8, 128), jnp.float32).at[0, :4].set(local_sums))[0]
    norm_now, curvature, cross, image_norm = sums[0], sums[1], sums[2], sums[3]
    step_size = norm_now / curvature
    increment = increment + step_size * direction
    residual = residual - step_size * image_field
    norm_next = norm_now - 2.0 * step_size * cross + step_size * step_size * image_norm
    direction = residual + norm_next / norm_now * direction
    return (increment, residual, direction)


def solution(mesh):
    in_specs = (
        P(None, None, "lon", "lat"),
        P(None, None, "lon", "lat"),
        P(None, None, "lon", "lat"),
        P(None, None, "lon", "lat"),
        P(None, None, "lon", "lat"),
        P(("lat", "lon"), None),
        P(("lat", "lon"), None, None),
        P(None, ("lat", "lon"), None),
        P(("lat", "lon"), None),
        P(("lat", "lon"), None),
    )
    out_specs = (
        P(None, None, "lon", "lat"),
        P(None, None, "lon", "lat"),
        P(None, None, "lon", "lat"),
    )
    return jax.shard_map(shards, mesh=mesh, in_specs=in_specs, out_specs=out_specs, check_vma=False)
```

```python
import functools
import math

import jax
import jax.numpy as jnp
from jax import lax
from jax.experimental import pallas as pl
from jax.experimental.pallas import tpu as pltpu
from jax.sharding import PartitionSpec as P

STEPS = 4
CAP = 2


precise = lax.Precision.HIGHEST


def widen_halo(value, width):
    lat_dim, lon_dim = value.ndim - 1, value.ndim - 2
    for axis, dim, wrap in (("lat", lat_dim, False), ("lon", lon_dim, True)):
        size, length = lax.axis_size(axis), value.shape[dim]
        up = [(i, (i + 1) % size) for i in range(size if wrap else size - 1)]
        down = [(j, i) for i, j in up]
        before = lax.ppermute(lax.slice_in_dim(value, length - width, length, axis=dim), axis, up)
        after = lax.ppermute(lax.slice_in_dim(value, 0, width, axis=dim), axis, down)
        value = jnp.concatenate([before, value, after], axis=dim)
    return value


def face_coeffs(wide, width):
    wide = jnp.pad(wide, ((0, 0), (0, 0), (1, 1), (1, 1)))
    lat_count = wide.shape[3] - 2 * (width + 1)
    lat_devices = lax.axis_size("lat")
    first = lax.axis_index("lat") * lat_count - width
    cells = first + jnp.arange(lat_count + 2 * width, dtype=jnp.int32)
    inside = ((cells >= 0) & (cells < lat_devices * lat_count)).astype(jnp.float32)
    centre = wide[:, :, 1:-1, 1:-1]
    return (
        inside * (0.5 * (centre + wide[:, :, 1:-1, 2:])),
        inside * (0.5 * (centre + wide[:, :, 1:-1, :-2])),
        inside * (0.5 * (centre + wide[:, :, 2:, 1:-1])),
        inside * (0.5 * (centre + wide[:, :, :-2, 1:-1])),
    )


def diffuse_kernel(steps, field_ref, north_ref, south_ref, east_ref, west_ref, out_ref):
    field = field_ref[...]
    rows, lanes = field.shape[1], field.shape[2]
    north, south, east, west = north_ref[...], south_ref[...], east_ref[...], west_ref[...]
    for sweep in range(steps):
        field = (
            field
            + north * (pltpu.roll(field, lanes - 1, 2) - field)
            + south * (pltpu.roll(field, 1, 2) - field)
            + east * (pltpu.roll(field, rows - 1, 1) - field)
            + west * (pltpu.roll(field, 1, 1) - field)
        )
    field = pltpu.roll(pltpu.roll(field, lanes - steps, 2), rows - steps, 1)
    out_ref[...] = field[:, : out_ref.shape[1], : out_ref.shape[2]]


def pad_lanes(value):
    planes, rows, lanes = value.shape
    return jnp.pad(value, ((0, 0), (0, 0), (0, -lanes % 128)))


def padded_coeffs(coeffs):
    return tuple(pad_lanes(c.reshape((-1,) + c.shape[-2:])) for c in coeffs)


def diffuse(field, coeffs, planes_per_step=50):
    lead = field.shape[:-2]
    flat = pad_lanes(field.reshape((-1,) + field.shape[-2:]))
    planes, rows, lanes = flat.shape
    lon_count, lat_count = rows - 2 * STEPS, field.shape[-1] - 2 * STEPS
    spec = pl.BlockSpec((planes_per_step, rows, lanes), lambda i: (i, 0, 0))
    out = pl.pallas_call(
        functools.partial(diffuse_kernel, STEPS),
        grid=(planes // planes_per_step,),
        in_specs=[spec] * 5,
        out_specs=pl.BlockSpec((planes_per_step, lon_count, lat_count), lambda i: (i, 0, 0)),
        out_shape=jax.ShapeDtypeStruct((planes, lon_count, lat_count), field.dtype),
        cost_estimate=pl.CostEstimate(
            flops=14 * STEPS * planes * rows * lanes, transcendentals=0, bytes_accessed=24 * planes * rows * lanes
        ),
    )(flat, *coeffs)
    return out.reshape(lead + (lon_count, lat_count))


PARTS = 2


def split_parts(value):
    parts = []
    rest = value
    for part in range(PARTS):
        piece = rest.astype(jnp.bfloat16)
        parts.append(piece)
        rest = rest - piece.astype(jnp.float32)
    return parts


def obs_lines(cell_ref, weight_ref, group, lat_count):
    cells = cell_ref[...]
    rows = cells // lat_count
    lats = cells - rows * lat_count
    row_line = jnp.concatenate([rows[g : g + 1, :] for g in range(group)], axis=1)
    lat_line = jnp.concatenate([lats[g : g + 1, :] for g in range(group)], axis=1)
    weights = [
        jnp.concatenate([weight_ref[g, c : c + 1, :] for g in range(group)], axis=1) for c in range(4)
    ]
    return row_line, lat_line, weights


def select_maps(row_line, lat_line, weights, row_count, lat_count):
    width = row_line.shape[1]
    row_ids = lax.broadcasted_iota(jnp.int32, (row_count, width), 0)
    near_rows = (row_ids == row_line).astype(jnp.bfloat16)
    lat_ids = lax.broadcasted_iota(jnp.int32, (lat_count, width), 0)
    at_first = lat_ids == lat_line
    at_second = lat_ids == lat_line + 1
    near_lat = jnp.where(at_first, weights[0], 0.0) + jnp.where(at_second, weights[1], 0.0)
    far_lat = jnp.where(at_first, weights[2], 0.0) + jnp.where(at_second, weights[3], 0.0)
    return near_rows, near_lat, far_lat


def observe_kernel(group, var_count, row_count, lat_count, table_ref, cell_ref, weight_ref, scale_ref, out_ref):
    row_line, lat_line, weights = obs_lines(cell_ref, weight_ref, group, lat_count)
    near_rows, near_lat, far_lat = select_maps(row_line, lat_line, weights, row_count, lat_count)
    table = jnp.concatenate(split_parts(table_ref[...]), axis=1)
    picked = jnp.dot(table, jnp.concatenate([near_rows] * PARTS, axis=0), preferred_element_type=jnp.float32)
    half = var_count * lat_count
    for v in range(var_count):
        near_span = slice(v * lat_count, (v + 1) * lat_count)
        far_span = slice(half + v * lat_count, half + (v + 1) * lat_count)
        line = jnp.sum(picked[near_span] * near_lat + picked[far_span] * far_lat, axis=0, keepdims=True)
        for g in range(group):
            out_ref[v, g : g + 1, :] = scale_ref[v, g : g + 1, :] * line[:, g * 128 : (g + 1) * 128]


def spread_kernel(group, var_count, row_count, lat_count, value_ref, cell_ref, weight_ref, out_ref, total_ref):
    step = pl.program_id(0)

    @pl.when(step == 0)
    def _():
        total_ref[...] = jnp.zeros_like(total_ref)

    row_line, lat_line, weights = obs_lines(cell_ref, weight_ref, group, lat_count)
    near_rows, near_lat, far_lat = select_maps(row_line, lat_line, weights, row_count, lat_count)
    near_parts, far_parts = [], []
    for v in range(var_count):
        line = jnp.concatenate([value_ref[v, g : g + 1, :] for g in range(group)], axis=1)
        near_parts.append(near_lat * line)
        far_parts.append(far_lat * line)
    rhs = jnp.concatenate(split_parts(jnp.concatenate(near_parts + far_parts, axis=0)), axis=1)
    lhs = jnp.concatenate([near_rows] * PARTS, axis=1)
    total_ref[...] += lax.dot_general(
        lhs, rhs, (((1,), (1,)), ((), ())), preferred_element_type=jnp.float32
    )

    @pl.when(step == pl.num_programs(0) - 1)
    def _():
        total = total_ref[...]
        half = var_count * lat_count
        summed = total[:, :half] + pltpu.roll(total[:, half:], 1, 0)
        for v in range(var_count):
            out_ref[v] = summed[:, v * lat_count : (v + 1) * lat_count]


def observe_pallas(field, stencil, bilinear, obs_weight, group=32):
    var_count, level_count, lon_count, lat_count = field.shape
    row_count = level_count * lon_count
    block_count = stencil.shape[0]
    rows_t = jnp.transpose(field.reshape(var_count, row_count, lat_count), (0, 2, 1))
    shifted = jnp.concatenate([rows_t[:, :, 1:], jnp.zeros_like(rows_t[:, :, :1])], axis=2)
    table = jnp.concatenate([rows_t, shifted], axis=0).reshape(2 * var_count * lat_count, row_count)
    kernel = functools.partial(observe_kernel, group, var_count, row_count, lat_count)
    width = group * stencil.shape[1]
    flops = 2 * 2 * var_count * lat_count * PARTS * row_count * width * (block_count // group)
    return pl.pallas_call(
        kernel,
        grid=(block_count // group,),
        in_specs=[
            pl.BlockSpec(table.shape, lambda i: (0, 0)),
            pl.BlockSpec((group, stencil.shape[1]), lambda i: (i, 0)),
            pl.BlockSpec((group, 4, stencil.shape[1]), lambda i: (i, 0, 0)),
            pl.BlockSpec((var_count, group, stencil.shape[1]), lambda i: (0, i, 0)),
        ],
        out_specs=pl.BlockSpec((var_count, group, stencil.shape[1]), lambda i: (0, i, 0)),
        out_shape=jax.ShapeDtypeStruct(obs_weight.shape, jnp.float32),
        cost_estimate=pl.CostEstimate(flops=flops, transcendentals=0, bytes_accessed=4 * 1024 * 1024),
    )(table, stencil, bilinear, obs_weight)


def spread_pallas(values, stencil, bilinear, field_shape, group=32):
    var_count, level_count, lon_count, lat_count = field_shape
    row_count = level_count * lon_count
    block_count = stencil.shape[0]
    kernel = functools.partial(spread_kernel, group, var_count, row_count, lat_count)
    width = group * stencil.shape[1]
    flops = 2 * 2 * var_count * lat_count * PARTS * row_count * width * (block_count // group)
    total = pl.pallas_call(
        kernel,
        grid=(block_count // group,),
        in_specs=[
            pl.BlockSpec((var_count, group, stencil.shape[1]), lambda i: (0, i, 0)),
            pl.BlockSpec((group, stencil.shape[1]), lambda i: (i, 0)),
            pl.BlockSpec((group, 4, stencil.shape[1]), lambda i: (i, 0, 0)),
        ],
        out_specs=pl.BlockSpec((var_count, row_count, lat_count), lambda i: (0, 0, 0)),
        out_shape=jax.ShapeDtypeStruct((var_count, row_count, lat_count), jnp.float32),
        scratch_shapes=[pltpu.VMEM((row_count, 2 * var_count * lat_count), jnp.float32)],
        cost_estimate=pl.CostEstimate(flops=flops, transcendentals=0, bytes_accessed=4 * 1024 * 1024),
    )(values, stencil, bilinear)
    return total.reshape(field_shape)


def allreduce_kernel(lat_devices, lon_devices, part_ref, out_ref, lon_buf, lat_buf, lon_send, lon_recv, lat_send, lat_recv):
    mesh_id = pl.DeviceIdType.MESH
    lat_me = lax.axis_index("lat")
    lon_me = lax.axis_index("lon")
    barrier = pltpu.get_barrier_semaphore()
    for peer in range(1, lon_devices):
        pl.semaphore_signal(barrier, inc=1, device_id=(lat_me, (lon_me + peer) % lon_devices), device_id_type=mesh_id)
    for peer in range(1, lat_devices):
        pl.semaphore_signal(barrier, inc=1, device_id=((lat_me + peer) % lat_devices, lon_me), device_id_type=mesh_id)
    pl.semaphore_wait(barrier, lon_devices + lat_devices - 2)

    def gather(buf, send, recv, count, me, target_of, source):
        copies = []
        for peer in range(1, count):
            target = (me + peer) % count
            copy = pltpu.make_async_remote_copy(
                src_ref=source,
                dst_ref=buf.at[me],
                send_sem=send.at[target],
                recv_sem=recv.at[me],
                device_id=target_of(target),
                device_id_type=mesh_id,
            )
            copy.start()
            copies.append((peer, copy))
        for peer, copy in copies:
            copy.wait_send()
        for peer in range(1, count):
            source_index = (me + count - peer) % count
            pltpu.make_async_remote_copy(
                src_ref=source,
                dst_ref=buf.at[source_index],
                send_sem=send.at[source_index],
                recv_sem=recv.at[source_index],
                device_id=target_of(source_index),
                device_id_type=mesh_id,
            ).wait_recv()

    gather(lon_buf, lon_send, lon_recv, lon_devices, lon_me, lambda t: (lat_me, t), part_ref)
    lon_buf[lon_me] = part_ref[...]
    total = lon_buf[0]
    for i in range(1, lon_devices):
        total = total + lon_buf[i]
    out_ref[...] = total
    gather(lat_buf, lat_send, lat_recv, lat_devices, lat_me, lambda t: (t, lon_me), out_ref)
    lat_buf[lat_me] = out_ref[...]
    total = lat_buf[0]
    for i in range(1, lat_devices):
        total = total + lat_buf[i]
    out_ref[...] = total


def allreduce_pallas(part):
    lat_devices = lax.axis_size("lat")
    lon_devices = lax.axis_size("lon")
    kernel = functools.partial(allreduce_kernel, lat_devices, lon_devices)
    return pl.pallas_call(
        kernel,
        in_specs=[pl.BlockSpec(memory_space=pltpu.VMEM)],
        out_specs=pl.BlockSpec(memory_space=pltpu.VMEM),
        out_shape=jax.ShapeDtypeStruct(part.shape, jnp.float32),
        scratch_shapes=[
            pltpu.VMEM((lon_devices,) + part.shape, jnp.float32),
            pltpu.VMEM((lat_devices,) + part.shape, jnp.float32),
            pltpu.SemaphoreType.DMA((lon_devices,)),
            pltpu.SemaphoreType.DMA((lon_devices,)),
            pltpu.SemaphoreType.DMA((lat_devices,)),
            pltpu.SemaphoreType.DMA((lat_devices,)),
        ],
        compiler_params=pltpu.CompilerParams(collective_id=0, has_side_effects=True),
    )(part)


def slots_of(block_owner, tile_count):
    targets = block_owner[:, 0]
    block_count = targets.shape[0]
    same_owner = (targets[:, None] == jnp.arange(tile_count, dtype=jnp.int32)[None, :]).astype(
        jnp.int32
    )
    order = jnp.arange(block_count, dtype=jnp.int32)
    lower = (order[:, None] > order[None, :]).astype(jnp.int32)
    earlier = jnp.dot(lower, same_owner)
    rank_within = jnp.sum(earlier * same_owner, axis=1)
    return targets * CAP + rank_within


def mix_blocks(values, correlation):
    return jnp.einsum("vsk,ik->vsi", values, correlation, precision=precise)


def shards(
    increment,
    residual,
    direction,
    diffusivity,
    deviation,
    stencil,
    bilinear,
    obs_weight,
    block_owner,
    correlation,
):
    lat_devices = lax.axis_size("lat")
    lon_devices = lax.axis_size("lon")
    tile_count = lat_devices * lon_devices
    both = widen_halo(jnp.stack([direction, diffusivity]), STEPS)
    coeffs = padded_coeffs(face_coeffs(both[1], STEPS))

    def apply_diffusion(field):
        return diffuse(widen_halo(field, STEPS), coeffs)

    slots = slots_of(block_owner, tile_count)
    slot_table = (slots[:, None] == jnp.arange(tile_count * CAP, dtype=jnp.int32)[None, :]).astype(
        jnp.float32
    )
    field_shape = direction.shape
    state_field = deviation * diffuse(both[0], coeffs)
    observed = observe_pallas(state_field, stencil, bilinear, obs_weight)
    buffer = jnp.einsum("vbk,bs->vsk", observed, slot_table, precision=precise)
    returned = lax.all_to_all(
        mix_blocks(
            lax.all_to_all(buffer, ("lat", "lon"), split_axis=1, concat_axis=1, tiled=True),
            correlation,
        ),
        ("lat", "lon"),
        split_axis=1,
        concat_axis=1,
        tiled=True,
    )
    weighted = obs_weight * jnp.einsum("vsk,bs->vbk", returned, slot_table, precision=precise)
    spread_field = deviation * spread_pallas(weighted, stencil, bilinear, field_shape)
    image_field = direction + apply_diffusion(spread_field)
    local_sums = jnp.stack(
        [
            jnp.sum(residual * residual),
            jnp.sum(direction * image_field),
            jnp.sum(residual * image_field),
            jnp.sum(image_field * image_field),
        ]
    )
    sums = allreduce_pallas(jnp.zeros((8, 128), jnp.float32).at[0, :4].set(local_sums))[0]
    norm_now, curvature, cross, image_norm = sums[0], sums[1], sums[2], sums[3]
    step_size = norm_now / curvature
    increment = increment + step_size * direction
    residual = residual - step_size * image_field
    norm_next = norm_now - 2.0 * step_size * cross + step_size * step_size * image_norm
    direction = residual + norm_next / norm_now * direction
    return (increment, residual, direction)


def solution(mesh):
    in_specs = (
        P(None, None, "lon", "lat"),
        P(None, None, "lon", "lat"),
        P(None, None, "lon", "lat"),
        P(None, None, "lon", "lat"),
        P(None, None, "lon", "lat"),
        P(("lat", "lon"), None),
        P(("lat", "lon"), None, None),
        P(None, ("lat", "lon"), None),
        P(("lat", "lon"), None),
        P(("lat", "lon"), None),
    )
    out_specs = (
        P(None, None, "lon", "lat"),
        P(None, None, "lon", "lat"),
        P(None, None, "lon", "lat"),
    )
    return jax.shard_map(shards, mesh=mesh, in_specs=in_specs, out_specs=out_specs, check_vma=False)
```

```python
import functools
import math

import jax
import jax.numpy as jnp
from jax import lax
from jax.experimental import pallas as pl
from jax.experimental.pallas import tpu as pltpu
from jax.sharding import PartitionSpec as P

STEPS = 4
CAP = 2


precise = lax.Precision.HIGHEST


def widen_halo(value, width):
    lat_dim, lon_dim = value.ndim - 1, value.ndim - 2
    for axis, dim, wrap in (("lat", lat_dim, False), ("lon", lon_dim, True)):
        size, length = lax.axis_size(axis), value.shape[dim]
        up = [(i, (i + 1) % size) for i in range(size if wrap else size - 1)]
        down = [(j, i) for i, j in up]
        before = lax.ppermute(lax.slice_in_dim(value, length - width, length, axis=dim), axis, up)
        after = lax.ppermute(lax.slice_in_dim(value, 0, width, axis=dim), axis, down)
        value = jnp.concatenate([before, value, after], axis=dim)
    return value


def face_coeffs(wide, width):
    lat_count = wide.shape[3] - 2 * width
    lanes = -(-wide.shape[3] // 128) * 128
    wide = jnp.pad(wide, ((0, 0), (0, 0), (1, 1), (1, 1 + lanes - wide.shape[3])))
    lat_devices = lax.axis_size("lat")
    first = lax.axis_index("lat") * lat_count - width
    cells = first + jnp.arange(lanes, dtype=jnp.int32)
    inside = ((cells >= 0) & (cells < lat_devices * lat_count)).astype(jnp.float32)
    centre = wide[:, :, 1:-1, 1:-1]
    return (
        inside * (0.5 * (centre + wide[:, :, 1:-1, 2:])),
        inside * (0.5 * (centre + wide[:, :, 1:-1, :-2])),
        inside * (0.5 * (centre + wide[:, :, 2:, 1:-1])),
        inside * (0.5 * (centre + wide[:, :, :-2, 1:-1])),
    )


def diffuse_kernel(steps, field_ref, north_ref, south_ref, east_ref, west_ref, out_ref):
    field = field_ref[...]
    rows, lanes = field.shape[1], field.shape[2]
    north, south, east, west = north_ref[...], south_ref[...], east_ref[...], west_ref[...]
    for sweep in range(steps):
        field = (
            field
            + north * (pltpu.roll(field, lanes - 1, 2) - field)
            + south * (pltpu.roll(field, 1, 2) - field)
            + east * (pltpu.roll(field, rows - 1, 1) - field)
            + west * (pltpu.roll(field, 1, 1) - field)
        )
    field = pltpu.roll(pltpu.roll(field, lanes - steps, 2), rows - steps, 1)
    out_ref[...] = field[:, : out_ref.shape[1], : out_ref.shape[2]]


def pad_lanes(value):
    planes, rows, lanes = value.shape
    return jnp.pad(value, ((0, 0), (0, 0), (0, -lanes % 128)))


def padded_coeffs(coeffs):
    return tuple(pad_lanes(c.reshape((-1,) + c.shape[-2:])) for c in coeffs)


def diffuse(field, coeffs, planes_per_step=50):
    lead = field.shape[:-2]
    flat = pad_lanes(field.reshape((-1,) + field.shape[-2:]))
    planes, rows, lanes = flat.shape
    lon_count, lat_count = rows - 2 * STEPS, field.shape[-1] - 2 * STEPS
    spec = pl.BlockSpec((planes_per_step, rows, lanes), lambda i: (i, 0, 0))
    out = pl.pallas_call(
        functools.partial(diffuse_kernel, STEPS),
        grid=(planes // planes_per_step,),
        in_specs=[spec] * 5,
        out_specs=pl.BlockSpec((planes_per_step, lon_count, lat_count), lambda i: (i, 0, 0)),
        out_shape=jax.ShapeDtypeStruct((planes, lon_count, lat_count), field.dtype),
        cost_estimate=pl.CostEstimate(
            flops=14 * STEPS * planes * rows * lanes, transcendentals=0, bytes_accessed=24 * planes * rows * lanes
        ),
    )(flat, *coeffs)
    return out.reshape(lead + (lon_count, lat_count))


PARTS = 2


def split_parts(value):
    parts = []
    rest = value
    for part in range(PARTS):
        piece = rest.astype(jnp.bfloat16)
        parts.append(piece)
        rest = rest - piece.astype(jnp.float32)
    return parts


def obs_lines(cell_ref, weight_ref, group, lat_count):
    cells = cell_ref[...]
    rows = cells // lat_count
    lats = cells - rows * lat_count
    row_line = jnp.concatenate([rows[g : g + 1, :] for g in range(group)], axis=1)
    lat_line = jnp.concatenate([lats[g : g + 1, :] for g in range(group)], axis=1)
    weights = [
        jnp.concatenate([weight_ref[g, c : c + 1, :] for g in range(group)], axis=1) for c in range(4)
    ]
    return row_line, lat_line, weights


def select_maps(row_line, lat_line, weights, row_count, lat_count):
    width = row_line.shape[1]
    row_ids = lax.broadcasted_iota(jnp.int32, (row_count, width), 0)
    near_rows = (row_ids == row_line).astype(jnp.bfloat16)
    lat_ids = lax.broadcasted_iota(jnp.int32, (lat_count, width), 0)
    at_first = lat_ids == lat_line
    at_second = lat_ids == lat_line + 1
    near_lat = jnp.where(at_first, weights[0], 0.0) + jnp.where(at_second, weights[1], 0.0)
    far_lat = jnp.where(at_first, weights[2], 0.0) + jnp.where(at_second, weights[3], 0.0)
    return near_rows, near_lat, far_lat


def observe_kernel(group, var_count, row_count, lat_count, table_ref, cell_ref, weight_ref, scale_ref, out_ref):
    row_line, lat_line, weights = obs_lines(cell_ref, weight_ref, group, lat_count)
    near_rows, near_lat, far_lat = select_maps(row_line, lat_line, weights, row_count, lat_count)
    table = jnp.concatenate(split_parts(table_ref[...]), axis=1)
    picked = jnp.dot(table, jnp.concatenate([near_rows] * PARTS, axis=0), preferred_element_type=jnp.float32)
    half = var_count * lat_count
    for v in range(var_count):
        near_span = slice(v * lat_count, (v + 1) * lat_count)
        far_span = slice(half + v * lat_count, half + (v + 1) * lat_count)
        line = jnp.sum(picked[near_span] * near_lat + picked[far_span] * far_lat, axis=0, keepdims=True)
        for g in range(group):
            out_ref[v, g : g + 1, :] = scale_ref[v, g : g + 1, :] * line[:, g * 128 : (g + 1) * 128]


def spread_kernel(group, var_count, row_count, lat_count, value_ref, cell_ref, weight_ref, out_ref, total_ref):
    step = pl.program_id(0)

    @pl.when(step == 0)
    def _():
        total_ref[...] = jnp.zeros_like(total_ref)

    row_line, lat_line, weights = obs_lines(cell_ref, weight_ref, group, lat_count)
    near_rows, near_lat, far_lat = select_maps(row_line, lat_line, weights, row_count, lat_count)
    near_parts, far_parts = [], []
    for v in range(var_count):
        line = jnp.concatenate([value_ref[v, g : g + 1, :] for g in range(group)], axis=1)
        near_parts.append(near_lat * line)
        far_parts.append(far_lat * line)
    rhs = jnp.concatenate(split_parts(jnp.concatenate(near_parts + far_parts, axis=0)), axis=1)
    lhs = jnp.concatenate([near_rows] * PARTS, axis=1)
    total_ref[...] += lax.dot_general(
        lhs, rhs, (((1,), (1,)), ((), ())), preferred_element_type=jnp.float32
    )

    @pl.when(step == pl.num_programs(0) - 1)
    def _():
        total = total_ref[...]
        half = var_count * lat_count
        summed = total[:, :half] + pltpu.roll(total[:, half:], 1, 0)
        for v in range(var_count):
            out_ref[v] = summed[:, v * lat_count : (v + 1) * lat_count]


def observe_pallas(field, stencil, bilinear, obs_weight, group=32):
    var_count, level_count, lon_count, lat_count = field.shape
    row_count = level_count * lon_count
    block_count = stencil.shape[0]
    rows_t = jnp.transpose(field.reshape(var_count, row_count, lat_count), (0, 2, 1))
    shifted = jnp.concatenate([rows_t[:, :, 1:], jnp.zeros_like(rows_t[:, :, :1])], axis=2)
    table = jnp.concatenate([rows_t, shifted], axis=0).reshape(2 * var_count * lat_count, row_count)
    kernel = functools.partial(observe_kernel, group, var_count, row_count, lat_count)
    width = group * stencil.shape[1]
    flops = 2 * 2 * var_count * lat_count * PARTS * row_count * width * (block_count // group)
    return pl.pallas_call(
        kernel,
        grid=(block_count // group,),
        in_specs=[
            pl.BlockSpec(table.shape, lambda i: (0, 0)),
            pl.BlockSpec((group, stencil.shape[1]), lambda i: (i, 0)),
            pl.BlockSpec((group, 4, stencil.shape[1]), lambda i: (i, 0, 0)),
            pl.BlockSpec((var_count, group, stencil.shape[1]), lambda i: (0, i, 0)),
        ],
        out_specs=pl.BlockSpec((var_count, group, stencil.shape[1]), lambda i: (0, i, 0)),
        out_shape=jax.ShapeDtypeStruct(obs_weight.shape, jnp.float32),
        cost_estimate=pl.CostEstimate(flops=flops, transcendentals=0, bytes_accessed=4 * 1024 * 1024),
    )(table, stencil, bilinear, obs_weight)


def spread_pallas(values, stencil, bilinear, field_shape, group=32):
    var_count, level_count, lon_count, lat_count = field_shape
    row_count = level_count * lon_count
    block_count = stencil.shape[0]
    kernel = functools.partial(spread_kernel, group, var_count, row_count, lat_count)
    width = group * stencil.shape[1]
    flops = 2 * 2 * var_count * lat_count * PARTS * row_count * width * (block_count // group)
    total = pl.pallas_call(
        kernel,
        grid=(block_count // group,),
        in_specs=[
            pl.BlockSpec((var_count, group, stencil.shape[1]), lambda i: (0, i, 0)),
            pl.BlockSpec((group, stencil.shape[1]), lambda i: (i, 0)),
            pl.BlockSpec((group, 4, stencil.shape[1]), lambda i: (i, 0, 0)),
        ],
        out_specs=pl.BlockSpec((var_count, row_count, lat_count), lambda i: (0, 0, 0)),
        out_shape=jax.ShapeDtypeStruct((var_count, row_count, lat_count), jnp.float32),
        scratch_shapes=[pltpu.VMEM((row_count, 2 * var_count * lat_count), jnp.float32)],
        cost_estimate=pl.CostEstimate(flops=flops, transcendentals=0, bytes_accessed=4 * 1024 * 1024),
    )(values, stencil, bilinear)
    return total.reshape(field_shape)


def allreduce_kernel(lat_devices, lon_devices, part_ref, out_ref, lon_buf, lat_buf, lon_send, lon_recv, lat_send, lat_recv):
    mesh_id = pl.DeviceIdType.MESH
    lat_me = lax.axis_index("lat")
    lon_me = lax.axis_index("lon")
    barrier = pltpu.get_barrier_semaphore()
    for peer in range(1, lon_devices):
        pl.semaphore_signal(barrier, inc=1, device_id=(lat_me, (lon_me + peer) % lon_devices), device_id_type=mesh_id)
    for peer in range(1, lat_devices):
        pl.semaphore_signal(barrier, inc=1, device_id=((lat_me + peer) % lat_devices, lon_me), device_id_type=mesh_id)
    pl.semaphore_wait(barrier, lon_devices + lat_devices - 2)

    def gather(buf, send, recv, count, me, target_of, source):
        copies = []
        for peer in range(1, count):
            target = (me + peer) % count
            copy = pltpu.make_async_remote_copy(
                src_ref=source,
                dst_ref=buf.at[me],
                send_sem=send.at[target],
                recv_sem=recv.at[me],
                device_id=target_of(target),
                device_id_type=mesh_id,
            )
            copy.start()
            copies.append((peer, copy))
        for peer, copy in copies:
            copy.wait_send()
        for peer in range(1, count):
            source_index = (me + count - peer) % count
            pltpu.make_async_remote_copy(
                src_ref=source,
                dst_ref=buf.at[source_index],
                send_sem=send.at[source_index],
                recv_sem=recv.at[source_index],
                device_id=target_of(source_index),
                device_id_type=mesh_id,
            ).wait_recv()

    gather(lon_buf, lon_send, lon_recv, lon_devices, lon_me, lambda t: (lat_me, t), part_ref)
    lon_buf[lon_me] = part_ref[...]
    total = lon_buf[0]
    for i in range(1, lon_devices):
        total = total + lon_buf[i]
    out_ref[...] = total
    gather(lat_buf, lat_send, lat_recv, lat_devices, lat_me, lambda t: (t, lon_me), out_ref)
    lat_buf[lat_me] = out_ref[...]
    total = lat_buf[0]
    for i in range(1, lat_devices):
        total = total + lat_buf[i]
    out_ref[...] = total


def allreduce_pallas(part):
    lat_devices = lax.axis_size("lat")
    lon_devices = lax.axis_size("lon")
    kernel = functools.partial(allreduce_kernel, lat_devices, lon_devices)
    return pl.pallas_call(
        kernel,
        in_specs=[pl.BlockSpec(memory_space=pltpu.VMEM)],
        out_specs=pl.BlockSpec(memory_space=pltpu.VMEM),
        out_shape=jax.ShapeDtypeStruct(part.shape, jnp.float32),
        scratch_shapes=[
            pltpu.VMEM((lon_devices,) + part.shape, jnp.float32),
            pltpu.VMEM((lat_devices,) + part.shape, jnp.float32),
            pltpu.SemaphoreType.DMA((lon_devices,)),
            pltpu.SemaphoreType.DMA((lon_devices,)),
            pltpu.SemaphoreType.DMA((lat_devices,)),
            pltpu.SemaphoreType.DMA((lat_devices,)),
        ],
        compiler_params=pltpu.CompilerParams(collective_id=0, has_side_effects=True),
    )(part)


def slots_of(block_owner, tile_count):
    targets = block_owner[:, 0]
    block_count = targets.shape[0]
    same_owner = (targets[:, None] == jnp.arange(tile_count, dtype=jnp.int32)[None, :]).astype(
        jnp.int32
    )
    order = jnp.arange(block_count, dtype=jnp.int32)
    lower = (order[:, None] > order[None, :]).astype(jnp.int32)
    earlier = jnp.dot(lower, same_owner)
    rank_within = jnp.sum(earlier * same_owner, axis=1)
    return targets * CAP + rank_within


def mix_blocks(values, correlation):
    return jnp.einsum("vsk,ik->vsi", values, correlation, precision=precise)


def shards(
    increment,
    residual,
    direction,
    diffusivity,
    deviation,
    stencil,
    bilinear,
    obs_weight,
    block_owner,
    correlation,
):
    lat_devices = lax.axis_size("lat")
    lon_devices = lax.axis_size("lon")
    tile_count = lat_devices * lon_devices
    both = widen_halo(jnp.stack([direction, diffusivity]), STEPS)
    coeffs = padded_coeffs(face_coeffs(both[1], STEPS))

    def apply_diffusion(field):
        return diffuse(widen_halo(field, STEPS), coeffs)

    slots = slots_of(block_owner, tile_count)
    slot_table = (slots[:, None] == jnp.arange(tile_count * CAP, dtype=jnp.int32)[None, :]).astype(
        jnp.float32
    )
    field_shape = direction.shape
    state_field = deviation * diffuse(both[0], coeffs)
    observed = observe_pallas(state_field, stencil, bilinear, obs_weight)
    buffer = jnp.einsum("vbk,bs->vsk", observed, slot_table, precision=precise)
    returned = lax.all_to_all(
        mix_blocks(
            lax.all_to_all(buffer, ("lat", "lon"), split_axis=1, concat_axis=1, tiled=True),
            correlation,
        ),
        ("lat", "lon"),
        split_axis=1,
        concat_axis=1,
        tiled=True,
    )
    weighted = obs_weight * jnp.einsum("vsk,bs->vbk", returned, slot_table, precision=precise)
    spread_field = deviation * spread_pallas(weighted, stencil, bilinear, field_shape)
    image_field = direction + apply_diffusion(spread_field)
    local_sums = jnp.stack(
        [
            jnp.sum(residual * residual),
            jnp.sum(direction * image_field),
            jnp.sum(residual * image_field),
            jnp.sum(image_field * image_field),
        ]
    )
    sums = allreduce_pallas(jnp.zeros((8, 128), jnp.float32).at[0, :4].set(local_sums))[0]
    norm_now, curvature, cross, image_norm = sums[0], sums[1], sums[2], sums[3]
    step_size = norm_now / curvature
    increment = increment + step_size * direction
    residual = residual - step_size * image_field
    norm_next = norm_now - 2.0 * step_size * cross + step_size * step_size * image_norm
    direction = residual + norm_next / norm_now * direction
    return (increment, residual, direction)


def solution(mesh):
    in_specs = (
        P(None, None, "lon", "lat"),
        P(None, None, "lon", "lat"),
        P(None, None, "lon", "lat"),
        P(None, None, "lon", "lat"),
        P(None, None, "lon", "lat"),
        P(("lat", "lon"), None),
        P(("lat", "lon"), None, None),
        P(None, ("lat", "lon"), None),
        P(("lat", "lon"), None),
        P(("lat", "lon"), None),
    )
    out_specs = (
        P(None, None, "lon", "lat"),
        P(None, None, "lon", "lat"),
        P(None, None, "lon", "lat"),
    )
    return jax.shard_map(shards, mesh=mesh, in_specs=in_specs, out_specs=out_specs, check_vma=False)
```

```python
import functools
import math

import jax
import jax.numpy as jnp
from jax import lax
from jax.experimental import pallas as pl
from jax.experimental.pallas import tpu as pltpu
from jax.sharding import PartitionSpec as P

STEPS = 4
CAP = 2


precise = lax.Precision.HIGHEST


def widen_halo(value, width):
    lat_dim, lon_dim = value.ndim - 1, value.ndim - 2
    for axis, dim, wrap in (("lat", lat_dim, False), ("lon", lon_dim, True)):
        size, length = lax.axis_size(axis), value.shape[dim]
        up = [(i, (i + 1) % size) for i in range(size if wrap else size - 1)]
        down = [(j, i) for i, j in up]
        before = lax.ppermute(lax.slice_in_dim(value, length - width, length, axis=dim), axis, up)
        after = lax.ppermute(lax.slice_in_dim(value, 0, width, axis=dim), axis, down)
        pieces = [before, value, after]
        spare = -(length + 2 * width) % 128
        if dim == lat_dim and spare:
            pieces.append(jnp.zeros(value.shape[:-1] + (spare,), value.dtype))
        value = jnp.concatenate(pieces, axis=dim)
    return value


def face_coeffs(wide, width, lat_count):
    lanes = -(-wide.shape[3] // 128) * 128
    wide = jnp.pad(wide, ((0, 0), (0, 0), (1, 1), (1, 1 + lanes - wide.shape[3])))
    lat_devices = lax.axis_size("lat")
    first = lax.axis_index("lat") * lat_count - width
    cells = first + jnp.arange(lanes, dtype=jnp.int32)
    inside = ((cells >= 0) & (cells < lat_devices * lat_count)).astype(jnp.float32)
    centre = wide[:, :, 1:-1, 1:-1]
    return (
        inside * (0.5 * (centre + wide[:, :, 1:-1, 2:])),
        inside * (0.5 * (centre + wide[:, :, 1:-1, :-2])),
        inside * (0.5 * (centre + wide[:, :, 2:, 1:-1])),
        inside * (0.5 * (centre + wide[:, :, :-2, 1:-1])),
    )


def diffuse_kernel(steps, field_ref, north_ref, south_ref, east_ref, west_ref, out_ref):
    field = field_ref[...]
    rows, lanes = field.shape[1], field.shape[2]
    north, south, east, west = north_ref[...], south_ref[...], east_ref[...], west_ref[...]
    for sweep in range(steps):
        field = (
            field
            + north * (pltpu.roll(field, lanes - 1, 2) - field)
            + south * (pltpu.roll(field, 1, 2) - field)
            + east * (pltpu.roll(field, rows - 1, 1) - field)
            + west * (pltpu.roll(field, 1, 1) - field)
        )
    field = pltpu.roll(pltpu.roll(field, lanes - steps, 2), rows - steps, 1)
    out_ref[...] = field[:, : out_ref.shape[1], : out_ref.shape[2]]


def pad_lanes(value):
    planes, rows, lanes = value.shape
    return jnp.pad(value, ((0, 0), (0, 0), (0, -lanes % 128)))


def padded_coeffs(coeffs):
    return tuple(pad_lanes(c.reshape((-1,) + c.shape[-2:])) for c in coeffs)


def diffuse(field, coeffs, lat_count, planes_per_step=50):
    lead = field.shape[:-2]
    flat = pad_lanes(field.reshape((-1,) + field.shape[-2:]))
    planes, rows, lanes = flat.shape
    lon_count = rows - 2 * STEPS
    spec = pl.BlockSpec((planes_per_step, rows, lanes), lambda i: (i, 0, 0))
    out = pl.pallas_call(
        functools.partial(diffuse_kernel, STEPS),
        grid=(planes // planes_per_step,),
        in_specs=[spec] * 5,
        out_specs=pl.BlockSpec((planes_per_step, lon_count, lat_count), lambda i: (i, 0, 0)),
        out_shape=jax.ShapeDtypeStruct((planes, lon_count, lat_count), field.dtype),
        cost_estimate=pl.CostEstimate(
            flops=14 * STEPS * planes * rows * lanes, transcendentals=0, bytes_accessed=24 * planes * rows * lanes
        ),
    )(flat, *coeffs)
    return out.reshape(lead + (lon_count, lat_count))


PARTS = 2


def split_parts(value):
    parts = []
    rest = value
    for part in range(PARTS):
        piece = rest.astype(jnp.bfloat16)
        parts.append(piece)
        rest = rest - piece.astype(jnp.float32)
    return parts


def obs_lines(cell_ref, weight_ref, group, lat_count):
    cells = cell_ref[...]
    rows = cells // lat_count
    lats = cells - rows * lat_count
    row_line = jnp.concatenate([rows[g : g + 1, :] for g in range(group)], axis=1)
    lat_line = jnp.concatenate([lats[g : g + 1, :] for g in range(group)], axis=1)
    weights = [
        jnp.concatenate([weight_ref[g, c : c + 1, :] for g in range(group)], axis=1) for c in range(4)
    ]
    return row_line, lat_line, weights


def select_maps(row_line, lat_line, weights, row_count, lat_count):
    width = row_line.shape[1]
    row_ids = lax.broadcasted_iota(jnp.int32, (row_count, width), 0)
    near_rows = (row_ids == row_line).astype(jnp.bfloat16)
    lat_ids = lax.broadcasted_iota(jnp.int32, (lat_count, width), 0)
    at_first = lat_ids == lat_line
    at_second = lat_ids == lat_line + 1
    near_lat = jnp.where(at_first, weights[0], 0.0) + jnp.where(at_second, weights[1], 0.0)
    far_lat = jnp.where(at_first, weights[2], 0.0) + jnp.where(at_second, weights[3], 0.0)
    return near_rows, near_lat, far_lat


def observe_kernel(group, var_count, row_count, lat_count, table_ref, cell_ref, weight_ref, scale_ref, out_ref):
    row_line, lat_line, weights = obs_lines(cell_ref, weight_ref, group, lat_count)
    near_rows, near_lat, far_lat = select_maps(row_line, lat_line, weights, row_count, lat_count)
    table = jnp.concatenate(split_parts(table_ref[...]), axis=1)
    picked = jnp.dot(table, jnp.concatenate([near_rows] * PARTS, axis=0), preferred_element_type=jnp.float32)
    half = var_count * lat_count
    for v in range(var_count):
        near_span = slice(v * lat_count, (v + 1) * lat_count)
        far_span = slice(half + v * lat_count, half + (v + 1) * lat_count)
        line = jnp.sum(picked[near_span] * near_lat + picked[far_span] * far_lat, axis=0, keepdims=True)
        for g in range(group):
            out_ref[v, g : g + 1, :] = scale_ref[v, g : g + 1, :] * line[:, g * 128 : (g + 1) * 128]


def spread_kernel(group, var_count, row_count, lat_count, value_ref, cell_ref, weight_ref, out_ref, total_ref):
    step = pl.program_id(0)

    @pl.when(step == 0)
    def _():
        total_ref[...] = jnp.zeros_like(total_ref)

    row_line, lat_line, weights = obs_lines(cell_ref, weight_ref, group, lat_count)
    near_rows, near_lat, far_lat = select_maps(row_line, lat_line, weights, row_count, lat_count)
    near_parts, far_parts = [], []
    for v in range(var_count):
        line = jnp.concatenate([value_ref[v, g : g + 1, :] for g in range(group)], axis=1)
        near_parts.append(near_lat * line)
        far_parts.append(far_lat * line)
    rhs = jnp.concatenate(split_parts(jnp.concatenate(near_parts + far_parts, axis=0)), axis=1)
    lhs = jnp.concatenate([near_rows] * PARTS, axis=1)
    total_ref[...] += lax.dot_general(
        lhs, rhs, (((1,), (1,)), ((), ())), preferred_element_type=jnp.float32
    )

    @pl.when(step == pl.num_programs(0) - 1)
    def _():
        total = total_ref[...]
        half = var_count * lat_count
        summed = total[:, :half] + pltpu.roll(total[:, half:], 1, 0)
        for v in range(var_count):
            out_ref[v] = summed[:, v * lat_count : (v + 1) * lat_count]


def observe_pallas(field, stencil, bilinear, obs_weight, group=32):
    var_count, level_count, lon_count, lat_count = field.shape
    row_count = level_count * lon_count
    block_count = stencil.shape[0]
    rows_t = jnp.transpose(field.reshape(var_count, row_count, lat_count), (0, 2, 1))
    shifted = jnp.concatenate([rows_t[:, :, 1:], jnp.zeros_like(rows_t[:, :, :1])], axis=2)
    table = jnp.concatenate([rows_t, shifted], axis=0).reshape(2 * var_count * lat_count, row_count)
    kernel = functools.partial(observe_kernel, group, var_count, row_count, lat_count)
    width = group * stencil.shape[1]
    flops = 2 * 2 * var_count * lat_count * PARTS * row_count * width * (block_count // group)
    return pl.pallas_call(
        kernel,
        grid=(block_count // group,),
        in_specs=[
            pl.BlockSpec(table.shape, lambda i: (0, 0)),
            pl.BlockSpec((group, stencil.shape[1]), lambda i: (i, 0)),
            pl.BlockSpec((group, 4, stencil.shape[1]), lambda i: (i, 0, 0)),
            pl.BlockSpec((var_count, group, stencil.shape[1]), lambda i: (0, i, 0)),
        ],
        out_specs=pl.BlockSpec((var_count, group, stencil.shape[1]), lambda i: (0, i, 0)),
        out_shape=jax.ShapeDtypeStruct(obs_weight.shape, jnp.float32),
        cost_estimate=pl.CostEstimate(flops=flops, transcendentals=0, bytes_accessed=4 * 1024 * 1024),
    )(table, stencil, bilinear, obs_weight)


def spread_pallas(values, stencil, bilinear, field_shape, group=32):
    var_count, level_count, lon_count, lat_count = field_shape
    row_count = level_count * lon_count
    block_count = stencil.shape[0]
    kernel = functools.partial(spread_kernel, group, var_count, row_count, lat_count)
    width = group * stencil.shape[1]
    flops = 2 * 2 * var_count * lat_count * PARTS * row_count * width * (block_count // group)
    total = pl.pallas_call(
        kernel,
        grid=(block_count // group,),
        in_specs=[
            pl.BlockSpec((var_count, group, stencil.shape[1]), lambda i: (0, i, 0)),
            pl.BlockSpec((group, stencil.shape[1]), lambda i: (i, 0)),
            pl.BlockSpec((group, 4, stencil.shape[1]), lambda i: (i, 0, 0)),
        ],
        out_specs=pl.BlockSpec((var_count, row_count, lat_count), lambda i: (0, 0, 0)),
        out_shape=jax.ShapeDtypeStruct((var_count, row_count, lat_count), jnp.float32),
        scratch_shapes=[pltpu.VMEM((row_count, 2 * var_count * lat_count), jnp.float32)],
        cost_estimate=pl.CostEstimate(flops=flops, transcendentals=0, bytes_accessed=4 * 1024 * 1024),
    )(values, stencil, bilinear)
    return total.reshape(field_shape)


def allreduce_kernel(lat_devices, lon_devices, part_ref, out_ref, lon_buf, lat_buf, lon_send, lon_recv, lat_send, lat_recv):
    mesh_id = pl.DeviceIdType.MESH
    lat_me = lax.axis_index("lat")
    lon_me = lax.axis_index("lon")
    barrier = pltpu.get_barrier_semaphore()
    for peer in range(1, lon_devices):
        pl.semaphore_signal(barrier, inc=1, device_id=(lat_me, (lon_me + peer) % lon_devices), device_id_type=mesh_id)
    for peer in range(1, lat_devices):
        pl.semaphore_signal(barrier, inc=1, device_id=((lat_me + peer) % lat_devices, lon_me), device_id_type=mesh_id)
    pl.semaphore_wait(barrier, lon_devices + lat_devices - 2)

    def gather(buf, send, recv, count, me, target_of, source):
        copies = []
        for peer in range(1, count):
            target = (me + peer) % count
            copy = pltpu.make_async_remote_copy(
                src_ref=source,
                dst_ref=buf.at[me],
                send_sem=send.at[target],
                recv_sem=recv.at[me],
                device_id=target_of(target),
                device_id_type=mesh_id,
            )
            copy.start()
            copies.append((peer, copy))
        for peer, copy in copies:
            copy.wait_send()
        for peer in range(1, count):
            source_index = (me + count - peer) % count
            pltpu.make_async_remote_copy(
                src_ref=source,
                dst_ref=buf.at[source_index],
                send_sem=send.at[source_index],
                recv_sem=recv.at[source_index],
                device_id=target_of(source_index),
                device_id_type=mesh_id,
            ).wait_recv()

    gather(lon_buf, lon_send, lon_recv, lon_devices, lon_me, lambda t: (lat_me, t), part_ref)
    lon_buf[lon_me] = part_ref[...]
    total = lon_buf[0]
    for i in range(1, lon_devices):
        total = total + lon_buf[i]
    out_ref[...] = total
    gather(lat_buf, lat_send, lat_recv, lat_devices, lat_me, lambda t: (t, lon_me), out_ref)
    lat_buf[lat_me] = out_ref[...]
    total = lat_buf[0]
    for i in range(1, lat_devices):
        total = total + lat_buf[i]
    out_ref[...] = total


def allreduce_pallas(part):
    lat_devices = lax.axis_size("lat")
    lon_devices = lax.axis_size("lon")
    kernel = functools.partial(allreduce_kernel, lat_devices, lon_devices)
    return pl.pallas_call(
        kernel,
        in_specs=[pl.BlockSpec(memory_space=pltpu.VMEM)],
        out_specs=pl.BlockSpec(memory_space=pltpu.VMEM),
        out_shape=jax.ShapeDtypeStruct(part.shape, jnp.float32),
        scratch_shapes=[
            pltpu.VMEM((lon_devices,) + part.shape, jnp.float32),
            pltpu.VMEM((lat_devices,) + part.shape, jnp.float32),
            pltpu.SemaphoreType.DMA((lon_devices,)),
            pltpu.SemaphoreType.DMA((lon_devices,)),
            pltpu.SemaphoreType.DMA((lat_devices,)),
            pltpu.SemaphoreType.DMA((lat_devices,)),
        ],
        compiler_params=pltpu.CompilerParams(collective_id=0, has_side_effects=True),
    )(part)


def slots_of(block_owner, tile_count):
    targets = block_owner[:, 0]
    block_count = targets.shape[0]
    same_owner = (targets[:, None] == jnp.arange(tile_count, dtype=jnp.int32)[None, :]).astype(
        jnp.int32
    )
    order = jnp.arange(block_count, dtype=jnp.int32)
    lower = (order[:, None] > order[None, :]).astype(jnp.int32)
    earlier = jnp.dot(lower, same_owner)
    rank_within = jnp.sum(earlier * same_owner, axis=1)
    return targets * CAP + rank_within


def mix_blocks(values, correlation):
    return jnp.einsum("vsk,ik->vsi", values, correlation, precision=precise)


def shards(
    increment,
    residual,
    direction,
    diffusivity,
    deviation,
    stencil,
    bilinear,
    obs_weight,
    block_owner,
    correlation,
):
    lat_devices = lax.axis_size("lat")
    lon_devices = lax.axis_size("lon")
    tile_count = lat_devices * lon_devices
    both = widen_halo(jnp.stack([direction, diffusivity]), STEPS)
    coeffs = padded_coeffs(face_coeffs(both[1], STEPS, direction.shape[3]))

    def apply_diffusion(field):
        return diffuse(widen_halo(field, STEPS), coeffs, field.shape[3])

    slots = slots_of(block_owner, tile_count)
    slot_table = (slots[:, None] == jnp.arange(tile_count * CAP, dtype=jnp.int32)[None, :]).astype(
        jnp.float32
    )
    field_shape = direction.shape
    state_field = deviation * diffuse(both[0], coeffs, direction.shape[3])
    observed = observe_pallas(state_field, stencil, bilinear, obs_weight)
    buffer = jnp.einsum("vbk,bs->vsk", observed, slot_table, precision=precise)
    returned = lax.all_to_all(
        mix_blocks(
            lax.all_to_all(buffer, ("lat", "lon"), split_axis=1, concat_axis=1, tiled=True),
            correlation,
        ),
        ("lat", "lon"),
        split_axis=1,
        concat_axis=1,
        tiled=True,
    )
    weighted = obs_weight * jnp.einsum("vsk,bs->vbk", returned, slot_table, precision=precise)
    spread_field = deviation * spread_pallas(weighted, stencil, bilinear, field_shape)
    image_field = direction + apply_diffusion(spread_field)
    local_sums = jnp.stack(
        [
            jnp.sum(residual * residual),
            jnp.sum(direction * image_field),
            jnp.sum(residual * image_field),
            jnp.sum(image_field * image_field),
        ]
    )
    sums = allreduce_pallas(jnp.zeros((8, 128), jnp.float32).at[0, :4].set(local_sums))[0]
    norm_now, curvature, cross, image_norm = sums[0], sums[1], sums[2], sums[3]
    step_size = norm_now / curvature
    increment = increment + step_size * direction
    residual = residual - step_size * image_field
    norm_next = norm_now - 2.0 * step_size * cross + step_size * step_size * image_norm
    direction = residual + norm_next / norm_now * direction
    return (increment, residual, direction)


def solution(mesh):
    in_specs = (
        P(None, None, "lon", "lat"),
        P(None, None, "lon", "lat"),
        P(None, None, "lon", "lat"),
        P(None, None, "lon", "lat"),
        P(None, None, "lon", "lat"),
        P(("lat", "lon"), None),
        P(("lat", "lon"), None, None),
        P(None, ("lat", "lon"), None),
        P(("lat", "lon"), None),
        P(("lat", "lon"), None),
    )
    out_specs = (
        P(None, None, "lon", "lat"),
        P(None, None, "lon", "lat"),
        P(None, None, "lon", "lat"),
    )
    return jax.shard_map(shards, mesh=mesh, in_specs=in_specs, out_specs=out_specs, check_vma=False)
```

```python
import functools
import math

import jax
import jax.numpy as jnp
from jax import lax
from jax.experimental import pallas as pl
from jax.experimental.pallas import tpu as pltpu
from jax.sharding import PartitionSpec as P

STEPS = 4
CAP = 2


precise = lax.Precision.HIGHEST


def widen_halo(value, width):
    lat_dim, lon_dim = value.ndim - 1, value.ndim - 2
    for axis, dim, wrap in (("lat", lat_dim, False), ("lon", lon_dim, True)):
        size, length = lax.axis_size(axis), value.shape[dim]
        up = [(i, (i + 1) % size) for i in range(size if wrap else size - 1)]
        down = [(j, i) for i, j in up]
        before = lax.ppermute(lax.slice_in_dim(value, length - width, length, axis=dim), axis, up)
        after = lax.ppermute(lax.slice_in_dim(value, 0, width, axis=dim), axis, down)
        value = jnp.concatenate([before, value, after], axis=dim)
    return value


def face_coeffs(wide, width):
    lat_count = wide.shape[3] - 2 * width
    lanes = -(-wide.shape[3] // 128) * 128
    wide = jnp.pad(wide, ((0, 0), (0, 0), (1, 1), (1, 1 + lanes - wide.shape[3])))
    lat_devices = lax.axis_size("lat")
    first = lax.axis_index("lat") * lat_count - width
    cells = first + jnp.arange(lanes, dtype=jnp.int32)
    inside = ((cells >= 0) & (cells < lat_devices * lat_count)).astype(jnp.float32)
    centre = wide[:, :, 1:-1, 1:-1]
    return (
        inside * (0.5 * (centre + wide[:, :, 1:-1, 2:])),
        inside * (0.5 * (centre + wide[:, :, 1:-1, :-2])),
        inside * (0.5 * (centre + wide[:, :, 2:, 1:-1])),
        inside * (0.5 * (centre + wide[:, :, :-2, 1:-1])),
    )


def diffuse_kernel(steps, field_ref, north_ref, south_ref, east_ref, west_ref, out_ref):
    field = field_ref[...]
    rows, lanes = field.shape[1], field.shape[2]
    north, south, east, west = north_ref[...], south_ref[...], east_ref[...], west_ref[...]
    for sweep in range(steps):
        field = (
            field
            + north * (pltpu.roll(field, lanes - 1, 2) - field)
            + south * (pltpu.roll(field, 1, 2) - field)
            + east * (pltpu.roll(field, rows - 1, 1) - field)
            + west * (pltpu.roll(field, 1, 1) - field)
        )
    field = pltpu.roll(pltpu.roll(field, lanes - steps, 2), rows - steps, 1)
    out_ref[...] = field[:, : out_ref.shape[1], : out_ref.shape[2]]


def pad_lanes(value):
    planes, rows, lanes = value.shape
    return jnp.pad(value, ((0, 0), (0, 0), (0, -lanes % 128)))


def padded_coeffs(coeffs):
    return tuple(pad_lanes(c.reshape((-1,) + c.shape[-2:])) for c in coeffs)


def diffuse(field, coeffs, planes_per_step=25):
    lead = field.shape[:-2]
    flat = pad_lanes(field.reshape((-1,) + field.shape[-2:]))
    planes, rows, lanes = flat.shape
    lon_count, lat_count = rows - 2 * STEPS, field.shape[-1] - 2 * STEPS
    spec = pl.BlockSpec((planes_per_step, rows, lanes), lambda i: (i, 0, 0))
    out = pl.pallas_call(
        functools.partial(diffuse_kernel, STEPS),
        grid=(planes // planes_per_step,),
        in_specs=[spec] * 5,
        out_specs=pl.BlockSpec((planes_per_step, lon_count, lat_count), lambda i: (i, 0, 0)),
        out_shape=jax.ShapeDtypeStruct((planes, lon_count, lat_count), field.dtype),
        cost_estimate=pl.CostEstimate(
            flops=14 * STEPS * planes * rows * lanes, transcendentals=0, bytes_accessed=24 * planes * rows * lanes
        ),
    )(flat, *coeffs)
    return out.reshape(lead + (lon_count, lat_count))


PARTS = 2


def split_parts(value):
    parts = []
    rest = value
    for part in range(PARTS):
        piece = rest.astype(jnp.bfloat16)
        parts.append(piece)
        rest = rest - piece.astype(jnp.float32)
    return parts


def obs_lines(cell_ref, weight_ref, group, lat_count):
    cells = cell_ref[...]
    rows = cells // lat_count
    lats = cells - rows * lat_count
    row_line = jnp.concatenate([rows[g : g + 1, :] for g in range(group)], axis=1)
    lat_line = jnp.concatenate([lats[g : g + 1, :] for g in range(group)], axis=1)
    weights = [
        jnp.concatenate([weight_ref[g, c : c + 1, :] for g in range(group)], axis=1) for c in range(4)
    ]
    return row_line, lat_line, weights


def select_maps(row_line, lat_line, weights, row_count, lat_count):
    width = row_line.shape[1]
    row_ids = lax.broadcasted_iota(jnp.int32, (row_count, width), 0)
    near_rows = (row_ids == row_line).astype(jnp.bfloat16)
    lat_ids = lax.broadcasted_iota(jnp.int32, (lat_count, width), 0)
    at_first = lat_ids == lat_line
    at_second = lat_ids == lat_line + 1
    near_lat = jnp.where(at_first, weights[0], 0.0) + jnp.where(at_second, weights[1], 0.0)
    far_lat = jnp.where(at_first, weights[2], 0.0) + jnp.where(at_second, weights[3], 0.0)
    return near_rows, near_lat, far_lat


def observe_kernel(group, var_count, row_count, lat_count, table_ref, cell_ref, weight_ref, scale_ref, out_ref):
    row_line, lat_line, weights = obs_lines(cell_ref, weight_ref, group, lat_count)
    near_rows, near_lat, far_lat = select_maps(row_line, lat_line, weights, row_count, lat_count)
    table = jnp.concatenate(split_parts(table_ref[...]), axis=1)
    picked = jnp.dot(table, jnp.concatenate([near_rows] * PARTS, axis=0), preferred_element_type=jnp.float32)
    half = var_count * lat_count
    for v in range(var_count):
        near_span = slice(v * lat_count, (v + 1) * lat_count)
        far_span = slice(half + v * lat_count, half + (v + 1) * lat_count)
        line = jnp.sum(picked[near_span] * near_lat + picked[far_span] * far_lat, axis=0, keepdims=True)
        for g in range(group):
            out_ref[v, g : g + 1, :] = scale_ref[v, g : g + 1, :] * line[:, g * 128 : (g + 1) * 128]


def spread_kernel(group, var_count, row_count, lat_count, value_ref, cell_ref, weight_ref, out_ref, total_ref):
    step = pl.program_id(0)

    @pl.when(step == 0)
    def _():
        total_ref[...] = jnp.zeros_like(total_ref)

    row_line, lat_line, weights = obs_lines(cell_ref, weight_ref, group, lat_count)
    near_rows, near_lat, far_lat = select_maps(row_line, lat_line, weights, row_count, lat_count)
    near_parts, far_parts = [], []
    for v in range(var_count):
        line = jnp.concatenate([value_ref[v, g : g + 1, :] for g in range(group)], axis=1)
        near_parts.append(near_lat * line)
        far_parts.append(far_lat * line)
    rhs = jnp.concatenate(split_parts(jnp.concatenate(near_parts + far_parts, axis=0)), axis=1)
    lhs = jnp.concatenate([near_rows] * PARTS, axis=1)
    total_ref[...] += lax.dot_general(
        lhs, rhs, (((1,), (1,)), ((), ())), preferred_element_type=jnp.float32
    )

    @pl.when(step == pl.num_programs(0) - 1)
    def _():
        total = total_ref[...]
        half = var_count * lat_count
        summed = total[:, :half] + pltpu.roll(total[:, half:], 1, 0)
        for v in range(var_count):
            out_ref[v] = summed[:, v * lat_count : (v + 1) * lat_count]


def observe_pallas(field, stencil, bilinear, obs_weight, group=32):
    var_count, level_count, lon_count, lat_count = field.shape
    row_count = level_count * lon_count
    block_count = stencil.shape[0]
    rows_t = jnp.transpose(field.reshape(var_count, row_count, lat_count), (0, 2, 1))
    shifted = jnp.concatenate([rows_t[:, :, 1:], jnp.zeros_like(rows_t[:, :, :1])], axis=2)
    table = jnp.concatenate([rows_t, shifted], axis=0).reshape(2 * var_count * lat_count, row_count)
    kernel = functools.partial(observe_kernel, group, var_count, row_count, lat_count)
    width = group * stencil.shape[1]
    flops = 2 * 2 * var_count * lat_count * PARTS * row_count * width * (block_count // group)
    return pl.pallas_call(
        kernel,
        grid=(block_count // group,),
        in_specs=[
            pl.BlockSpec(table.shape, lambda i: (0, 0)),
            pl.BlockSpec((group, stencil.shape[1]), lambda i: (i, 0)),
            pl.BlockSpec((group, 4, stencil.shape[1]), lambda i: (i, 0, 0)),
            pl.BlockSpec((var_count, group, stencil.shape[1]), lambda i: (0, i, 0)),
        ],
        out_specs=pl.BlockSpec((var_count, group, stencil.shape[1]), lambda i: (0, i, 0)),
        out_shape=jax.ShapeDtypeStruct(obs_weight.shape, jnp.float32),
        cost_estimate=pl.CostEstimate(flops=flops, transcendentals=0, bytes_accessed=4 * 1024 * 1024),
    )(table, stencil, bilinear, obs_weight)


def spread_pallas(values, stencil, bilinear, field_shape, group=32):
    var_count, level_count, lon_count, lat_count = field_shape
    row_count = level_count * lon_count
    block_count = stencil.shape[0]
    kernel = functools.partial(spread_kernel, group, var_count, row_count, lat_count)
    width = group * stencil.shape[1]
    flops = 2 * 2 * var_count * lat_count * PARTS * row_count * width * (block_count // group)
    total = pl.pallas_call(
        kernel,
        grid=(block_count // group,),
        in_specs=[
            pl.BlockSpec((var_count, group, stencil.shape[1]), lambda i: (0, i, 0)),
            pl.BlockSpec((group, stencil.shape[1]), lambda i: (i, 0)),
            pl.BlockSpec((group, 4, stencil.shape[1]), lambda i: (i, 0, 0)),
        ],
        out_specs=pl.BlockSpec((var_count, row_count, lat_count), lambda i: (0, 0, 0)),
        out_shape=jax.ShapeDtypeStruct((var_count, row_count, lat_count), jnp.float32),
        scratch_shapes=[pltpu.VMEM((row_count, 2 * var_count * lat_count), jnp.float32)],
        cost_estimate=pl.CostEstimate(flops=flops, transcendentals=0, bytes_accessed=4 * 1024 * 1024),
    )(values, stencil, bilinear)
    return total.reshape(field_shape)


def allreduce_kernel(lat_devices, lon_devices, part_ref, out_ref, lon_buf, lat_buf, lon_send, lon_recv, lat_send, lat_recv):
    mesh_id = pl.DeviceIdType.MESH
    lat_me = lax.axis_index("lat")
    lon_me = lax.axis_index("lon")
    barrier = pltpu.get_barrier_semaphore()
    for peer in range(1, lon_devices):
        pl.semaphore_signal(barrier, inc=1, device_id=(lat_me, (lon_me + peer) % lon_devices), device_id_type=mesh_id)
    for peer in range(1, lat_devices):
        pl.semaphore_signal(barrier, inc=1, device_id=((lat_me + peer) % lat_devices, lon_me), device_id_type=mesh_id)
    pl.semaphore_wait(barrier, lon_devices + lat_devices - 2)

    def gather(buf, send, recv, count, me, target_of, source):
        copies = []
        for peer in range(1, count):
            target = (me + peer) % count
            copy = pltpu.make_async_remote_copy(
                src_ref=source,
                dst_ref=buf.at[me],
                send_sem=send.at[target],
                recv_sem=recv.at[me],
                device_id=target_of(target),
                device_id_type=mesh_id,
            )
            copy.start()
            copies.append((peer, copy))
        for peer, copy in copies:
            copy.wait_send()
        for peer in range(1, count):
            source_index = (me + count - peer) % count
            pltpu.make_async_remote_copy(
                src_ref=source,
                dst_ref=buf.at[source_index],
                send_sem=send.at[source_index],
                recv_sem=recv.at[source_index],
                device_id=target_of(source_index),
                device_id_type=mesh_id,
            ).wait_recv()

    gather(lon_buf, lon_send, lon_recv, lon_devices, lon_me, lambda t: (lat_me, t), part_ref)
    lon_buf[lon_me] = part_ref[...]
    total = lon_buf[0]
    for i in range(1, lon_devices):
        total = total + lon_buf[i]
    out_ref[...] = total
    gather(lat_buf, lat_send, lat_recv, lat_devices, lat_me, lambda t: (t, lon_me), out_ref)
    lat_buf[lat_me] = out_ref[...]
    total = lat_buf[0]
    for i in range(1, lat_devices):
        total = total + lat_buf[i]
    out_ref[...] = total


def allreduce_pallas(part):
    lat_devices = lax.axis_size("lat")
    lon_devices = lax.axis_size("lon")
    kernel = functools.partial(allreduce_kernel, lat_devices, lon_devices)
    return pl.pallas_call(
        kernel,
        in_specs=[pl.BlockSpec(memory_space=pltpu.VMEM)],
        out_specs=pl.BlockSpec(memory_space=pltpu.VMEM),
        out_shape=jax.ShapeDtypeStruct(part.shape, jnp.float32),
        scratch_shapes=[
            pltpu.VMEM((lon_devices,) + part.shape, jnp.float32),
            pltpu.VMEM((lat_devices,) + part.shape, jnp.float32),
            pltpu.SemaphoreType.DMA((lon_devices,)),
            pltpu.SemaphoreType.DMA((lon_devices,)),
            pltpu.SemaphoreType.DMA((lat_devices,)),
            pltpu.SemaphoreType.DMA((lat_devices,)),
        ],
        compiler_params=pltpu.CompilerParams(collective_id=0, has_side_effects=True),
    )(part)


def slots_of(block_owner, tile_count):
    targets = block_owner[:, 0]
    block_count = targets.shape[0]
    same_owner = (targets[:, None] == jnp.arange(tile_count, dtype=jnp.int32)[None, :]).astype(
        jnp.int32
    )
    order = jnp.arange(block_count, dtype=jnp.int32)
    lower = (order[:, None] > order[None, :]).astype(jnp.int32)
    earlier = jnp.dot(lower, same_owner)
    rank_within = jnp.sum(earlier * same_owner, axis=1)
    return targets * CAP + rank_within


def mix_blocks(values, correlation):
    return jnp.einsum("vsk,ik->vsi", values, correlation, precision=precise)


def shards(
    increment,
    residual,
    direction,
    diffusivity,
    deviation,
    stencil,
    bilinear,
    obs_weight,
    block_owner,
    correlation,
):
    lat_devices = lax.axis_size("lat")
    lon_devices = lax.axis_size("lon")
    tile_count = lat_devices * lon_devices
    both = widen_halo(jnp.stack([direction, diffusivity]), STEPS)
    coeffs = padded_coeffs(face_coeffs(both[1], STEPS))

    def apply_diffusion(field):
        return diffuse(widen_halo(field, STEPS), coeffs)

    slots = slots_of(block_owner, tile_count)
    slot_table = (slots[:, None] == jnp.arange(tile_count * CAP, dtype=jnp.int32)[None, :]).astype(
        jnp.float32
    )
    field_shape = direction.shape
    state_field = deviation * diffuse(both[0], coeffs)
    observed = observe_pallas(state_field, stencil, bilinear, obs_weight)
    buffer = jnp.einsum("vbk,bs->vsk", observed, slot_table, precision=precise)
    returned = lax.all_to_all(
        mix_blocks(
            lax.all_to_all(buffer, ("lat", "lon"), split_axis=1, concat_axis=1, tiled=True),
            correlation,
        ),
        ("lat", "lon"),
        split_axis=1,
        concat_axis=1,
        tiled=True,
    )
    weighted = obs_weight * jnp.einsum("vsk,bs->vbk", returned, slot_table, precision=precise)
    spread_field = deviation * spread_pallas(weighted, stencil, bilinear, field_shape)
    image_field = direction + apply_diffusion(spread_field)
    local_sums = jnp.stack(
        [
            jnp.sum(residual * residual),
            jnp.sum(direction * image_field),
            jnp.sum(residual * image_field),
            jnp.sum(image_field * image_field),
        ]
    )
    sums = allreduce_pallas(jnp.zeros((8, 128), jnp.float32).at[0, :4].set(local_sums))[0]
    norm_now, curvature, cross, image_norm = sums[0], sums[1], sums[2], sums[3]
    step_size = norm_now / curvature
    increment = increment + step_size * direction
    residual = residual - step_size * image_field
    norm_next = norm_now - 2.0 * step_size * cross + step_size * step_size * image_norm
    direction = residual + norm_next / norm_now * direction
    return (increment, residual, direction)


def solution(mesh):
    in_specs = (
        P(None, None, "lon", "lat"),
        P(None, None, "lon", "lat"),
        P(None, None, "lon", "lat"),
        P(None, None, "lon", "lat"),
        P(None, None, "lon", "lat"),
        P(("lat", "lon"), None),
        P(("lat", "lon"), None, None),
        P(None, ("lat", "lon"), None),
        P(("lat", "lon"), None),
        P(("lat", "lon"), None),
    )
    out_specs = (
        P(None, None, "lon", "lat"),
        P(None, None, "lon", "lat"),
        P(None, None, "lon", "lat"),
    )
    return jax.shard_map(shards, mesh=mesh, in_specs=in_specs, out_specs=out_specs, check_vma=False)
```

```python
import functools
import math

import jax
import jax.numpy as jnp
from jax import lax
from jax.experimental import pallas as pl
from jax.experimental.pallas import tpu as pltpu
from jax.sharding import PartitionSpec as P

STEPS = 4
CAP = 2


precise = lax.Precision.HIGHEST


def widen_halo(value, width):
    lat_dim, lon_dim = value.ndim - 1, value.ndim - 2
    for axis, dim, wrap in (("lat", lat_dim, False), ("lon", lon_dim, True)):
        size, length = lax.axis_size(axis), value.shape[dim]
        up = [(i, (i + 1) % size) for i in range(size if wrap else size - 1)]
        down = [(j, i) for i, j in up]
        before = lax.ppermute(lax.slice_in_dim(value, length - width, length, axis=dim), axis, up)
        after = lax.ppermute(lax.slice_in_dim(value, 0, width, axis=dim), axis, down)
        value = jnp.concatenate([before, value, after], axis=dim)
    return value


def face_coeffs(wide, width):
    lat_count = wide.shape[3] - 2 * width
    lanes = -(-wide.shape[3] // 128) * 128
    wide = jnp.pad(wide, ((0, 0), (0, 0), (1, 1), (1, 1 + lanes - wide.shape[3])))
    lat_devices = lax.axis_size("lat")
    first = lax.axis_index("lat") * lat_count - width
    cells = first + jnp.arange(lanes, dtype=jnp.int32)
    inside = ((cells >= 0) & (cells < lat_devices * lat_count)).astype(jnp.float32)
    centre = wide[:, :, 1:-1, 1:-1]
    return (
        inside * (0.5 * (centre + wide[:, :, 1:-1, 2:])),
        inside * (0.5 * (centre + wide[:, :, 1:-1, :-2])),
        inside * (0.5 * (centre + wide[:, :, 2:, 1:-1])),
        inside * (0.5 * (centre + wide[:, :, :-2, 1:-1])),
    )


def diffuse_kernel(steps, field_ref, north_ref, south_ref, east_ref, west_ref, out_ref):
    field = field_ref[...]
    rows, lanes = field.shape[1], field.shape[2]
    north, south, east, west = north_ref[...], south_ref[...], east_ref[...], west_ref[...]
    for sweep in range(steps):
        field = (
            field
            + north * (pltpu.roll(field, lanes - 1, 2) - field)
            + south * (pltpu.roll(field, 1, 2) - field)
            + east * (pltpu.roll(field, rows - 1, 1) - field)
            + west * (pltpu.roll(field, 1, 1) - field)
        )
    field = pltpu.roll(pltpu.roll(field, lanes - steps, 2), rows - steps, 1)
    out_ref[...] = field[:, : out_ref.shape[1], : out_ref.shape[2]]


def pad_lanes(value):
    planes, rows, lanes = value.shape
    return jnp.pad(value, ((0, 0), (0, 0), (0, -lanes % 128)))


def padded_coeffs(coeffs):
    return tuple(pad_lanes(c.reshape((-1,) + c.shape[-2:])) for c in coeffs)


def diffuse(field, coeffs, planes_per_step=20):
    lead = field.shape[:-2]
    flat = pad_lanes(field.reshape((-1,) + field.shape[-2:]))
    planes, rows, lanes = flat.shape
    lon_count, lat_count = rows - 2 * STEPS, field.shape[-1] - 2 * STEPS
    spec = pl.BlockSpec((planes_per_step, rows, lanes), lambda i: (i, 0, 0))
    out = pl.pallas_call(
        functools.partial(diffuse_kernel, STEPS),
        grid=(planes // planes_per_step,),
        in_specs=[spec] * 5,
        out_specs=pl.BlockSpec((planes_per_step, lon_count, lat_count), lambda i: (i, 0, 0)),
        out_shape=jax.ShapeDtypeStruct((planes, lon_count, lat_count), field.dtype),
        cost_estimate=pl.CostEstimate(
            flops=14 * STEPS * planes * rows * lanes, transcendentals=0, bytes_accessed=24 * planes * rows * lanes
        ),
    )(flat, *coeffs)
    return out.reshape(lead + (lon_count, lat_count))


PARTS = 2


def split_parts(value):
    parts = []
    rest = value
    for part in range(PARTS):
        piece = rest.astype(jnp.bfloat16)
        parts.append(piece)
        rest = rest - piece.astype(jnp.float32)
    return parts


def obs_lines(cell_ref, weight_ref, group, lat_count):
    cells = cell_ref[...]
    rows = cells // lat_count
    lats = cells - rows * lat_count
    row_line = jnp.concatenate([rows[g : g + 1, :] for g in range(group)], axis=1)
    lat_line = jnp.concatenate([lats[g : g + 1, :] for g in range(group)], axis=1)
    weights = [
        jnp.concatenate([weight_ref[g, c : c + 1, :] for g in range(group)], axis=1) for c in range(4)
    ]
    return row_line, lat_line, weights


def select_maps(row_line, lat_line, weights, row_count, lat_count):
    width = row_line.shape[1]
    row_ids = lax.broadcasted_iota(jnp.int32, (row_count, width), 0)
    near_rows = (row_ids == row_line).astype(jnp.bfloat16)
    lat_ids = lax.broadcasted_iota(jnp.int32, (lat_count, width), 0)
    at_first = lat_ids == lat_line
    at_second = lat_ids == lat_line + 1
    near_lat = jnp.where(at_first, weights[0], 0.0) + jnp.where(at_second, weights[1], 0.0)
    far_lat = jnp.where(at_first, weights[2], 0.0) + jnp.where(at_second, weights[3], 0.0)
    return near_rows, near_lat, far_lat


def observe_kernel(group, var_count, row_count, lat_count, table_ref, cell_ref, weight_ref, scale_ref, out_ref):
    row_line, lat_line, weights = obs_lines(cell_ref, weight_ref, group, lat_count)
    near_rows, near_lat, far_lat = select_maps(row_line, lat_line, weights, row_count, lat_count)
    table = jnp.concatenate(split_parts(table_ref[...]), axis=1)
    picked = jnp.dot(table, jnp.concatenate([near_rows] * PARTS, axis=0), preferred_element_type=jnp.float32)
    half = var_count * lat_count
    for v in range(var_count):
        near_span = slice(v * lat_count, (v + 1) * lat_count)
        far_span = slice(half + v * lat_count, half + (v + 1) * lat_count)
        line = jnp.sum(picked[near_span] * near_lat + picked[far_span] * far_lat, axis=0, keepdims=True)
        for g in range(group):
            out_ref[v, g : g + 1, :] = scale_ref[v, g : g + 1, :] * line[:, g * 128 : (g + 1) * 128]


def spread_kernel(group, var_count, row_count, lat_count, value_ref, cell_ref, weight_ref, out_ref, total_ref):
    step = pl.program_id(0)

    @pl.when(step == 0)
    def _():
        total_ref[...] = jnp.zeros_like(total_ref)

    row_line, lat_line, weights = obs_lines(cell_ref, weight_ref, group, lat_count)
    near_rows, near_lat, far_lat = select_maps(row_line, lat_line, weights, row_count, lat_count)
    near_parts, far_parts = [], []
    for v in range(var_count):
        line = jnp.concatenate([value_ref[v, g : g + 1, :] for g in range(group)], axis=1)
        near_parts.append(near_lat * line)
        far_parts.append(far_lat * line)
    rhs = jnp.concatenate(split_parts(jnp.concatenate(near_parts + far_parts, axis=0)), axis=1)
    lhs = jnp.concatenate([near_rows] * PARTS, axis=1)
    total_ref[...] += lax.dot_general(
        lhs, rhs, (((1,), (1,)), ((), ())), preferred_element_type=jnp.float32
    )

    @pl.when(step == pl.num_programs(0) - 1)
    def _():
        total = total_ref[...]
        half = var_count * lat_count
        summed = total[:, :half] + pltpu.roll(total[:, half:], 1, 0)
        for v in range(var_count):
            out_ref[v] = summed[:, v * lat_count : (v + 1) * lat_count]


def observe_pallas(field, stencil, bilinear, obs_weight, group=32):
    var_count, level_count, lon_count, lat_count = field.shape
    row_count = level_count * lon_count
    block_count = stencil.shape[0]
    rows_t = jnp.transpose(field.reshape(var_count, row_count, lat_count), (0, 2, 1))
    shifted = jnp.concatenate([rows_t[:, :, 1:], jnp.zeros_like(rows_t[:, :, :1])], axis=2)
    table = jnp.concatenate([rows_t, shifted], axis=0).reshape(2 * var_count * lat_count, row_count)
    kernel = functools.partial(observe_kernel, group, var_count, row_count, lat_count)
    width = group * stencil.shape[1]
    flops = 2 * 2 * var_count * lat_count * PARTS * row_count * width * (block_count // group)
    return pl.pallas_call(
        kernel,
        grid=(block_count // group,),
        in_specs=[
            pl.BlockSpec(table.shape, lambda i: (0, 0)),
            pl.BlockSpec((group, stencil.shape[1]), lambda i: (i, 0)),
            pl.BlockSpec((group, 4, stencil.shape[1]), lambda i: (i, 0, 0)),
            pl.BlockSpec((var_count, group, stencil.shape[1]), lambda i: (0, i, 0)),
        ],
        out_specs=pl.BlockSpec((var_count, group, stencil.shape[1]), lambda i: (0, i, 0)),
        out_shape=jax.ShapeDtypeStruct(obs_weight.shape, jnp.float32),
        cost_estimate=pl.CostEstimate(flops=flops, transcendentals=0, bytes_accessed=4 * 1024 * 1024),
    )(table, stencil, bilinear, obs_weight)


def spread_pallas(values, stencil, bilinear, field_shape, group=32):
    var_count, level_count, lon_count, lat_count = field_shape
    row_count = level_count * lon_count
    block_count = stencil.shape[0]
    kernel = functools.partial(spread_kernel, group, var_count, row_count, lat_count)
    width = group * stencil.shape[1]
    flops = 2 * 2 * var_count * lat_count * PARTS * row_count * width * (block_count // group)
    total = pl.pallas_call(
        kernel,
        grid=(block_count // group,),
        in_specs=[
            pl.BlockSpec((var_count, group, stencil.shape[1]), lambda i: (0, i, 0)),
            pl.BlockSpec((group, stencil.shape[1]), lambda i: (i, 0)),
            pl.BlockSpec((group, 4, stencil.shape[1]), lambda i: (i, 0, 0)),
        ],
        out_specs=pl.BlockSpec((var_count, row_count, lat_count), lambda i: (0, 0, 0)),
        out_shape=jax.ShapeDtypeStruct((var_count, row_count, lat_count), jnp.float32),
        scratch_shapes=[pltpu.VMEM((row_count, 2 * var_count * lat_count), jnp.float32)],
        cost_estimate=pl.CostEstimate(flops=flops, transcendentals=0, bytes_accessed=4 * 1024 * 1024),
    )(values, stencil, bilinear)
    return total.reshape(field_shape)


def allreduce_kernel(lat_devices, lon_devices, part_ref, out_ref, lon_buf, lat_buf, lon_send, lon_recv, lat_send, lat_recv):
    mesh_id = pl.DeviceIdType.MESH
    lat_me = lax.axis_index("lat")
    lon_me = lax.axis_index("lon")
    barrier = pltpu.get_barrier_semaphore()
    for peer in range(1, lon_devices):
        pl.semaphore_signal(barrier, inc=1, device_id=(lat_me, (lon_me + peer) % lon_devices), device_id_type=mesh_id)
    for peer in range(1, lat_devices):
        pl.semaphore_signal(barrier, inc=1, device_id=((lat_me + peer) % lat_devices, lon_me), device_id_type=mesh_id)
    pl.semaphore_wait(barrier, lon_devices + lat_devices - 2)

    def gather(buf, send, recv, count, me, target_of, source):
        copies = []
        for peer in range(1, count):
            target = (me + peer) % count
            copy = pltpu.make_async_remote_copy(
                src_ref=source,
                dst_ref=buf.at[me],
                send_sem=send.at[target],
                recv_sem=recv.at[me],
                device_id=target_of(target),
                device_id_type=mesh_id,
            )
            copy.start()
            copies.append((peer, copy))
        for peer, copy in copies:
            copy.wait_send()
        for peer in range(1, count):
            source_index = (me + count - peer) % count
            pltpu.make_async_remote_copy(
                src_ref=source,
                dst_ref=buf.at[source_index],
                send_sem=send.at[source_index],
                recv_sem=recv.at[source_index],
                device_id=target_of(source_index),
                device_id_type=mesh_id,
            ).wait_recv()

    gather(lon_buf, lon_send, lon_recv, lon_devices, lon_me, lambda t: (lat_me, t), part_ref)
    lon_buf[lon_me] = part_ref[...]
    total = lon_buf[0]
    for i in range(1, lon_devices):
        total = total + lon_buf[i]
    out_ref[...] = total
    gather(lat_buf, lat_send, lat_recv, lat_devices, lat_me, lambda t: (t, lon_me), out_ref)
    lat_buf[lat_me] = out_ref[...]
    total = lat_buf[0]
    for i in range(1, lat_devices):
        total = total + lat_buf[i]
    out_ref[...] = total


def allreduce_pallas(part):
    lat_devices = lax.axis_size("lat")
    lon_devices = lax.axis_size("lon")
    kernel = functools.partial(allreduce_kernel, lat_devices, lon_devices)
    return pl.pallas_call(
        kernel,
        in_specs=[pl.BlockSpec(memory_space=pltpu.VMEM)],
        out_specs=pl.BlockSpec(memory_space=pltpu.VMEM),
        out_shape=jax.ShapeDtypeStruct(part.shape, jnp.float32),
        scratch_shapes=[
            pltpu.VMEM((lon_devices,) + part.shape, jnp.float32),
            pltpu.VMEM((lat_devices,) + part.shape, jnp.float32),
            pltpu.SemaphoreType.DMA((lon_devices,)),
            pltpu.SemaphoreType.DMA((lon_devices,)),
            pltpu.SemaphoreType.DMA((lat_devices,)),
            pltpu.SemaphoreType.DMA((lat_devices,)),
        ],
        compiler_params=pltpu.CompilerParams(collective_id=0, has_side_effects=True),
    )(part)


def slots_of(block_owner, tile_count):
    targets = block_owner[:, 0]
    block_count = targets.shape[0]
    same_owner = (targets[:, None] == jnp.arange(tile_count, dtype=jnp.int32)[None, :]).astype(
        jnp.int32
    )
    order = jnp.arange(block_count, dtype=jnp.int32)
    lower = (order[:, None] > order[None, :]).astype(jnp.int32)
    earlier = jnp.dot(lower, same_owner)
    rank_within = jnp.sum(earlier * same_owner, axis=1)
    return targets * CAP + rank_within


def mix_blocks(values, correlation):
    return jnp.einsum("vsk,ik->vsi", values, correlation, precision=precise)


def shards(
    increment,
    residual,
    direction,
    diffusivity,
    deviation,
    stencil,
    bilinear,
    obs_weight,
    block_owner,
    correlation,
):
    lat_devices = lax.axis_size("lat")
    lon_devices = lax.axis_size("lon")
    tile_count = lat_devices * lon_devices
    both = widen_halo(jnp.stack([direction, diffusivity]), STEPS)
    coeffs = padded_coeffs(face_coeffs(both[1], STEPS))

    def apply_diffusion(field):
        return diffuse(widen_halo(field, STEPS), coeffs)

    slots = slots_of(block_owner, tile_count)
    slot_table = (slots[:, None] == jnp.arange(tile_count * CAP, dtype=jnp.int32)[None, :]).astype(
        jnp.float32
    )
    field_shape = direction.shape
    state_field = deviation * diffuse(both[0], coeffs)
    observed = observe_pallas(state_field, stencil, bilinear, obs_weight)
    buffer = jnp.einsum("vbk,bs->vsk", observed, slot_table, precision=precise)
    returned = lax.all_to_all(
        mix_blocks(
            lax.all_to_all(buffer, ("lat", "lon"), split_axis=1, concat_axis=1, tiled=True),
            correlation,
        ),
        ("lat", "lon"),
        split_axis=1,
        concat_axis=1,
        tiled=True,
    )
    weighted = obs_weight * jnp.einsum("vsk,bs->vbk", returned, slot_table, precision=precise)
    spread_field = deviation * spread_pallas(weighted, stencil, bilinear, field_shape)
    image_field = direction + apply_diffusion(spread_field)
    local_sums = jnp.stack(
        [
            jnp.sum(residual * residual),
            jnp.sum(direction * image_field),
            jnp.sum(residual * image_field),
            jnp.sum(image_field * image_field),
        ]
    )
    sums = allreduce_pallas(jnp.zeros((8, 128), jnp.float32).at[0, :4].set(local_sums))[0]
    norm_now, curvature, cross, image_norm = sums[0], sums[1], sums[2], sums[3]
    step_size = norm_now / curvature
    increment = increment + step_size * direction
    residual = residual - step_size * image_field
    norm_next = norm_now - 2.0 * step_size * cross + step_size * step_size * image_norm
    direction = residual + norm_next / norm_now * direction
    return (increment, residual, direction)


def solution(mesh):
    in_specs = (
        P(None, None, "lon", "lat"),
        P(None, None, "lon", "lat"),
        P(None, None, "lon", "lat"),
        P(None, None, "lon", "lat"),
        P(None, None, "lon", "lat"),
        P(("lat", "lon"), None),
        P(("lat", "lon"), None, None),
        P(None, ("lat", "lon"), None),
        P(("lat", "lon"), None),
        P(("lat", "lon"), None),
    )
    out_specs = (
        P(None, None, "lon", "lat"),
        P(None, None, "lon", "lat"),
        P(None, None, "lon", "lat"),
    )
    return jax.shard_map(shards, mesh=mesh, in_specs=in_specs, out_specs=out_specs, check_vma=False)
```
